256 devices in a mesh: lon: 32 (over z, y_hi, core), lat: 8 (over y_lo, x).
Axes of the slice: x: 4, y: 4 (y_hi: 2, y_lo: 2; y = y_hi * 2 + y_lo), z: 8, core: 2. Of those that a mesh axis runs over, the one named last changes fastest.
Arguments:
- state: bfloat16 [360, 768, 128], P('lat', 'lon'), may hold values from -6 to 6
- land_sea: int32 [360, 768], P('lat', 'lon'), may hold values 0 or 1
- cotangent: bfloat16 [360, 768, 128], P('lat', 'lon'), may hold values from -6 to 6
- dw_kernel: bfloat16 [2, 7, 7, 128], replicated, may hold values from -0.875 to 0.875
- conv_bias: float32 [2, 128], replicated, may hold values from -3 to 3
- norm_gain: float32 [2, 128], replicated, may hold values from 0.1 to 1.9
- norm_bias: float32 [2, 128], replicated, may hold values from -3 to 3
- weight_in: bfloat16 [2, 128, 512], replicated, may hold values from -0.5 to 0.5
- bias_in: float32 [2, 512], replicated, may hold values from -3 to 3
- weight_out: bfloat16 [2, 512, 128], replicated, may hold values from -0.25 to 0.25
- bias_out: float32 [2, 128], replicated, may hold values from -3 to 3
- layer_scale: float32 [2, 128], replicated, may hold values from 0.3 to 1
Outputs:
- output: bfloat16 [360, 768, 128], P('lat', 'lon')
- grad_state: bfloat16 [360, 768, 128], P('lat', 'lon')
- grad_dw_kernel: float32 [2, 7, 7, 128], replicated
- grad_conv_bias: float32 [2, 128], replicated
- grad_norm_gain: float32 [2, 128], replicated
- grad_norm_bias: float32 [2, 128], replicated
- grad_weight_in: float32 [2, 128, 512], replicated
- grad_bias_in: float32 [2, 512], replicated
- grad_weight_out: float32 [2, 512, 128], replicated
- grad_bias_out: float32 [2, 128], replicated
- grad_layer_scale: float32 [2, 128], replicated
The draws below stay inside these ranges and needn't reach their ends.
All inputs are finite; a program needn't handle non-finite values. No bound on the sum of `land_sea` on one device may be relied on, other than what follows from the above.
Results may differ from the reference program's by a relative error of at most 0.02.
Values may be sent and summed in bfloat16 or wider, within the bound.
A program may use at most 64 MiB of HBM per device.

```python
import math
import jax
import jax.numpy as jnp
from jax import lax

C = 128
F = 512
KSIZE = 7
BLOCKS = 2
LAT_DEV = 45
NLAT = 360
NLON = 768


def plant(entries, own_key, smallest, top_value):
    longest = entries.shape.index(max(entries.shape))
    spots = []
    for shift in (0, 1):
        where = [jax.random.randint(jax.random.fold_in(own_key, axis), (), 0, length) for axis, length in enumerate(entries.shape)]
        where[longest] = (where[longest] + shift) % entries.shape[longest]
        spots.append(tuple(where))
    return entries.at[spots[0]].set(smallest).at[spots[1]].set(top_value)


def block_scale(rng, extent, cuts, smallest, largest):
    def one(dim, shards_of):
        steps = jax.random.uniform(jax.random.fold_in(jax.random.fold_in(rng, 6), dim), (shards_of,), jnp.float32, smallest / len(cuts), largest / len(cuts))
        return jnp.repeat(jnp.exp(steps), extent[dim] // shards_of).reshape((-1,) + (1,) * (len(extent) - dim - 1))

    level = one(*cuts[0])
    for cut in cuts[1:]:
        level = level * one(*cut)
    return level


def noise(stream_key, shape, deviation, most, split=(), held_as=jnp.bfloat16):
    array = deviation * jax.random.normal(stream_key, shape, jnp.float32)
    if split:
        array = array * block_scale(stream_key, shape, split, -0.22, 0.18)
    return jnp.clip(array, -most, most).astype(held_as)


def setup_inputs(seed: int = 0) -> dict:
    key_of = jax.random.split(jax.random.key(seed), 13)
    return {
        "state": noise(key_of[0], (NLAT, NLON, C), 1.0, 6.0, ((0, 8), (1, 32))),
        "land_sea": plant((jax.random.randint(key_of[1], (NLAT, NLON), 0, 10) < 7).astype(jnp.int32), jax.random.fold_in(key_of[1], 1), 0, 1),
        "cotangent": noise(key_of[2], (NLAT, NLON, C), 1.0, 6.0, ((0, 8), (1, 32))),
        "dw_kernel": noise(key_of[3], (BLOCKS, KSIZE, KSIZE, C), (KSIZE * KSIZE) ** -0.5, 0.875),
        "conv_bias": noise(key_of[4], (BLOCKS, C), 0.5, 3.0, (), jnp.float32),
        "norm_gain": jnp.clip(1.0 + 0.18 * jax.random.normal(key_of[5], (BLOCKS, C), jnp.float32), 0.1, 1.9),
        "norm_bias": noise(key_of[6], (BLOCKS, C), 0.5, 3.0, (), jnp.float32),
        "weight_in": noise(key_of[7], (BLOCKS, C, F), C ** -0.5, 0.5),
        "bias_in": noise(key_of[8], (BLOCKS, F), 0.5, 3.0, (), jnp.float32),
        "weight_out": noise(key_of[9], (BLOCKS, F, C), F ** -0.5, 0.25),
        "bias_out": noise(key_of[10], (BLOCKS, C), 0.5, 3.0, (), jnp.float32),
        "layer_scale": jnp.clip(jnp.exp(jax.random.uniform(key_of[11], (BLOCKS, C), jnp.float32, math.log(0.3), math.log(1.0))), 0.3, 1.0),
    }


EPS_NORM = 1e-06
INV_ROOT_TWO = 0.7071067811865476
INV_ROOT_TWO_PI = 0.3989422804014327

def depthwise(window, kernel, height, breadth):
    summed = jnp.zeros((height, breadth, window.shape[2]), jnp.float32)
    for tap_row in range(KSIZE):
        for tap_col in range(KSIZE):
            piece = window[tap_row:tap_row + height, tap_col:tap_col + breadth].astype(jnp.float32)
            summed = summed + piece * kernel[tap_row, tap_col].astype(jnp.float32)
    return summed

def block_forward(window, land_rows, params):
    kernel, conv_bias, norm_gain, norm_bias, weight_in, bias_in, weight_out, bias_out, layer_scale = params
    margin = KSIZE // 2
    height = window.shape[0] - 2 * margin
    breadth = window.shape[1] - 2 * margin
    channels = window.shape[2]
    cell_count = height * breadth
    mixed_sum = depthwise(window, kernel, height, breadth) + conv_bias
    center = mixed_sum - lax.optimization_barrier(jnp.mean(mixed_sum, axis=-1, keepdims=True))
    inverse = lax.rsqrt(lax.optimization_barrier(jnp.mean(center * center, axis=-1, keepdims=True)) + EPS_NORM)
    normed = (center * inverse).reshape(cell_count, channels)
    lifted = (normed * norm_gain + norm_bias).astype(jnp.bfloat16)
    hidden = jnp.dot(lifted, weight_in, preferred_element_type=jnp.float32) + bias_in
    active = jax.nn.gelu(hidden, approximate=False).astype(jnp.bfloat16)
    branch = jnp.dot(active, weight_out, preferred_element_type=jnp.float32) + bias_out
    interior = window[margin:margin + height, margin:margin + breadth].astype(jnp.float32).reshape(cell_count, channels)
    ocean_mask = land_rows.reshape(cell_count, 1).astype(jnp.float32)
    result = ((interior + layer_scale * branch) * ocean_mask).astype(jnp.bfloat16).reshape(height, breadth, channels)
    return (result, (normed, inverse.reshape(cell_count, 1), lifted, hidden, active, branch))

def block_backward(window, land_rows, incoming, params, stored):
    kernel, conv_bias, norm_gain, norm_bias, weight_in, bias_in, weight_out, bias_out, layer_scale = params
    normed, inverse, lifted, hidden, active, branch = stored
    margin = KSIZE // 2
    height = window.shape[0] - 2 * margin
    breadth = window.shape[1] - 2 * margin
    channels = window.shape[2]
    cell_count = height * breadth
    ocean_mask = land_rows.reshape(cell_count, 1).astype(jnp.float32)
    masked = incoming.reshape(cell_count, channels).astype(jnp.float32) * ocean_mask
    grad_branch = (masked * layer_scale).astype(jnp.bfloat16)
    contract_rows = (((0,), (0,)), ((), ()))
    contract_cols = (((1,), (1,)), ((), ()))
    grad_scale = lax.optimization_barrier(jnp.sum(masked * branch, axis=0))
    grad_bias_out = lax.optimization_barrier(jnp.sum(grad_branch.astype(jnp.float32), axis=0))
    grad_weight_out = lax.dot_general(active, grad_branch, contract_rows, preferred_element_type=jnp.float32)
    grad_active = lax.dot_general(grad_branch, weight_out, contract_cols, preferred_element_type=jnp.float32)
    cumulative = 0.5 * (1.0 + lax.erf(hidden * INV_ROOT_TWO))
    density = jnp.exp(-0.5 * hidden * hidden) * INV_ROOT_TWO_PI
    grad_hidden = (grad_active * (cumulative + hidden * density)).astype(jnp.bfloat16)
    grad_bias_in = lax.optimization_barrier(jnp.sum(grad_hidden.astype(jnp.float32), axis=0))
    grad_weight_in = lax.dot_general(lifted, grad_hidden, contract_rows, preferred_element_type=jnp.float32)
    grad_lifted = lax.dot_general(grad_hidden, weight_in, contract_cols, preferred_element_type=jnp.float32)
    grad_gain = lax.optimization_barrier(jnp.sum(grad_lifted * normed, axis=0))
    grad_shift = lax.optimization_barrier(jnp.sum(grad_lifted, axis=0))
    scaled = grad_lifted * norm_gain
    grad_mixed = inverse * (scaled - lax.optimization_barrier(jnp.mean(scaled, axis=-1, keepdims=True)) - normed * lax.optimization_barrier(jnp.mean(scaled * normed, axis=-1, keepdims=True)))
    grad_mixed = grad_mixed.astype(jnp.bfloat16).reshape(height, breadth, channels)
    spread = grad_mixed.astype(jnp.float32)
    grad_conv_bias = lax.optimization_barrier(jnp.sum(spread, axis=(0, 1)))
    tap_sums = []
    for tap_row in range(KSIZE):
        for tap_col in range(KSIZE):
            piece = window[tap_row:tap_row + height, tap_col:tap_col + breadth].astype(jnp.float32)
            tap_sums.append(lax.optimization_barrier(jnp.sum(spread * piece, axis=(0, 1))))
    grad_kernel = jnp.stack(tap_sums).reshape(KSIZE, KSIZE, channels)
    gradients = (grad_kernel, grad_conv_bias, grad_gain, grad_shift, grad_weight_in, grad_bias_in, grad_weight_out, grad_bias_out, grad_scale)
    return (grad_mixed, masked.reshape(height, breadth, channels), gradients)

def adjoint(padded, masked, kernel):
    margin = KSIZE // 2
    height = masked.shape[0]
    breadth = masked.shape[1]
    summed = masked
    for tap_row in range(KSIZE):
        for tap_col in range(KSIZE):
            first_row = 2 * margin - tap_row
            first_col = 2 * margin - tap_col
            piece = padded[first_row:first_row + height, first_col:first_col + breadth].astype(jnp.float32)
            summed = summed + piece * kernel[tap_row, tap_col].astype(jnp.float32)
    return summed.astype(jnp.bfloat16)

def pad_grid(grid_field):
    margin = KSIZE // 2
    columns = grid_field.shape[1]
    wrapped = jnp.concatenate([grid_field[:, columns - margin:], grid_field, grid_field[:, :margin]], axis=1)
    return jnp.pad(wrapped, ((margin, margin), (0, 0), (0, 0)))

def rows_forward(padded, land_sea, params):
    row_blocks = land_sea.shape[0] // LAT_DEV
    row_span = LAT_DEV + KSIZE - 1

    def one_block(position):
        row_start = position * LAT_DEV
        window = lax.dynamic_slice_in_dim(padded, row_start, row_span, 0)
        land_rows = lax.dynamic_slice_in_dim(land_sea, row_start, LAT_DEV, 0)
        return block_forward(window, land_rows, params)[0]
    pieces = lax.map(one_block, jnp.arange(row_blocks, dtype=jnp.int32))
    return pieces.reshape(land_sea.shape[0], land_sea.shape[1], pieces.shape[3])

def rows_backward(padded, land_sea, incoming, params):
    row_blocks = land_sea.shape[0] // LAT_DEV
    row_span = LAT_DEV + KSIZE - 1
    empty_sums = tuple((jnp.zeros(member.shape, jnp.float32) for member in params))

    def advance(running, position):
        row_start = position * LAT_DEV
        window = lax.dynamic_slice_in_dim(padded, row_start, row_span, 0)
        land_rows = lax.dynamic_slice_in_dim(land_sea, row_start, LAT_DEV, 0)
        grad_rows = lax.dynamic_slice_in_dim(incoming, row_start, LAT_DEV, 0)
        stored = block_forward(window, land_rows, params)[1]
        grad_mixed, masked, gradients = block_backward(window, land_rows, grad_rows, params, stored)
        return (tuple((left + right for left, right in zip(running, gradients))), (grad_mixed, masked))
    totals, (mixed_rows, masked_rows) = lax.scan(advance, empty_sums, jnp.arange(row_blocks, dtype=jnp.int32))
    shape_out = (land_sea.shape[0], land_sea.shape[1], incoming.shape[2])
    return (mixed_rows.reshape(shape_out), masked_rows.reshape(shape_out), totals)

def reference(state, land_sea, cotangent, dw_kernel, conv_bias, norm_gain, norm_bias, weight_in, bias_in, weight_out, bias_out, layer_scale):
    stacked = (dw_kernel, conv_bias, norm_gain, norm_bias, weight_in, bias_in, weight_out, bias_out, layer_scale)
    current = state
    padded_inputs = []
    for layer_index in range(BLOCKS):
        params = tuple((member[layer_index] for member in stacked))
        padded = pad_grid(current)
        padded_inputs.append(padded)
        current = rows_forward(padded, land_sea, params)
    incoming = cotangent
    per_layer = [None] * BLOCKS
    for layer_index in reversed(range(BLOCKS)):
        params = tuple((member[layer_index] for member in stacked))
        grad_mixed, masked, gradients = rows_backward(padded_inputs[layer_index], land_sea, incoming, params)
        incoming = adjoint(pad_grid(grad_mixed), masked, params[0])
        per_layer[layer_index] = gradients
    grad_norm = 1.0 / math.sqrt(NLAT * NLON)
    summed = [jnp.stack([per_layer[layer_index][member] for layer_index in range(BLOCKS)]) * grad_norm for member in range(9)]
    return (current, incoming, summed[0], summed[1], summed[2], summed[3], summed[4], summed[5], summed[6], summed[7], summed[8])
```

```python
import math

import jax
import jax.numpy as jnp
from jax import lax
from jax.experimental import pallas as pl
from jax.experimental.pallas import tpu as pltpu
from jax.sharding import PartitionSpec as P

KSIZE = 7
BLOCKS = 2
C = 128
F = 512
EPS_NORM = 1e-06
INV_ROOT_TWO = 0.7071067811865476
INV_ROOT_TWO_PI = 0.3989422804014327
MESH_ID = pl.DeviceIdType.MESH
GROUP = 16


def position():
    lon = lax.axis_index("lon")
    lat = lax.axis_index("lat")
    z = lon // 4
    y_hi = lax.rem(lon // 2, 2)
    core = lax.rem(lon, 2)
    plane = y_hi * 8 + lat
    line = z * 2 + core
    return plane, line


def plane_peer(plane, line):
    lon = (line // 2) * 4 + (plane // 8) * 2 + lax.rem(line, 2)
    return {"lon": lon, "lat": lax.rem(plane, 8)}


def greet(barrier):
    plane, line = position()

    def one(k, carry):
        other = lax.rem(plane + k, GROUP)
        pl.semaphore_signal(
            barrier, inc=1, device_id=plane_peer(other, line), device_id_type=MESH_ID
        )
        other = lax.rem(line + k, GROUP)
        pl.semaphore_signal(
            barrier, inc=1, device_id=plane_peer(plane, other), device_id_type=MESH_ID
        )
        return carry

    lax.fori_loop(1, GROUP, one, 0)
    pl.semaphore_wait(barrier, 2 * (GROUP - 1))


class Exchange:
    def __init__(self, kind, scatter, src, dst, send, recv):
        self.plane, self.line = position()
        self.kind = kind
        self.scatter = scatter
        self.src, self.dst, self.send, self.recv = src, dst, send, recv
        self.me = self.plane if kind == "plane" else self.line

    def copy(self, k):
        other = lax.rem(self.me + k, GROUP)
        if self.kind == "plane":
            target = plane_peer(other, self.line)
        else:
            target = plane_peer(self.plane, other)
        src = self.src.at[other] if self.scatter else self.src
        return pltpu.make_async_remote_copy(
            src_ref=src,
            dst_ref=self.dst.at[k],
            send_sem=self.send.at[k],
            recv_sem=self.recv.at[k],
            device_id=target,
            device_id_type=MESH_ID,
        )

    def start(self):
        def one(k, carry):
            self.copy(k).start()
            return carry

        lax.fori_loop(1, GROUP, one, 0)

    def wait(self):
        def one(k, carry):
            self.copy(k).wait()
            return carry

        lax.fori_loop(1, GROUP, one, 0)


def slot_sum(own, slots, count=GROUP):
    def one(k, total):
        return total + slots[k].astype(jnp.float32)

    return lax.fori_loop(1, count, one, own)


def reduce_kernel(
    grad_norm,
    win_ref,
    wout_ref,
    small_ref,
    win_out,
    wout_out,
    small_out,
    send_a,
    recv_a,
    send_b,
    recv_b,
    own_b,
    back_b,
    own_a,
    back_a,
    srecv_a,
    sown_b,
    srecv_b,
    sown_a,
    sback_a,
    sem_w,
    sem_s,
):
    plane, line = position()
    greet(pltpu.get_barrier_semaphore())

    ex_s1 = Exchange("plane", True, small_ref, srecv_a, sem_s.at[0], sem_s.at[1])
    ex_s1.start()
    phases = []
    for blk in range(BLOCKS):
        for p in range(8):
            send_a[blk, p] = win_ref[
                blk, (p % 2) * 64 : (p % 2) * 64 + 64, (p // 2) * 128 : (p // 2) * 128 + 128
            ].astype(jnp.bfloat16)
            send_a[blk, 8 + p] = wout_ref[blk, p * 64 : p * 64 + 64].astype(jnp.bfloat16)
        ex = Exchange(
            "plane", True, send_a.at[blk], recv_a.at[blk], sem_w.at[blk, 0], sem_w.at[blk, 1]
        )
        ex.start()
        phases.append(ex)
    ex_s1.wait()
    sown_b[...] = slot_sum(small_ref[plane], srecv_a)
    ex_s2 = Exchange("line", False, sown_b, srecv_b, sem_s.at[2], sem_s.at[3])
    ex_s2.start()
    for blk in range(BLOCKS):
        phases[blk].wait()
        total = slot_sum(send_a[blk, plane].astype(jnp.float32), recv_a.at[blk])
        for j in range(GROUP):
            send_b[blk, j] = total[j * 4 : j * 4 + 4]
        ex = Exchange(
            "line", True, send_b.at[blk], recv_b.at[blk], sem_w.at[blk, 2], sem_w.at[blk, 3]
        )
        ex.start()
        phases[blk] = ex
    ex_s2.wait()
    sown_a[...] = slot_sum(sown_b[...], srecv_b)
    ex_s3 = Exchange("plane", False, sown_a, sback_a, sem_s.at[4], sem_s.at[5])
    ex_s3.start()
    for blk in range(BLOCKS):
        phases[blk].wait()
        own_b[blk] = slot_sum(send_b[blk, line], recv_b.at[blk])
        ex = Exchange(
            "line", False, own_b.at[blk], back_b.at[blk], sem_w.at[blk, 4], sem_w.at[blk, 5]
        )
        ex.start()
        phases[blk] = ex
    for blk in range(BLOCKS):
        phases[blk].wait()
        back_b[blk, 0] = own_b[blk]
        for j in range(GROUP):
            sub = back_b[blk, lax.rem(line - j + GROUP, GROUP)]
            own_a[blk, j * 4 : j * 4 + 4] = sub.astype(jnp.bfloat16)
        ex = Exchange(
            "plane", False, own_a.at[blk], back_a.at[blk], sem_w.at[blk, 6], sem_w.at[blk, 7]
        )
        ex.start()
        phases[blk] = ex
    ex_s3.wait()
    sback_a[0] = sown_a[...]
    for p in range(GROUP):
        small_out[p] = sback_a[lax.rem(plane - p + GROUP, GROUP)] * grad_norm
    for blk in range(BLOCKS):
        phases[blk].wait()
        back_a[blk, 0] = own_a[blk]
        for p in range(GROUP):
            piece = back_a[blk, lax.rem(plane - p + GROUP, GROUP)].astype(jnp.float32) * grad_norm
            if p < 8:
                win_out[
                    blk, (p % 2) * 64 : (p % 2) * 64 + 64, (p // 2) * 128 : (p // 2) * 128 + 128
                ] = piece
            else:
                wout_out[blk, (p - 8) * 64 : (p - 8) * 64 + 64] = piece


def reduce_gradients(win, wout, small, grad_norm):
    vmem = pl.BlockSpec(memory_space=pltpu.VMEM)
    return pl.pallas_call(
        lambda *refs: reduce_kernel(grad_norm, *refs),
        name="reduce_gradients",
        out_shape=(
            jax.ShapeDtypeStruct((BLOCKS, C, F), jnp.float32),
            jax.ShapeDtypeStruct((BLOCKS, F, C), jnp.float32),
            jax.ShapeDtypeStruct((GROUP, 8, C), jnp.float32),
        ),
        in_specs=[vmem] * 3,
        out_specs=(vmem,) * 3,
        scratch_shapes=[
            pltpu.VMEM((BLOCKS, GROUP, 64, C), jnp.bfloat16),
            pltpu.VMEM((BLOCKS, GROUP, 64, C), jnp.bfloat16),
            pltpu.VMEM((BLOCKS, GROUP, 4, C), jnp.float32),
            pltpu.VMEM((BLOCKS, GROUP, 4, C), jnp.float32),
            pltpu.VMEM((BLOCKS, 4, C), jnp.float32),
            pltpu.VMEM((BLOCKS, GROUP, 4, C), jnp.float32),
            pltpu.VMEM((BLOCKS, 64, C), jnp.bfloat16),
            pltpu.VMEM((BLOCKS, GROUP, 64, C), jnp.bfloat16),
            pltpu.VMEM((GROUP, 8, C), jnp.float32),
            pltpu.VMEM((8, C), jnp.float32),
            pltpu.VMEM((GROUP, 8, C), jnp.float32),
            pltpu.VMEM((8, C), jnp.float32),
            pltpu.VMEM((GROUP, 8, C), jnp.float32),
            pltpu.SemaphoreType.DMA((BLOCKS, 8, GROUP)),
            pltpu.SemaphoreType.DMA((6, GROUP)),
        ],
        compiler_params=pltpu.CompilerParams(
            collective_id=0, has_side_effects=True, vmem_limit_bytes=32 << 20
        ),
    )(win, wout, small)

def with_halo(shard, sides, width, wrap):
    for axis, dim in sides:
        count, length = (lax.axis_size(axis), shard.shape[dim])
        up = [(i, (i + 1) % count) for i in range(count if wrap else count - 1)]
        down = [(j, i) for i, j in up]
        last = lax.slice_in_dim(shard, length - width, length, axis=dim)
        first = lax.slice_in_dim(shard, 0, width, axis=dim)
        before = lax.ppermute(last, axis, up)
        after = lax.ppermute(first, axis, down)
        shard = jnp.concatenate([before, shard, after], axis=dim)
    return shard


def depthwise(window, kernel, height, breadth):
    summed = jnp.zeros((height, breadth, window.shape[2]), jnp.float32)
    for tap_row in range(KSIZE):
        for tap_col in range(KSIZE):
            piece = window[tap_row : tap_row + height, tap_col : tap_col + breadth].astype(
                jnp.float32
            )
            summed = summed + piece * kernel[tap_row, tap_col].astype(jnp.float32)
    return summed


def block_forward(window, land_rows, params):
    (
        kernel,
        conv_bias,
        norm_gain,
        norm_bias,
        weight_in,
        bias_in,
        weight_out,
        bias_out,
        layer_scale,
    ) = params
    margin = KSIZE // 2
    height = window.shape[0] - 2 * margin
    breadth = window.shape[1] - 2 * margin
    channels = window.shape[2]
    cell_count = height * breadth
    mixed_sum = depthwise(window, kernel, height, breadth) + conv_bias
    center = mixed_sum - jnp.mean(mixed_sum, axis=-1, keepdims=True)
    inverse = lax.rsqrt(jnp.mean(center * center, axis=-1, keepdims=True) + EPS_NORM)
    normed = (center * inverse).reshape(cell_count, channels)
    lifted = (normed * norm_gain + norm_bias).astype(jnp.bfloat16)
    hidden = jnp.dot(lifted, weight_in, preferred_element_type=jnp.float32) + bias_in
    active = jax.nn.gelu(hidden, approximate=False).astype(jnp.bfloat16)
    branch = jnp.dot(active, weight_out, preferred_element_type=jnp.float32) + bias_out
    interior = (
        window[margin : margin + height, margin : margin + breadth]
        .astype(jnp.float32)
        .reshape(cell_count, channels)
    )
    ocean_mask = land_rows.reshape(cell_count, 1).astype(jnp.float32)
    result = (
        ((interior + layer_scale * branch) * ocean_mask)
        .astype(jnp.bfloat16)
        .reshape(height, breadth, channels)
    )
    return (result, (normed, inverse.reshape(cell_count, 1), lifted, hidden, active, branch))


def block_backward(window, land_rows, incoming, params, stored):
    (
        kernel,
        conv_bias,
        norm_gain,
        norm_bias,
        weight_in,
        bias_in,
        weight_out,
        bias_out,
        layer_scale,
    ) = params
    normed, inverse, lifted, hidden, active, branch = stored
    margin = KSIZE // 2
    height = window.shape[0] - 2 * margin
    breadth = window.shape[1] - 2 * margin
    channels = window.shape[2]
    cell_count = height * breadth
    ocean_mask = land_rows.reshape(cell_count, 1).astype(jnp.float32)
    masked = incoming.reshape(cell_count, channels).astype(jnp.float32) * ocean_mask
    grad_branch = (masked * layer_scale).astype(jnp.bfloat16)
    contract_rows = (((0,), (0,)), ((), ()))
    contract_cols = (((1,), (1,)), ((), ()))
    grad_scale = jnp.sum(masked * branch, axis=0)
    grad_bias_out = jnp.sum(grad_branch.astype(jnp.float32), axis=0)
    grad_weight_out = lax.dot_general(
        active, grad_branch, contract_rows, preferred_element_type=jnp.float32
    )
    grad_active = lax.dot_general(
        grad_branch, weight_out, contract_cols, preferred_element_type=jnp.float32
    )
    cumulative = 0.5 * (1.0 + lax.erf(hidden * INV_ROOT_TWO))
    density = jnp.exp(-0.5 * hidden * hidden) * INV_ROOT_TWO_PI
    grad_hidden = (grad_active * (cumulative + hidden * density)).astype(jnp.bfloat16)
    grad_bias_in = jnp.sum(grad_hidden.astype(jnp.float32), axis=0)
    grad_weight_in = lax.dot_general(
        lifted, grad_hidden, contract_rows, preferred_element_type=jnp.float32
    )
    grad_lifted = lax.dot_general(
        grad_hidden, weight_in, contract_cols, preferred_element_type=jnp.float32
    )
    grad_gain = jnp.sum(grad_lifted * normed, axis=0)
    grad_shift = jnp.sum(grad_lifted, axis=0)
    scaled = grad_lifted * norm_gain
    grad_mixed = inverse * (
        scaled
        - jnp.mean(scaled, axis=-1, keepdims=True)
        - normed * jnp.mean(scaled * normed, axis=-1, keepdims=True)
    )
    grad_mixed = grad_mixed.astype(jnp.bfloat16).reshape(height, breadth, channels)
    spread = grad_mixed.astype(jnp.float32)
    grad_conv_bias = jnp.sum(spread, axis=(0, 1))
    tap_sums = []
    for tap_row in range(KSIZE):
        for tap_col in range(KSIZE):
            piece = window[tap_row : tap_row + height, tap_col : tap_col + breadth].astype(
                jnp.float32
            )
            tap_sums.append(jnp.sum(spread * piece, axis=(0, 1)))
    grad_kernel = jnp.stack(tap_sums).reshape(KSIZE, KSIZE, channels)
    gradients = (
        grad_kernel,
        grad_conv_bias,
        grad_gain,
        grad_shift,
        grad_weight_in,
        grad_bias_in,
        grad_weight_out,
        grad_bias_out,
        grad_scale,
    )
    return (grad_mixed, masked.reshape(height, breadth, channels), gradients)


def adjoint(padded, masked, kernel):
    margin = KSIZE // 2
    height = masked.shape[0]
    breadth = masked.shape[1]
    summed = masked
    for tap_row in range(KSIZE):
        for tap_col in range(KSIZE):
            first_row = 2 * margin - tap_row
            first_col = 2 * margin - tap_col
            piece = padded[first_row : first_row + height, first_col : first_col + breadth].astype(
                jnp.float32
            )
            summed = summed + piece * kernel[tap_row, tap_col].astype(jnp.float32)
    return summed.astype(jnp.bfloat16)


def extend(tile_field):
    beside_all = with_halo(tile_field, (("lon", 1),), KSIZE // 2, True)
    return with_halo(beside_all, (("lat", 0),), KSIZE // 2, False)


def sum_everything(parts, grad_norm):
    kernel_part, conv_part, gain_part, shift_part, first_part, first_bias, second_part, second_bias, scale_part = parts
    rows = jnp.concatenate(
        [
            kernel_part.reshape(BLOCKS, KSIZE * KSIZE, C),
            conv_part[:, None],
            gain_part[:, None],
            shift_part[:, None],
            second_bias[:, None],
            scale_part[:, None],
            first_bias.reshape(BLOCKS, F // C, C),
            jnp.zeros((BLOCKS, 6, C), jnp.float32),
        ],
        axis=1,
    )
    small = rows.reshape(BLOCKS, GROUP, 4, C).transpose(1, 0, 2, 3).reshape(GROUP, 8, C)
    first, second, small = reduce_gradients(first_part, second_part, small, grad_norm)
    rows = small.reshape(GROUP, BLOCKS, 4, C).transpose(1, 0, 2, 3).reshape(BLOCKS, 64, C)
    return (
        rows[:, :49].reshape(BLOCKS, KSIZE, KSIZE, C),
        rows[:, 49],
        rows[:, 50],
        rows[:, 51],
        first,
        rows[:, 54:58].reshape(BLOCKS, F),
        second,
        rows[:, 52],
        rows[:, 53],
    )


def on_device(
    state,
    land_sea,
    cotangent,
    dw_kernel,
    conv_bias,
    norm_gain,
    norm_bias,
    weight_in,
    bias_in,
    weight_out,
    bias_out,
    layer_scale,
):
    stacked = (
        dw_kernel,
        conv_bias,
        norm_gain,
        norm_bias,
        weight_in,
        bias_in,
        weight_out,
        bias_out,
        layer_scale,
    )
    height = state.shape[0]
    breadth = state.shape[1]
    grad_norm = 1.0 / math.sqrt(lax.axis_size("lat") * height * lax.axis_size("lon") * breadth)
    current = state
    windows = []
    stored_all = []
    for layer_index in range(BLOCKS):
        params = tuple((member[layer_index] for member in stacked))
        window = extend(current)
        windows.append(window)
        outcome = block_forward(window, land_sea, params)
        current = outcome[0]
        stored_all.append(outcome[1])
    incoming = cotangent
    per_layer = [None] * BLOCKS
    for layer_index in reversed(range(BLOCKS)):
        params = tuple((member[layer_index] for member in stacked))
        stored = stored_all[layer_index]
        grad_mixed, masked, gradients = block_backward(
            windows[layer_index], land_sea, incoming, params, stored
        )
        incoming = adjoint(extend(grad_mixed), masked, params[0])
        per_layer[layer_index] = gradients
    combined = tuple(
        (
            jnp.stack([per_layer[layer_index][member] for layer_index in range(BLOCKS)])
            for member in range(9)
        )
    )
    scaled = sum_everything(combined, grad_norm)
    return (
        current,
        incoming,
        scaled[0],
        scaled[1],
        scaled[2],
        scaled[3],
        scaled[4],
        scaled[5],
        scaled[6],
        scaled[7],
        scaled[8],
    )


def solution(mesh):
    placed = (
        P("lat", "lon", None),
        P("lat", "lon"),
        P("lat", "lon", None),
        P(),
        P(),
        P(),
        P(),
        P(),
        P(),
        P(),
        P(),
        P(),
    )
    return jax.shard_map(
        on_device,
        mesh=mesh,
        in_specs=placed,
        out_specs=(
            P("lat", "lon", None),
            P("lat", "lon", None),
            P(),
            P(),
            P(),
            P(),
            P(),
            P(),
            P(),
            P(),
            P(),
        ),
        check_vma=False,
    )
```

```python
import math

import jax
import jax.numpy as jnp
from jax import lax
from jax.experimental import pallas as pl
from jax.experimental.pallas import tpu as pltpu
from jax.sharding import PartitionSpec as P

KSIZE = 7
BLOCKS = 2
C = 128
F = 512
EPS_NORM = 1e-06
INV_ROOT_TWO = 0.7071067811865476
INV_ROOT_TWO_PI = 0.3989422804014327
MESH_ID = pl.DeviceIdType.MESH
GROUP = 16
ROWS = 45
COLS = 24
MARGIN = 3
AROUND = ((1, 0), (-1, 0), (0, 1), (0, -1), (1, 1), (1, -1), (-1, 1), (-1, -1))
STRIP = 9
CHUNKS = ROWS // STRIP
CELLS = STRIP * COLS


def position():
    lon = lax.axis_index("lon")
    lat = lax.axis_index("lat")
    z = lon // 4
    y_hi = lax.rem(lon // 2, 2)
    core = lax.rem(lon, 2)
    plane = y_hi * 8 + lat
    line = z * 2 + core
    return plane, line


def plane_peer(plane, line):
    lon = (line // 2) * 4 + (plane // 8) * 2 + lax.rem(line, 2)
    return {"lon": lon, "lat": lax.rem(plane, 8)}


def beside(east, south):
    return {
        "lon": lax.rem(lax.axis_index("lon") + east + 32, 32),
        "lat": lax.rem(lax.axis_index("lat") + south + 8, 8),
    }


def greet(barrier):
    plane, line = position()

    def one(k, carry):
        other = lax.rem(plane + k, GROUP)
        pl.semaphore_signal(
            barrier, inc=1, device_id=plane_peer(other, line), device_id_type=MESH_ID
        )
        other = lax.rem(line + k, GROUP)
        pl.semaphore_signal(
            barrier, inc=1, device_id=plane_peer(plane, other), device_id_type=MESH_ID
        )
        return carry

    lax.fori_loop(1, GROUP, one, 0)
    for east, south in AROUND:
        pl.semaphore_signal(
            barrier, inc=1, device_id=beside(east, south), device_id_type=MESH_ID
        )
    pl.semaphore_wait(barrier, 2 * (GROUP - 1) + len(AROUND))


class Exchange:
    def __init__(self, kind, scatter, src, dst, send, recv):
        self.plane, self.line = position()
        self.kind = kind
        self.scatter = scatter
        self.src, self.dst, self.send, self.recv = src, dst, send, recv
        self.me = self.plane if kind == "plane" else self.line

    def copy(self, k):
        other = lax.rem(self.me + k, GROUP)
        if self.kind == "plane":
            target = plane_peer(other, self.line)
        else:
            target = plane_peer(self.plane, other)
        src = self.src.at[other] if self.scatter else self.src
        return pltpu.make_async_remote_copy(
            src_ref=src,
            dst_ref=self.dst.at[k],
            send_sem=self.send.at[k],
            recv_sem=self.recv.at[k],
            device_id=target,
            device_id_type=MESH_ID,
        )

    def start(self):
        def one(k, carry):
            self.copy(k).start()
            return carry

        lax.fori_loop(1, GROUP, one, 0)

    def wait(self):
        def one(k, carry):
            self.copy(k).wait()
            return carry

        lax.fori_loop(1, GROUP, one, 0)


def slot_sum(own, slots, count=GROUP):
    def one(k, total):
        return total + slots[k].astype(jnp.float32)

    return lax.fori_loop(1, count, one, own)


def f32(value):
    return value.astype(jnp.float32)


def bf16(value):
    return value.astype(jnp.bfloat16)


class Halo:
    def __init__(self, bufs, sems, index, window):
        east, west, north, south, from_west, from_east, from_north, from_south = (
            ref.at[index] for ref in bufs
        )
        self.bufs = (east, west, north, south, from_west, from_east, from_north, from_south)
        self.window = window
        last = ROWS - MARGIN
        tall = pl.ds(MARGIN, ROWS)
        above, below = pl.ds(0, MARGIN), pl.ds(MARGIN + ROWS, MARGIN)
        top, bottom = pl.ds(0, MARGIN), pl.ds(last, MARGIN)
        pairs = (
            (east, from_west.at[tall]),
            (west, from_east.at[tall]),
            (south, from_north),
            (north, from_south),
            (east.at[bottom], from_west.at[above]),
            (east.at[top], from_west.at[below]),
            (west.at[bottom], from_east.at[above]),
            (west.at[top], from_east.at[below]),
        )
        self.copies = [
            pltpu.make_async_remote_copy(
                src_ref=pair[0],
                dst_ref=pair[1],
                send_sem=sems.at[index, 0, k],
                recv_sem=sems.at[index, 1, k],
                device_id=beside(*AROUND[k]),
                device_id_type=MESH_ID,
            )
            for k, pair in enumerate(pairs)
        ]

    def start(self):
        east, west, north, south = self.bufs[:4]
        window = self.window
        inner = slice(MARGIN, MARGIN + ROWS)
        east[...] = bf16(window[inner, COLS : COLS + MARGIN, :])
        west[...] = bf16(window[inner, MARGIN : 2 * MARGIN, :])
        north[...] = bf16(window[MARGIN : 2 * MARGIN, MARGIN : MARGIN + COLS, :])
        south[...] = bf16(window[ROWS : ROWS + MARGIN, MARGIN : MARGIN + COLS, :])
        for copy in self.copies:
            copy.start()

    def finish(self):
        for copy in self.copies:
            copy.wait()
        from_west, from_east, from_north, from_south = self.bufs[4:]
        lat = lax.axis_index("lat")
        has_north = jnp.where(lat > 0, 1.0, 0.0).astype(jnp.float32)
        has_south = jnp.where(lat < 7, 1.0, 0.0).astype(jnp.float32)
        window = self.window
        inner = slice(MARGIN, MARGIN + ROWS)
        above, below = slice(0, MARGIN), slice(MARGIN + ROWS, 2 * MARGIN + ROWS)
        middle = slice(MARGIN, MARGIN + COLS)
        window[above, middle, :] = f32(from_north[...]) * has_north
        window[below, middle, :] = f32(from_south[...]) * has_south
        for ref, side in (
            (from_west, slice(0, MARGIN)),
            (from_east, slice(MARGIN + COLS, 2 * MARGIN + COLS)),
        ):
            window[inner, side, :] = f32(ref[inner])
            window[above, side, :] = f32(ref[above]) * has_north
            window[below, side, :] = f32(ref[below]) * has_south


def convolve(window, weight, first, flip):
    def rows(base):
        sums = first(base)
        for i in range(KSIZE + 2):
            for b in range(KSIZE):
                piece = window[base + i, b : b + COLS, :]
                for o in range(3):
                    a = i - o
                    if 0 <= a < KSIZE:
                        tap = weight(KSIZE - 1 - a, KSIZE - 1 - b) if flip else weight(a, b)
                        sums[o] = sums[o] + piece * tap
        return sums

    return rows


def fold(value):
    return jnp.sum(value.reshape(value.shape[0] // 8, 8, value.shape[1]), axis=0)


def lane_mean(value):
    return jnp.mean(value, axis=-1, keepdims=True)


def step_kernel(
    grad_norm,
    state,
    land_sea,
    cotangent,
    dw_kernel,
    conv_bias,
    norm_gain,
    norm_bias,
    weight_in,
    bias_in,
    weight_out,
    bias_out,
    layer_scale,
    out,
    grad_state,
    g_kernel,
    g_conv,
    g_gain,
    g_shift,
    g_win,
    g_bias_in,
    g_wout,
    g_bias_out,
    g_scale,
    win1,
    win2,
    gwin1,
    gwin2,
    taps,
    mask,
    mixed,
    hidden,
    active,
    slope,
    normed,
    inverse,
    branch,
    upstream,
    acc_win,
    acc_wout,
    acc_rows,
    acc_bias,
    acc_taps,
    h_east,
    h_west,
    h_north,
    h_south,
    h_from_west,
    h_from_east,
    h_from_north,
    h_from_south,
    sem_h,
    small,
    send_a,
    recv_a,
    send_b,
    recv_b,
    own_b,
    back_b,
    own_a,
    back_a,
    srecv_a,
    sown_b,
    srecv_b,
    sown_a,
    sback_a,
    sem_w,
    sem_s,
):
    plane, line = position()
    greet(pltpu.get_barrier_semaphore())
    halo_bufs = (
        h_east, h_west, h_north, h_south, h_from_west, h_from_east, h_from_north, h_from_south
    )
    middle = slice(MARGIN, MARGIN + COLS)

    def widen(c, carry):
        win1[pl.ds(MARGIN + c * STRIP, STRIP), middle, :] = f32(state[pl.ds(c * STRIP, STRIP)])
        return carry

    lax.fori_loop(0, CHUNKS, widen, 0)
    halo = Halo(halo_bufs, sem_h, 0, win1)
    halo.start()

    for blk in range(BLOCKS):
        for a in range(KSIZE):
            taps[blk, a, 0:KSIZE, :] = f32(dw_kernel[blk, a])
    eye = lax.broadcasted_iota(jnp.int32, (COLS, COLS), 0) == lax.broadcasted_iota(
        jnp.int32, (COLS, COLS), 1
    )
    ones = jnp.ones((COLS, C), jnp.float32)

    def spread(i, carry):
        row = jnp.broadcast_to(land_sea[pl.ds(i, 1), :].astype(jnp.float32), (COLS, COLS))
        mask[i] = jnp.dot(
            jnp.where(eye, row, 0.0), ones, preferred_element_type=jnp.float32
        )
        return carry

    lax.fori_loop(0, ROWS, spread, 0)
    acc_win[...] = jnp.zeros_like(acc_win)
    acc_wout[...] = jnp.zeros_like(acc_wout)
    acc_rows[...] = jnp.zeros_like(acc_rows)
    acc_bias[...] = jnp.zeros_like(acc_bias)
    acc_taps[...] = jnp.zeros_like(acc_taps)

    def mix(window, blk):
        start = jnp.broadcast_to(conv_bias[blk : blk + 1, :], (COLS, C))
        rows = convolve(
            window, lambda a, b: taps[blk, a, b : b + 1, :], lambda base: [start] * 3, False
        )

        def three(g, carry):
            sums = rows(g * 3)
            for o in range(3):
                mixed[g * 3 + o] = sums[o]
            return carry

        lax.fori_loop(0, ROWS // 3, three, 0)

    def forward(c, window, blk, keep):
        x = mixed[pl.ds(c * STRIP, STRIP)].reshape(CELLS, C)
        center = x - lane_mean(x)
        inv = lax.rsqrt(lane_mean(center * center) + EPS_NORM)
        norm = center * inv
        normed[keep] = norm
        inverse[keep] = jnp.broadcast_to(inv, (CELLS, C))
        lifted = bf16(norm * norm_gain[blk : blk + 1, :] + norm_bias[blk : blk + 1, :])
        hidden[...] = jnp.dot(lifted, weight_in[blk], preferred_element_type=jnp.float32)

        def gelu(t, carry):
            rows = pl.ds(pl.multiple_of(t * COLS, 8), COLS)
            h = hidden[rows, :] + bias_in[blk : blk + 1, :]
            cumulative = 0.5 * (1.0 + lax.erf(h * INV_ROOT_TWO))
            density = jnp.exp(-0.5 * h * h) * INV_ROOT_TWO_PI
            active[keep, rows, :] = h * cumulative
            slope[keep, rows, :] = cumulative + h * density
            return carry

        lax.fori_loop(0, STRIP, gelu, 0)
        act = bf16(active[keep])
        branch_c = (
            jnp.dot(act, weight_out[blk], preferred_element_type=jnp.float32)
            + bias_out[blk : blk + 1, :]
        )
        branch[keep] = branch_c
        inner = window[pl.ds(MARGIN + c * STRIP, STRIP), middle, :].reshape(CELLS, C)
        ocean = mask[pl.ds(c * STRIP, STRIP)].reshape(CELLS, C)
        return (inner + layer_scale[blk : blk + 1, :] * branch_c) * ocean

    def backward(c, incoming, gwindow, blk, keep):
        ocean = mask[pl.ds(c * STRIP, STRIP)].reshape(CELLS, C)
        masked = incoming * ocean
        upstream[pl.ds(c * STRIP, STRIP)] = masked.reshape(STRIP, COLS, C)
        gb = bf16(masked * layer_scale[blk : blk + 1, :])
        acc_rows[blk, 4] += fold(masked * branch[keep])
        acc_rows[blk, 3] += fold(f32(gb))
        rows_rows = (((0,), (0,)), ((), ()))
        cols_cols = (((1,), (1,)), ((), ()))
        acc_wout[blk] += lax.dot_general(
            gb, bf16(active[keep]), rows_rows, preferred_element_type=jnp.float32
        )
        hidden[...] = lax.dot_general(
            gb, weight_out[blk], cols_cols, preferred_element_type=jnp.float32
        )

        def through(t, total):
            rows = pl.ds(pl.multiple_of(t * COLS, 8), COLS)
            gh = f32(bf16(hidden[rows, :] * slope[keep, rows, :]))
            hidden[rows, :] = gh
            return total + fold(gh)

        acc_bias[blk] = lax.fori_loop(0, STRIP, through, acc_bias[blk])
        gh = bf16(hidden[...])
        norm = normed[keep]
        gain = norm_gain[blk : blk + 1, :]
        lifted = bf16(norm * gain + norm_bias[blk : blk + 1, :])
        acc_win[blk] += lax.dot_general(
            lifted, gh, rows_rows, preferred_element_type=jnp.float32
        )
        gl = lax.dot_general(gh, weight_in[blk], cols_cols, preferred_element_type=jnp.float32)
        acc_rows[blk, 1] += fold(gl * norm)
        acc_rows[blk, 2] += fold(gl)
        s = gl * gain
        gm = inverse[keep] * (s - lane_mean(s) - norm * lane_mean(s * norm))
        gm = f32(bf16(gm))
        acc_rows[blk, 0] += fold(gm)
        gwindow[pl.ds(MARGIN + c * STRIP, STRIP), middle, :] = gm.reshape(STRIP, COLS, C)

    def tap_sums(window, gwindow, blk):
        def three(g, carry):
            base = g * 3
            grads = [gwindow[base + MARGIN + o, middle, :] for o in range(3)]
            for b in range(KSIZE):
                parts = [None] * KSIZE
                for i in range(KSIZE + 2):
                    piece = window[base + i, b : b + COLS, :]
                    for o in range(3):
                        a = i - o
                        if 0 <= a < KSIZE:
                            term = piece * grads[o]
                            parts[a] = term if parts[a] is None else parts[a] + term
                for a in range(KSIZE):
                    acc_taps[blk, a * KSIZE + b] += fold(parts[a])
            return carry

        lax.fori_loop(0, ROWS // 3, three, 0)

    def adjoint(gwindow, blk, put):
        rows = convolve(
            gwindow,
            lambda a, b: taps[blk, a, b : b + 1, :],
            lambda base: [upstream[base + o] for o in range(3)],
            True,
        )

        def three(g, carry):
            sums = rows(g * 3)
            for o in range(3):
                put(g * 3 + o, sums[o])
            return carry

        lax.fori_loop(0, ROWS // 3, three, 0)

    def scatter_weights(blk):
        for q in range(4):
            for half in range(2):
                send_a[blk, 2 * q + half] = bf16(
                    acc_win[blk, half * 64 : half * 64 + 64, q * 128 : q * 128 + 128]
                )
            turned = jnp.transpose(acc_wout[blk, :, q * 128 : q * 128 + 128])
            for half in range(2):
                send_a[blk, 8 + 2 * q + half] = bf16(turned[half * 64 : half * 64 + 64])
        ex = Exchange(
            "plane", True, send_a.at[blk], recv_a.at[blk], sem_w.at[blk, 0], sem_w.at[blk, 1]
        )
        ex.start()
        return ex

    def line_scatter(ex, blk):
        ex.wait()
        total = slot_sum(f32(send_a[blk, plane]), recv_a.at[blk])
        for j in range(GROUP):
            send_b[blk, j] = total[j * 4 : j * 4 + 4]
        ex = Exchange(
            "line", True, send_b.at[blk], recv_b.at[blk], sem_w.at[blk, 2], sem_w.at[blk, 3]
        )
        ex.start()
        return ex

    def line_gather(ex, blk):
        ex.wait()
        own_b[blk] = slot_sum(send_b[blk, line], recv_b.at[blk])
        ex = Exchange(
            "line", False, own_b.at[blk], back_b.at[blk], sem_w.at[blk, 4], sem_w.at[blk, 5]
        )
        ex.start()
        return ex

    def plane_gather(ex, blk):
        ex.wait()
        back_b[blk, 0] = own_b[blk]
        for j in range(GROUP):
            sub = back_b[blk, lax.rem(line - j + GROUP, GROUP)]
            own_a[blk, j * 4 : j * 4 + 4] = bf16(sub)
        ex = Exchange(
            "plane", False, own_a.at[blk], back_a.at[blk], sem_w.at[blk, 6], sem_w.at[blk, 7]
        )
        ex.start()
        return ex

    def finish_weights(ex, blk):
        ex.wait()
        back_a[blk, 0] = own_a[blk]
        for p in range(GROUP):
            piece = f32(back_a[blk, lax.rem(plane - p + GROUP, GROUP)]) * grad_norm
            if p < 8:
                g_win[
                    blk, (p % 2) * 64 : (p % 2) * 64 + 64, (p // 2) * 128 : (p // 2) * 128 + 128
                ] = piece
            else:
                g_wout[blk, (p - 8) * 64 : (p - 8) * 64 + 64] = piece

    def small_row(blk, r, value):
        i = blk * 4 + r % 4
        small[r // 4, i : i + 1, :] = jnp.sum(value, axis=0, keepdims=True)

    def pack_rows(blk):
        for tap in range(KSIZE * KSIZE):
            small_row(blk, tap, acc_taps[blk, tap])
        for k in range(5):
            small_row(blk, 49 + k, acc_rows[blk, k])
        for q in range(4):
            small_row(blk, 54 + q, acc_bias[blk, :, q * 128 : q * 128 + 128])

    halo.finish()
    mix(win1, 0)

    def forward_one(c, carry):
        result = forward(c, win1, 0, c)
        win2[pl.ds(MARGIN + c * STRIP, STRIP), middle, :] = f32(bf16(result)).reshape(
            STRIP, COLS, C
        )
        return carry

    lax.fori_loop(0, CHUNKS, forward_one, 0)
    halo = Halo(halo_bufs, sem_h, 1, win2)
    halo.start()
    small[...] = jnp.zeros_like(small)
    halo.finish()
    mix(win2, 1)

    def both(c, carry):
        result = forward(c, win2, 1, CHUNKS)
        out[pl.ds(c * STRIP, STRIP)] = bf16(result.reshape(STRIP, COLS, C))
        incoming = f32(cotangent[pl.ds(c * STRIP, STRIP)]).reshape(CELLS, C)
        backward(c, incoming, gwin2, 1, CHUNKS)
        return carry

    lax.fori_loop(0, CHUNKS, both, 0)
    halo = Halo(halo_bufs, sem_h, 2, gwin2)
    halo.start()
    second = scatter_weights(1)
    tap_sums(win2, gwin2, 1)
    halo.finish()

    def put_mixed(row, value):
        mixed[row] = f32(bf16(value))

    adjoint(gwin2, 1, put_mixed)
    second = line_scatter(second, 1)

    def backward_one(c, carry):
        incoming = mixed[pl.ds(c * STRIP, STRIP)].reshape(CELLS, C)
        backward(c, incoming, gwin1, 0, c)
        return carry

    lax.fori_loop(0, CHUNKS, backward_one, 0)
    halo = Halo(halo_bufs, sem_h, 3, gwin1)
    halo.start()
    first = scatter_weights(0)
    second = line_gather(second, 1)
    tap_sums(win1, gwin1, 0)
    pack_rows(1)
    pack_rows(0)
    tiny = Exchange("plane", True, small, srecv_a, sem_s.at[0], sem_s.at[1])
    tiny.start()
    first = line_scatter(first, 0)
    halo.finish()

    def put_state(row, value):
        grad_state[row] = bf16(value)

    adjoint(gwin1, 0, put_state)
    first = line_gather(first, 0)
    tiny.wait()
    sown_b[...] = slot_sum(small[plane], srecv_a)
    tiny = Exchange("line", False, sown_b, srecv_b, sem_s.at[2], sem_s.at[3])
    tiny.start()
    second = plane_gather(second, 1)
    first = plane_gather(first, 0)
    tiny.wait()
    sown_a[...] = slot_sum(sown_b[...], srecv_b)
    tiny = Exchange("plane", False, sown_a, sback_a, sem_s.at[4], sem_s.at[5])
    tiny.start()
    finish_weights(second, 1)
    finish_weights(first, 0)
    tiny.wait()
    sback_a[0] = sown_a[...]
    for p in range(GROUP):
        small[p] = sback_a[lax.rem(plane - p + GROUP, GROUP)] * grad_norm
    for blk in range(BLOCKS):

        def row_of(r):
            return small[r // 4, blk * 4 + r % 4 : blk * 4 + r % 4 + 1, :]

        for a in range(KSIZE):
            for b in range(KSIZE):
                g_kernel[blk, a, b : b + 1, :] = row_of(a * KSIZE + b)
        for k, ref in enumerate((g_conv, g_gain, g_shift, g_bias_out, g_scale)):
            ref[blk : blk + 1, :] = row_of(49 + k)
        for q in range(4):
            g_bias_in[blk : blk + 1, q * 128 : q * 128 + 128] = row_of(54 + q)


def on_device(*arrays):
    vmem = pl.BlockSpec(memory_space=pltpu.VMEM)
    grad_norm = 1.0 / math.sqrt(
        lax.axis_size("lat") * ROWS * lax.axis_size("lon") * COLS
    )
    field = jax.ShapeDtypeStruct((ROWS, COLS, C), jnp.bfloat16)
    row = jax.ShapeDtypeStruct((BLOCKS, C), jnp.float32)

    def vm(*shape, dtype=jnp.float32):
        return pltpu.VMEM(shape, dtype)

    tall, wide = ROWS + 2 * MARGIN, COLS + 8
    half = jnp.bfloat16
    return pl.pallas_call(
        lambda *refs: step_kernel(grad_norm, *refs),
        name="ocean_step",
        out_shape=(
            field,
            field,
            jax.ShapeDtypeStruct((BLOCKS, KSIZE, KSIZE, C), jnp.float32),
            row,
            row,
            row,
            jax.ShapeDtypeStruct((BLOCKS, C, F), jnp.float32),
            jax.ShapeDtypeStruct((BLOCKS, F), jnp.float32),
            jax.ShapeDtypeStruct((BLOCKS, F, C), jnp.float32),
            row,
            row,
        ),
        in_specs=[vmem] * 12,
        out_specs=(vmem,) * 11,
        scratch_shapes=[
            vm(tall, wide, C),
            vm(tall, wide, C),
            vm(tall, wide, C),
            vm(tall, wide, C),
            vm(BLOCKS, KSIZE, 8, C),
            vm(ROWS, COLS, C),
            vm(ROWS, COLS, C),
            vm(CELLS, F),
            vm(CHUNKS + 1, CELLS, F),
            vm(CHUNKS + 1, CELLS, F),
            vm(CHUNKS + 1, CELLS, C),
            vm(CHUNKS + 1, CELLS, C),
            vm(CHUNKS + 1, CELLS, C),
            vm(ROWS, COLS, C),
            vm(BLOCKS, C, F),
            vm(BLOCKS, C, F),
            vm(BLOCKS, 5, 8, C),
            vm(BLOCKS, 8, F),
            vm(BLOCKS, KSIZE * KSIZE, 8, C),
            vm(4, ROWS, MARGIN, C, dtype=half),
            vm(4, ROWS, MARGIN, C, dtype=half),
            vm(4, MARGIN, COLS, C, dtype=half),
            vm(4, MARGIN, COLS, C, dtype=half),
            vm(4, tall, MARGIN, C, dtype=half),
            vm(4, tall, MARGIN, C, dtype=half),
            vm(4, MARGIN, COLS, C, dtype=half),
            vm(4, MARGIN, COLS, C, dtype=half),
            pltpu.SemaphoreType.DMA((4, 2, len(AROUND))),
            vm(GROUP, 8, C),
            vm(BLOCKS, GROUP, 64, C, dtype=half),
            vm(BLOCKS, GROUP, 64, C, dtype=half),
            vm(BLOCKS, GROUP, 4, C),
            vm(BLOCKS, GROUP, 4, C),
            vm(BLOCKS, 4, C),
            vm(BLOCKS, GROUP, 4, C),
            vm(BLOCKS, 64, C, dtype=half),
            vm(BLOCKS, GROUP, 64, C, dtype=half),
            vm(GROUP, 8, C),
            vm(8, C),
            vm(GROUP, 8, C),
            vm(8, C),
            vm(GROUP, 8, C),
            pltpu.SemaphoreType.DMA((BLOCKS, 8, GROUP)),
            pltpu.SemaphoreType.DMA((6, GROUP)),
        ],
        compiler_params=pltpu.CompilerParams(
            collective_id=0, has_side_effects=True, vmem_limit_bytes=56 << 20
        ),
    )(*arrays)


def solution(mesh):
    field = P("lat", "lon", None)
    return jax.shard_map(
        on_device,
        mesh=mesh,
        in_specs=(field, P("lat", "lon"), field) + (P(),) * 9,
        out_specs=(field, field) + (P(),) * 9,
        check_vma=False,
    )
```

```python
import math

import jax
import jax.numpy as jnp
from jax import lax
from jax.experimental import pallas as pl
from jax.experimental.pallas import tpu as pltpu
from jax.sharding import PartitionSpec as P

KSIZE = 7
BLOCKS = 2
C = 128
F = 512
EPS_NORM = 1e-06
INV_ROOT_TWO = 0.7071067811865476
INV_ROOT_TWO_PI = 0.3989422804014327
MESH_ID = pl.DeviceIdType.MESH
GROUP = 16
LINE = 8
PIECE = 32
PART = PIECE // LINE
ROWS = 45
COLS = 24
MARGIN = 3
AROUND = ((1, 0), (-1, 0), (0, 1), (0, -1), (1, 1), (1, -1), (-1, 1), (-1, -1))
STRIP = 9
CHUNKS = ROWS // STRIP
CELLS = STRIP * COLS


def position():
    lon = lax.axis_index("lon")
    plane = lax.rem(lon // 2, 2) * 8 + lax.axis_index("lat")
    return plane, lon // 4, lax.rem(lon, 2)


def device(plane, z, core):
    return {"lon": z * 4 + (plane // 8) * 2 + core, "lat": lax.rem(plane, 8)}


def beside(east, south):
    return {
        "lon": lax.rem(lax.axis_index("lon") + east + 32, 32),
        "lat": lax.rem(lax.axis_index("lat") + south + 8, 8),
    }


def greet(barrier):
    plane, z, core = position()

    def signal(target):
        pl.semaphore_signal(barrier, inc=1, device_id=target, device_id_type=MESH_ID)

    for east, south in AROUND:
        signal(beside(east, south))
    signal(device(plane, z, 1 - core))

    def in_plane(k, carry):
        signal(device(lax.rem(plane + k, GROUP), z, core))
        return carry

    def in_line(k, carry):
        signal(device(plane, lax.rem(z + k, LINE), core))
        return carry

    lax.fori_loop(1, GROUP, in_plane, 0)
    lax.fori_loop(1, LINE, in_line, 0)
    pl.semaphore_wait(barrier, GROUP + LINE - 1 + len(AROUND))


class Exchange:
    def __init__(self, kind, scatter, src, dst, sems):
        self.plane, self.z, self.core = position()
        self.kind, self.scatter = kind, scatter
        self.src, self.dst, self.sems = src, dst, sems
        self.me, self.size = (self.plane, GROUP) if kind == "plane" else (self.z, LINE)

    def copy(self, k, arriving):
        other = lax.rem(self.me + k, self.size)
        if self.kind == "plane":
            target = device(other, self.z, self.core)
        else:
            target = device(self.plane, other, self.core)
        if self.scatter:
            src, slot = self.src.at[other], k
        else:
            src = self.src
            slot = lax.rem(self.me - k + self.size, self.size) if arriving else self.me
        return pltpu.make_async_remote_copy(
            src_ref=src,
            dst_ref=self.dst.at[slot],
            send_sem=self.sems.at[0, k],
            recv_sem=self.sems.at[1, k],
            device_id=target,
            device_id_type=MESH_ID,
        )

    def start(self):
        def one(k, carry):
            self.copy(k, False).start()
            return carry

        lax.fori_loop(1, self.size, one, 0)
        return self

    def wait(self):
        def one(k, carry):
            self.copy(k, True).wait()
            return carry

        lax.fori_loop(1, self.size, one, 0)


def to_sibling(src, dst, sems):
    plane, z, core = position()
    return pltpu.make_async_remote_copy(
        src_ref=src,
        dst_ref=dst,
        send_sem=sems.at[0],
        recv_sem=sems.at[1],
        device_id=device(plane, z, 1 - core),
        device_id_type=MESH_ID,
    )


def slot_sum(own, slots, count=GROUP):
    def one(k, total):
        return total + slots[k].astype(jnp.float32)

    return lax.fori_loop(1, count, one, own)


def f32(value):
    return value.astype(jnp.float32)


def bf16(value):
    return value.astype(jnp.bfloat16)


class Halo:
    def __init__(self, bufs, sems, index, window):
        east, west, north, south, from_west, from_east, from_north, from_south = (
            ref.at[index] for ref in bufs
        )
        self.bufs = (east, west, north, south, from_west, from_east, from_north, from_south)
        self.window = window
        last = ROWS - MARGIN
        tall = pl.ds(MARGIN, ROWS)
        above, below = pl.ds(0, MARGIN), pl.ds(MARGIN + ROWS, MARGIN)
        top, bottom = pl.ds(0, MARGIN), pl.ds(last, MARGIN)
        pairs = (
            (east, from_west.at[tall]),
            (west, from_east.at[tall]),
            (south, from_north),
            (north, from_south),
            (east.at[bottom], from_west.at[above]),
            (east.at[top], from_west.at[below]),
            (west.at[bottom], from_east.at[above]),
            (west.at[top], from_east.at[below]),
        )
        self.copies = [
            pltpu.make_async_remote_copy(
                src_ref=pair[0],
                dst_ref=pair[1],
                send_sem=sems.at[index, 0, k],
                recv_sem=sems.at[index, 1, k],
                device_id=beside(*AROUND[k]),
                device_id_type=MESH_ID,
            )
            for k, pair in enumerate(pairs)
        ]

    def start(self):
        east, west, north, south = self.bufs[:4]
        window = self.window
        inner = slice(MARGIN, MARGIN + ROWS)
        east[...] = bf16(window[inner, COLS : COLS + MARGIN, :])
        west[...] = bf16(window[inner, MARGIN : 2 * MARGIN, :])
        north[...] = bf16(window[MARGIN : 2 * MARGIN, MARGIN : MARGIN + COLS, :])
        south[...] = bf16(window[ROWS : ROWS + MARGIN, MARGIN : MARGIN + COLS, :])
        for copy in self.copies:
            copy.start()

    def finish(self):
        for copy in self.copies:
            copy.wait()
        from_west, from_east, from_north, from_south = self.bufs[4:]
        lat = lax.axis_index("lat")
        has_north = jnp.where(lat > 0, 1.0, 0.0).astype(jnp.float32)
        has_south = jnp.where(lat < 7, 1.0, 0.0).astype(jnp.float32)
        window = self.window
        inner = slice(MARGIN, MARGIN + ROWS)
        above, below = slice(0, MARGIN), slice(MARGIN + ROWS, 2 * MARGIN + ROWS)
        middle = slice(MARGIN, MARGIN + COLS)
        window[above, middle, :] = f32(from_north[...]) * has_north
        window[below, middle, :] = f32(from_south[...]) * has_south
        for ref, side in (
            (from_west, slice(0, MARGIN)),
            (from_east, slice(MARGIN + COLS, 2 * MARGIN + COLS)),
        ):
            window[inner, side, :] = f32(ref[inner])
            window[above, side, :] = f32(ref[above]) * has_north
            window[below, side, :] = f32(ref[below]) * has_south


def convolve(window, weight, first, flip):
    def rows(base):
        sums = first(base)
        for i in range(KSIZE + 2):
            for b in range(KSIZE):
                piece = window[base + i, b : b + COLS, :]
                for o in range(3):
                    a = i - o
                    if 0 <= a < KSIZE:
                        tap = weight(KSIZE - 1 - a, KSIZE - 1 - b) if flip else weight(a, b)
                        sums[o] = sums[o] + piece * tap
        return sums

    return rows


def fold(value):
    return jnp.sum(value.reshape(value.shape[0] // 8, 8, value.shape[1]), axis=0)


def lane_mean(value):
    return jnp.mean(value, axis=-1, keepdims=True)


def step_kernel(
    state,
    land_sea,
    cotangent,
    dw_kernel,
    conv_bias,
    norm_gain,
    norm_bias,
    weight_in,
    bias_in,
    weight_out,
    bias_out,
    layer_scale,
    out,
    grad_state,
    gathered,
    win1,
    win2,
    gwin1,
    gwin2,
    taps,
    mask,
    mixed,
    hidden,
    active,
    slope,
    normed,
    inverse,
    branch,
    upstream,
    acc_win,
    acc_wout,
    acc_rows,
    acc_bias,
    acc_taps,
    h_east,
    h_west,
    h_north,
    h_south,
    h_from_west,
    h_from_east,
    h_from_north,
    h_from_south,
    sem_h,
    small,
    halves,
    from_core,
    send_a,
    recv_a,
    tiny_a,
    line_send,
    line_recv,
    line_own,
    line_all,
    piece,
    total,
    both_halves,
    seeds,
    pulled,
    sem_core,
    sem_a,
    sem_tiny,
    sem_line,
    sem_back,
):
    plane, z, core = position()
    greet(pltpu.get_barrier_semaphore())
    halo_bufs = (
        h_east, h_west, h_north, h_south, h_from_west, h_from_east, h_from_north, h_from_south
    )
    middle = slice(MARGIN, MARGIN + COLS)

    def widen(c, carry):
        win1[pl.ds(MARGIN + c * STRIP, STRIP), middle, :] = f32(state[pl.ds(c * STRIP, STRIP)])
        return carry

    lax.fori_loop(0, CHUNKS, widen, 0)
    halo = Halo(halo_bufs, sem_h, 0, win1)
    halo.start()

    taps[...] = f32(dw_kernel[...])
    ocean_t = land_sea[...].astype(jnp.float32)
    for i in range(ROWS):
        mask[i] = jnp.broadcast_to(ocean_t[:, i : i + 1], (COLS, C))
    acc_win[...] = jnp.zeros_like(acc_win)
    acc_wout[...] = jnp.zeros_like(acc_wout)
    acc_rows[...] = jnp.zeros_like(acc_rows)
    acc_bias[...] = jnp.zeros_like(acc_bias)
    acc_taps[...] = jnp.zeros_like(acc_taps)

    def mix(window, blk):
        start = jnp.broadcast_to(conv_bias[blk : blk + 1, :], (COLS, C))
        rows = convolve(
            window, lambda a, b: taps[a, b, blk : blk + 1, :], lambda base: [start] * 3, False
        )

        def three(g, carry):
            sums = rows(g * 3)
            for o in range(3):
                mixed[g * 3 + o] = sums[o]
            return carry

        lax.fori_loop(0, ROWS // 3, three, 0)

    def forward(c, window, blk, keep):
        x = mixed[pl.ds(c * STRIP, STRIP)].reshape(CELLS, C)
        center = x - lane_mean(x)
        inv = lax.rsqrt(lane_mean(center * center) + EPS_NORM)
        norm = center * inv
        normed[keep] = norm
        inverse[keep] = jnp.broadcast_to(inv, (CELLS, C))
        lifted = bf16(norm * norm_gain[blk : blk + 1, :] + norm_bias[blk : blk + 1, :])
        hidden[...] = jnp.dot(lifted, weight_in[blk], preferred_element_type=jnp.float32)

        def gelu(t, carry):
            rows = pl.ds(pl.multiple_of(t * COLS, 8), COLS)
            h = hidden[rows, :] + bias_in[blk : blk + 1, :]
            cumulative = 0.5 * (1.0 + lax.erf(h * INV_ROOT_TWO))
            density = jnp.exp(-0.5 * h * h) * INV_ROOT_TWO_PI
            active[keep, rows, :] = h * cumulative
            slope[keep, rows, :] = cumulative + h * density
            return carry

        lax.fori_loop(0, STRIP, gelu, 0)
        act = bf16(active[keep])
        branch_c = (
            jnp.dot(act, weight_out[blk], preferred_element_type=jnp.float32)
            + bias_out[blk : blk + 1, :]
        )
        branch[keep] = branch_c
        inner = window[pl.ds(MARGIN + c * STRIP, STRIP), middle, :].reshape(CELLS, C)
        ocean = mask[pl.ds(c * STRIP, STRIP)].reshape(CELLS, C)
        return (inner + layer_scale[blk : blk + 1, :] * branch_c) * ocean

    def seed(c, incoming, blk):
        ocean = mask[pl.ds(c * STRIP, STRIP)].reshape(CELLS, C)
        masked = incoming * ocean
        upstream[pl.ds(c * STRIP, STRIP)] = masked.reshape(STRIP, COLS, C)
        gb = bf16(masked * layer_scale[blk : blk + 1, :])
        acc_rows[blk, 3] += fold(f32(gb))
        seeds[c] = gb
        pulled[c] = lax.dot_general(
            gb, weight_out[blk], (((1,), (1,)), ((), ())), preferred_element_type=jnp.float32
        )

    def backward(c, gwindow, blk, keep):
        masked = upstream[pl.ds(c * STRIP, STRIP)].reshape(CELLS, C)
        acc_rows[blk, 4] += fold(masked * branch[keep])
        rows_rows = (((0,), (0,)), ((), ()))
        cols_cols = (((1,), (1,)), ((), ()))
        acc_wout[blk] += lax.dot_general(
            seeds[c], bf16(active[keep]), rows_rows, preferred_element_type=jnp.float32
        )

        def through(t, total):
            rows = pl.ds(pl.multiple_of(t * COLS, 8), COLS)
            gh = f32(bf16(pulled[c, rows, :] * slope[keep, rows, :]))
            hidden[rows, :] = gh
            return total + fold(gh)

        acc_bias[blk] = lax.fori_loop(0, STRIP, through, acc_bias[blk])
        gh = bf16(hidden[...])
        norm = normed[keep]
        gain = norm_gain[blk : blk + 1, :]
        lifted = bf16(norm * gain + norm_bias[blk : blk + 1, :])
        acc_win[blk] += lax.dot_general(
            lifted, gh, rows_rows, preferred_element_type=jnp.float32
        )
        gl = lax.dot_general(gh, weight_in[blk], cols_cols, preferred_element_type=jnp.float32)
        acc_rows[blk, 1] += fold(gl * norm)
        acc_rows[blk, 2] += fold(gl)
        s = gl * gain
        gm = inverse[keep] * (s - lane_mean(s) - norm * lane_mean(s * norm))
        gm = f32(bf16(gm))
        acc_rows[blk, 0] += fold(gm)
        gwindow[pl.ds(MARGIN + c * STRIP, STRIP), middle, :] = gm.reshape(STRIP, COLS, C)

    def tap_sums(window, gwindow, blk, begin, end):
        def three(g, carry):
            base = g * 3
            grads = [gwindow[base + MARGIN + o, middle, :] for o in range(3)]
            for b in range(KSIZE):
                parts = [None] * KSIZE
                for i in range(KSIZE + 2):
                    piece = window[base + i, b : b + COLS, :]
                    for o in range(3):
                        a = i - o
                        if 0 <= a < KSIZE:
                            term = piece * grads[o]
                            parts[a] = term if parts[a] is None else parts[a] + term
                for a in range(KSIZE):
                    acc_taps[blk, a * KSIZE + b] += fold(parts[a])
            return carry

        lax.fori_loop(begin, end, three, 0)

    def adjoint(gwindow, blk, put, begin, end):
        rows = convolve(
            gwindow,
            lambda a, b: taps[a, b, blk : blk + 1, :],
            lambda base: [upstream[base + o] for o in range(3)],
            True,
        )

        def three(g, carry):
            sums = rows(g * 3)
            for o in range(3):
                put(g * 3 + o, sums[o])
            return carry

        lax.fori_loop(begin, end, three, 0)

    def core_sum(blk):
        for q in range(4):
            block = slice(q * 128, q * 128 + 128)
            halves[blk, 0, block, :] = bf16(acc_win[blk, :, block])
            halves[blk, 1, block, :] = bf16(jnp.transpose(acc_wout[blk, :, block]))
        copy = to_sibling(halves.at[blk, 1 - core], from_core.at[blk], sem_core.at[blk])
        copy.start()
        return copy

    def plane_sum(copy, blk):
        copy.wait()
        both = f32(halves[blk, core]) + f32(from_core[blk])
        send_a[blk] = bf16(both).reshape(GROUP, PIECE, C)
        return Exchange("plane", True, send_a.at[blk], recv_a.at[blk], sem_a.at[blk]).start()

    def add_slots(ex, blk):
        ex.wait()
        total[blk] = slot_sum(f32(send_a[blk, plane]), recv_a.at[blk])

    def small_row(blk, r, value):
        i = blk * 4 + r % 4
        small[r // 4, i : i + 1, :] = jnp.sum(value, axis=0, keepdims=True)

    def pack_rows(blk):
        for tap in range(KSIZE * KSIZE):
            small_row(blk, tap, acc_taps[blk, tap])
        for k in range(5):
            small_row(blk, 49 + k, acc_rows[blk, k])
        for q in range(4):
            small_row(blk, 54 + q, acc_bias[blk, :, q * 128 : q * 128 + 128])

    halo.finish()
    mix(win1, 0)

    def forward_one(c, carry):
        result = forward(c, win1, 0, c)
        win2[pl.ds(MARGIN + c * STRIP, STRIP), middle, :] = f32(bf16(result)).reshape(
            STRIP, COLS, C
        )
        return carry

    lax.fori_loop(0, CHUNKS, forward_one, 0)
    halo = Halo(halo_bufs, sem_h, 1, win2)
    halo.start()
    small[...] = jnp.zeros_like(small)

    def seed_two(c, carry):
        seed(c, f32(cotangent[pl.ds(c * STRIP, STRIP)]).reshape(CELLS, C), 1)
        return carry

    lax.fori_loop(0, CHUNKS, seed_two, 0)
    halo.finish()
    mix(win2, 1)

    def both(c, carry):
        result = forward(c, win2, 1, CHUNKS)
        out[pl.ds(c * STRIP, STRIP)] = bf16(result.reshape(STRIP, COLS, C))
        backward(c, gwin2, 1, CHUNKS)
        return carry

    lax.fori_loop(0, CHUNKS, both, 0)
    halo = Halo(halo_bufs, sem_h, 2, gwin2)
    halo.start()
    second = core_sum(1)
    tap_sums(win2, gwin2, 1, 0, 15)
    second = plane_sum(second, 1)
    halo.finish()

    def put_mixed(row, value):
        mixed[row] = f32(bf16(value))

    adjoint(gwin2, 1, put_mixed, 0, 15)

    def backward_one(c, carry):
        seed(c, mixed[pl.ds(c * STRIP, STRIP)].reshape(CELLS, C), 0)
        backward(c, gwin1, 0, c)
        return carry

    lax.fori_loop(0, CHUNKS, backward_one, 0)
    halo = Halo(halo_bufs, sem_h, 3, gwin1)
    halo.start()
    first = core_sum(0)
    pack_rows(1)
    tap_sums(win1, gwin1, 0, 0, 6)
    first = plane_sum(first, 0)
    tap_sums(win1, gwin1, 0, 6, 15)
    pack_rows(0)
    tiny = Exchange("plane", True, small, tiny_a, sem_tiny).start()
    halo.finish()

    def put_state(row, value):
        grad_state[row] = bf16(value)

    adjoint(gwin1, 0, put_state, 0, 8)
    add_slots(second, 1)
    add_slots(first, 0)
    tiny.wait()
    tiny_total = slot_sum(small[plane], tiny_a)
    for j in range(LINE):
        line_send[j, 0:PART] = total[0, j * PART : j * PART + PART]
        line_send[j, PART : 2 * PART] = total[1, j * PART : j * PART + PART]
        line_send[j, 2 * PART : 2 * PART + 1] = tiny_total[j : j + 1]
    line = Exchange("line", True, line_send, line_recv, sem_line.at[0]).start()
    adjoint(gwin1, 0, put_state, 8, 15)
    line.wait()
    own = slot_sum(line_send[z], line_recv, LINE)
    line_own[...] = own
    line = Exchange("line", False, line_own, line_all, sem_line.at[1]).start()
    line.wait()
    line_all[z] = own
    for j in range(LINE):
        piece[j * PART : j * PART + PART] = line_all[j, 0:PART]
        piece[PIECE + j * PART : PIECE + j * PART + PART] = line_all[j, PART : 2 * PART]
        piece[2 * PIECE + j : 2 * PIECE + j + 1] = line_all[j, 2 * PART : 2 * PART + 1]
    both_halves[core, plane] = bf16(piece[...])
    back = Exchange(
        "plane", False, both_halves.at[core, plane], both_halves.at[core], sem_back
    ).start()
    back.wait()
    swap = to_sibling(both_halves.at[core], both_halves.at[core], sem_core.at[BLOCKS])
    swap.start()
    swap.wait()
    gathered[...] = both_halves[...]


def write_kernel(
    grad_norm,
    out_from,
    state_from,
    gathered,
    out,
    grad_state,
    g_kernel,
    g_conv,
    g_gain,
    g_shift,
    g_win,
    g_bias_in,
    g_wout,
    g_bias_out,
    g_scale,
    small,
    sems,
):
    moves = [
        pltpu.make_async_copy(out_from, out, sems.at[0]),
        pltpu.make_async_copy(state_from, grad_state, sems.at[1]),
    ]
    for move in moves:
        move.start()
    for blk in range(BLOCKS):
        rows = slice(blk * PIECE, blk * PIECE + PIECE)
        for p in range(GROUP):
            g_win[
                blk, (p % 4) * PIECE : (p % 4) * PIECE + PIECE, (p // 4) * 128 : (p // 4) * 128 + 128
            ] = f32(gathered[0, p, rows, :]) * grad_norm
            g_wout[blk, p * PIECE : p * PIECE + PIECE] = f32(gathered[1, p, rows, :]) * grad_norm
    tiny = slice(2 * PIECE, 2 * PIECE + 8)
    for p in range(GROUP):
        small[p] = (f32(gathered[0, p, tiny, :]) + f32(gathered[1, p, tiny, :])) * grad_norm
    for blk in range(BLOCKS):

        def row_of(r):
            return small[r // 4, blk * 4 + r % 4 : blk * 4 + r % 4 + 1, :]

        for a in range(KSIZE):
            for b in range(KSIZE):
                g_kernel[a, b, blk : blk + 1, :] = row_of(a * KSIZE + b)
        for k, ref in enumerate((g_conv, g_gain, g_shift, g_bias_out, g_scale)):
            ref[blk : blk + 1, :] = row_of(49 + k)
        for q in range(4):
            g_bias_in[blk : blk + 1, q * 128 : q * 128 + 128] = row_of(54 + q)
    for move in moves:
        move.wait()


def on_device(
    state,
    land_sea,
    cotangent,
    dw_kernel,
    *rest,
):
    vmem = pl.BlockSpec(memory_space=pltpu.VMEM)
    anywhere = pl.BlockSpec(memory_space=pl.ANY)
    grad_norm = 1.0 / math.sqrt(
        lax.axis_size("lat") * ROWS * lax.axis_size("lon") * COLS
    )
    field = jax.ShapeDtypeStruct((ROWS, COLS, C), jnp.bfloat16)
    row = jax.ShapeDtypeStruct((BLOCKS, C), jnp.float32)

    def vm(*shape, dtype=jnp.float32):
        return pltpu.VMEM(shape, dtype)

    def sems(*shape):
        return pltpu.SemaphoreType.DMA(shape)

    tall, wide = ROWS + 2 * MARGIN, COLS + 8
    half = jnp.bfloat16
    packed = 2 * PIECE + 8
    fields = pl.pallas_call(
        step_kernel,
        name="ocean_step",
        out_shape=(
            field,
            field,
            jax.ShapeDtypeStruct((2, GROUP, packed, C), jnp.bfloat16),
        ),
        in_specs=[vmem] * 12,
        out_specs=(vmem,) * 3,
        scratch_shapes=[
            vm(tall, wide, C),
            vm(tall, wide, C),
            vm(tall, wide, C),
            vm(tall, wide, C),
            vm(KSIZE, KSIZE, BLOCKS, C),
            vm(ROWS, COLS, C),
            vm(ROWS, COLS, C),
            vm(CELLS, F),
            vm(CHUNKS + 1, CELLS, F),
            vm(CHUNKS + 1, CELLS, F),
            vm(CHUNKS + 1, CELLS, C),
            vm(CHUNKS + 1, CELLS, C),
            vm(CHUNKS + 1, CELLS, C),
            vm(ROWS, COLS, C),
            vm(BLOCKS, C, F),
            vm(BLOCKS, C, F),
            vm(BLOCKS, 5, 8, C),
            vm(BLOCKS, 8, F),
            vm(BLOCKS, KSIZE * KSIZE, 8, C),
            vm(4, ROWS, MARGIN, C, dtype=half),
            vm(4, ROWS, MARGIN, C, dtype=half),
            vm(4, MARGIN, COLS, C, dtype=half),
            vm(4, MARGIN, COLS, C, dtype=half),
            vm(4, tall, MARGIN, C, dtype=half),
            vm(4, tall, MARGIN, C, dtype=half),
            vm(4, MARGIN, COLS, C, dtype=half),
            vm(4, MARGIN, COLS, C, dtype=half),
            sems(4, 2, len(AROUND)),
            vm(GROUP, 8, C),
            vm(BLOCKS, 2, F, C, dtype=half),
            vm(BLOCKS, F, C, dtype=half),
            vm(BLOCKS, GROUP, PIECE, C, dtype=half),
            vm(BLOCKS, GROUP, PIECE, C, dtype=half),
            vm(GROUP, 8, C),
            vm(LINE, 2 * PART + 1, C),
            vm(LINE, 2 * PART + 1, C),
            vm(2 * PART + 1, C),
            vm(LINE, 2 * PART + 1, C),
            vm(packed, C),
            vm(BLOCKS, PIECE, C),
            vm(2, GROUP, packed, C, dtype=half),
            vm(CHUNKS, CELLS, C, dtype=half),
            vm(CHUNKS, CELLS, F),
            sems(BLOCKS + 1, 2),
            sems(BLOCKS, 2, GROUP),
            sems(2, GROUP),
            sems(2, 2, LINE),
            sems(2, GROUP),
        ],
        compiler_params=pltpu.CompilerParams(
            collective_id=0, has_side_effects=True, vmem_limit_bytes=40 << 20
        ),
    )(state, land_sea.T, cotangent, jnp.transpose(dw_kernel, (1, 2, 0, 3)), *rest)
    results = pl.pallas_call(
        lambda *refs: write_kernel(grad_norm, *refs),
        name="write_results",
        out_shape=(
            field,
            field,
            jax.ShapeDtypeStruct((KSIZE, KSIZE, BLOCKS, C), jnp.float32),
            row,
            row,
            row,
            jax.ShapeDtypeStruct((BLOCKS, C, F), jnp.float32),
            jax.ShapeDtypeStruct((BLOCKS, F), jnp.float32),
            jax.ShapeDtypeStruct((BLOCKS, F, C), jnp.float32),
            row,
            row,
        ),
        in_specs=[anywhere, anywhere, vmem],
        out_specs=(anywhere, anywhere) + (vmem,) * 9,
        scratch_shapes=[vm(GROUP, 8, C), sems(2)],
        compiler_params=pltpu.CompilerParams(vmem_limit_bytes=16 << 20),
    )(*fields)
    return results[:2] + (jnp.transpose(results[2], (2, 0, 1, 3)),) + results[3:]


def solution(mesh):
    field = P("lat", "lon", None)
    return jax.shard_map(
        on_device,
        mesh=mesh,
        in_specs=(field, P("lat", "lon"), field) + (P(),) * 9,
        out_specs=(field, field) + (P(),) * 9,
        check_vma=False,
    )
```

```python
import math

import jax
import jax.numpy as jnp
from jax import lax
from jax.experimental import pallas as pl
from jax.experimental.pallas import tpu as pltpu
from jax.sharding import PartitionSpec as P

KSIZE = 7
BLOCKS = 2
C = 128
F = 512
EPS_NORM = 1e-06
INV_ROOT_TWO = 0.7071067811865476
INV_ROOT_TWO_PI = 0.3989422804014327
MESH_ID = pl.DeviceIdType.MESH
GROUP = 16
LINE = 8
PIECE = 32
PART = PIECE // LINE
ROWS = 45
COLS = 24
MARGIN = 3
AROUND = ((1, 0), (-1, 0), (0, 1), (0, -1), (1, 1), (1, -1), (-1, 1), (-1, -1))
STRIP = 9
CHUNKS = ROWS // STRIP
CELLS = STRIP * COLS


def position():
    lon = lax.axis_index("lon")
    plane = lax.rem(lon // 2, 2) * 8 + lax.axis_index("lat")
    return plane, lon // 4, lax.rem(lon, 2)


def device(plane, z, core):
    return {"lon": z * 4 + (plane // 8) * 2 + core, "lat": lax.rem(plane, 8)}


def beside(east, south):
    return {
        "lon": lax.rem(lax.axis_index("lon") + east + 32, 32),
        "lat": lax.rem(lax.axis_index("lat") + south + 8, 8),
    }


def greet(barrier):
    plane, z, core = position()

    def signal(target):
        pl.semaphore_signal(barrier, inc=1, device_id=target, device_id_type=MESH_ID)

    for east, south in AROUND:
        signal(beside(east, south))
    signal(device(plane, z, 1 - core))

    def in_plane(k, carry):
        signal(device(lax.rem(plane + k, GROUP), z, core))
        return carry

    def in_line(k, carry):
        signal(device(plane, lax.rem(z + k, LINE), core))
        return carry

    lax.fori_loop(1, GROUP, in_plane, 0)
    lax.fori_loop(1, LINE, in_line, 0)
    pl.semaphore_wait(barrier, GROUP + LINE - 1 + len(AROUND))


class Exchange:
    def __init__(self, kind, scatter, src, dst, sems):
        self.plane, self.z, self.core = position()
        self.kind, self.scatter = kind, scatter
        self.src, self.dst, self.sems = src, dst, sems
        self.me, self.size = (self.plane, GROUP) if kind == "plane" else (self.z, LINE)

    def copy(self, k, arriving):
        other = lax.rem(self.me + k, self.size)
        if self.kind == "plane":
            target = device(other, self.z, self.core)
        else:
            target = device(self.plane, other, self.core)
        if self.scatter:
            src, slot = self.src.at[other], k
        else:
            src = self.src
            slot = lax.rem(self.me - k + self.size, self.size) if arriving else self.me
        return pltpu.make_async_remote_copy(
            src_ref=src,
            dst_ref=self.dst.at[slot],
            send_sem=self.sems.at[0, k],
            recv_sem=self.sems.at[1, k],
            device_id=target,
            device_id_type=MESH_ID,
        )

    def start(self):
        def one(k, carry):
            self.copy(k, False).start()
            return carry

        lax.fori_loop(1, self.size, one, 0)
        return self

    def wait(self):
        def one(k, carry):
            self.copy(k, True).wait()
            return carry

        lax.fori_loop(1, self.size, one, 0)


def to_sibling(src, dst, sems):
    plane, z, core = position()
    return pltpu.make_async_remote_copy(
        src_ref=src,
        dst_ref=dst,
        send_sem=sems.at[0],
        recv_sem=sems.at[1],
        device_id=device(plane, z, 1 - core),
        device_id_type=MESH_ID,
    )


def slot_sum(own, slots, count=GROUP):
    def one(k, total):
        return total + slots[k].astype(jnp.float32)

    return lax.fori_loop(1, count, one, own)


def f32(value):
    return value.astype(jnp.float32)


def bf16(value):
    return value.astype(jnp.bfloat16)


class Halo:
    def __init__(self, bufs, sems, index, window):
        east, west, north, south, from_west, from_east, from_north, from_south = (
            ref.at[index] for ref in bufs
        )
        self.bufs = (east, west, north, south, from_west, from_east, from_north, from_south)
        self.window = window
        last = ROWS - MARGIN
        tall = pl.ds(MARGIN, ROWS)
        above, below = pl.ds(0, MARGIN), pl.ds(MARGIN + ROWS, MARGIN)
        top, bottom = pl.ds(0, MARGIN), pl.ds(last, MARGIN)
        pairs = (
            (east, from_west.at[tall]),
            (west, from_east.at[tall]),
            (south, from_north),
            (north, from_south),
            (east.at[bottom], from_west.at[above]),
            (east.at[top], from_west.at[below]),
            (west.at[bottom], from_east.at[above]),
            (west.at[top], from_east.at[below]),
        )
        self.copies = [
            pltpu.make_async_remote_copy(
                src_ref=pair[0],
                dst_ref=pair[1],
                send_sem=sems.at[index, 0, k],
                recv_sem=sems.at[index, 1, k],
                device_id=beside(*AROUND[k]),
                device_id_type=MESH_ID,
            )
            for k, pair in enumerate(pairs)
        ]

    def start(self):
        self.stage()
        self.launch()

    def stage(self):
        east, west, north, south = self.bufs[:4]
        window = self.window
        inner = slice(MARGIN, MARGIN + ROWS)
        east[...] = bf16(window[inner, COLS : COLS + MARGIN, :])
        west[...] = bf16(window[inner, MARGIN : 2 * MARGIN, :])
        north[...] = bf16(window[MARGIN : 2 * MARGIN, MARGIN : MARGIN + COLS, :])
        south[...] = bf16(window[ROWS : ROWS + MARGIN, MARGIN : MARGIN + COLS, :])

    def launch(self):
        for copy in self.copies:
            copy.start()

    def finish(self):
        for copy in self.copies:
            copy.wait()
        from_west, from_east, from_north, from_south = self.bufs[4:]
        lat = lax.axis_index("lat")
        has_north = jnp.where(lat > 0, 1.0, 0.0).astype(jnp.float32)
        has_south = jnp.where(lat < 7, 1.0, 0.0).astype(jnp.float32)
        window = self.window
        inner = slice(MARGIN, MARGIN + ROWS)
        above, below = slice(0, MARGIN), slice(MARGIN + ROWS, 2 * MARGIN + ROWS)
        middle = slice(MARGIN, MARGIN + COLS)
        window[above, middle, :] = f32(from_north[...]) * has_north
        window[below, middle, :] = f32(from_south[...]) * has_south
        for ref, side in (
            (from_west, slice(0, MARGIN)),
            (from_east, slice(MARGIN + COLS, 2 * MARGIN + COLS)),
        ):
            window[inner, side, :] = f32(ref[inner])
            window[above, side, :] = f32(ref[above]) * has_north
            window[below, side, :] = f32(ref[below]) * has_south


def convolve(window, weight, first, flip):
    def rows(base):
        sums = first(base)
        for i in range(KSIZE + 2):
            for b in range(KSIZE):
                piece = window[base + i, b : b + COLS, :]
                for o in range(3):
                    a = i - o
                    if 0 <= a < KSIZE:
                        tap = weight(KSIZE - 1 - a, KSIZE - 1 - b) if flip else weight(a, b)
                        sums[o] = sums[o] + piece * tap
        return sums

    return rows


def fold(value):
    return jnp.sum(value.reshape(value.shape[0] // 8, 8, value.shape[1]), axis=0)


def lane_mean(value):
    return jnp.mean(value, axis=-1, keepdims=True)


def step_kernel(
    *refs,
):
    arguments, refs = refs[:12], refs[12:]
    (
    out_hbm,
    state_hbm,
    gathered,
    win1,
    win2,
    gwin1,
    gwin2,
    taps,
    mask,
    mixed,
    hidden,
    active,
    slope,
    normed,
    inverse,
    branch,
    upstream,
    acc_win,
    acc_wout,
    acc_rows,
    acc_bias,
    acc_taps,
    h_east,
    h_west,
    h_north,
    h_south,
    h_from_west,
    h_from_east,
    h_from_north,
    h_from_south,
    sem_h,
    small,
    halves,
    from_core,
    send_a,
    recv_a,
    tiny_a,
    line_send,
    line_recv,
    line_own,
    line_all,
    piece,
    total,
    both_halves,
    seeds,
    pulled,
    sem_core,
    sem_a,
    sem_tiny,
    sem_line,
    sem_back,
    sem_load,
    out,
    grad_state,
    sem_put,
    *arrived,
    ) = refs
    loads = [
        pltpu.make_async_copy(source, target, sem_load.at[n])
        for n, (source, target) in enumerate(zip(arguments, arrived))
    ]
    for load in loads:
        load.start()
    (
        state,
        land_sea,
        cotangent,
        dw_kernel,
        conv_bias,
        norm_gain,
        norm_bias,
        weight_in,
        bias_in,
        weight_out,
        bias_out,
        layer_scale,
    ) = arrived
    plane, z, core = position()
    loads[0].wait()
    halo_bufs = (
        h_east, h_west, h_north, h_south, h_from_west, h_from_east, h_from_north, h_from_south
    )
    middle = slice(MARGIN, MARGIN + COLS)

    def widen(c, carry):
        win1[pl.ds(MARGIN + c * STRIP, STRIP), middle, :] = f32(state[pl.ds(c * STRIP, STRIP)])
        return carry

    lax.fori_loop(0, CHUNKS, widen, 0)
    halo = Halo(halo_bufs, sem_h, 0, win1)
    halo.stage()
    greet(pltpu.get_barrier_semaphore())
    halo.launch()
    for load in loads[1:]:
        load.wait()

    taps[...] = f32(dw_kernel[...])
    ocean_t = land_sea[...].astype(jnp.float32)
    for i in range(ROWS):
        mask[i] = jnp.broadcast_to(ocean_t[:, i : i + 1], (COLS, C))
    acc_win[...] = jnp.zeros_like(acc_win)
    acc_wout[...] = jnp.zeros_like(acc_wout)
    acc_rows[...] = jnp.zeros_like(acc_rows)
    acc_bias[...] = jnp.zeros_like(acc_bias)
    acc_taps[...] = jnp.zeros_like(acc_taps)

    def mix(window, blk):
        start = jnp.broadcast_to(conv_bias[blk : blk + 1, :], (COLS, C))
        rows = convolve(
            window, lambda a, b: taps[a, b, blk : blk + 1, :], lambda base: [start] * 3, False
        )

        def three(g, carry):
            sums = rows(g * 3)
            for o in range(3):
                mixed[g * 3 + o] = sums[o]
            return carry

        lax.fori_loop(0, ROWS // 3, three, 0)

    def forward(c, window, blk, keep):
        x = mixed[pl.ds(c * STRIP, STRIP)].reshape(CELLS, C)
        center = x - lane_mean(x)
        inv = lax.rsqrt(lane_mean(center * center) + EPS_NORM)
        norm = center * inv
        normed[keep] = norm
        inverse[keep] = jnp.broadcast_to(inv, (CELLS, C))
        lifted = bf16(norm * norm_gain[blk : blk + 1, :] + norm_bias[blk : blk + 1, :])
        hidden[...] = jnp.dot(lifted, weight_in[blk], preferred_element_type=jnp.float32)

        def gelu(t, carry):
            rows = pl.ds(pl.multiple_of(t * COLS, 8), COLS)
            h = hidden[rows, :] + bias_in[blk : blk + 1, :]
            cumulative = 0.5 * (1.0 + lax.erf(h * INV_ROOT_TWO))
            density = jnp.exp(-0.5 * h * h) * INV_ROOT_TWO_PI
            active[keep, rows, :] = h * cumulative
            slope[keep, rows, :] = cumulative + h * density
            return carry

        lax.fori_loop(0, STRIP, gelu, 0)
        act = bf16(active[keep])
        branch_c = (
            jnp.dot(act, weight_out[blk], preferred_element_type=jnp.float32)
            + bias_out[blk : blk + 1, :]
        )
        branch[keep] = branch_c
        inner = window[pl.ds(MARGIN + c * STRIP, STRIP), middle, :].reshape(CELLS, C)
        ocean = mask[pl.ds(c * STRIP, STRIP)].reshape(CELLS, C)
        return (inner + layer_scale[blk : blk + 1, :] * branch_c) * ocean

    def seed(c, incoming, blk):
        ocean = mask[pl.ds(c * STRIP, STRIP)].reshape(CELLS, C)
        masked = incoming * ocean
        upstream[pl.ds(c * STRIP, STRIP)] = masked.reshape(STRIP, COLS, C)
        gb = bf16(masked * layer_scale[blk : blk + 1, :])
        acc_rows[blk, 3] += fold(f32(gb))
        seeds[c] = gb
        pulled[c] = lax.dot_general(
            gb, weight_out[blk], (((1,), (1,)), ((), ())), preferred_element_type=jnp.float32
        )

    def backward(c, gwindow, blk, keep):
        masked = upstream[pl.ds(c * STRIP, STRIP)].reshape(CELLS, C)
        acc_rows[blk, 4] += fold(masked * branch[keep])
        rows_rows = (((0,), (0,)), ((), ()))
        cols_cols = (((1,), (1,)), ((), ()))
        acc_wout[blk] += lax.dot_general(
            seeds[c], bf16(active[keep]), rows_rows, preferred_element_type=jnp.float32
        )

        def through(t, total):
            rows = pl.ds(pl.multiple_of(t * COLS, 8), COLS)
            gh = f32(bf16(pulled[c, rows, :] * slope[keep, rows, :]))
            hidden[rows, :] = gh
            return total + fold(gh)

        acc_bias[blk] = lax.fori_loop(0, STRIP, through, acc_bias[blk])
        gh = bf16(hidden[...])
        norm = normed[keep]
        gain = norm_gain[blk : blk + 1, :]
        lifted = bf16(norm * gain + norm_bias[blk : blk + 1, :])
        acc_win[blk] += lax.dot_general(
            lifted, gh, rows_rows, preferred_element_type=jnp.float32
        )
        gl = lax.dot_general(gh, weight_in[blk], cols_cols, preferred_element_type=jnp.float32)
        acc_rows[blk, 1] += fold(gl * norm)
        acc_rows[blk, 2] += fold(gl)
        s = gl * gain
        gm = inverse[keep] * (s - lane_mean(s) - norm * lane_mean(s * norm))
        gm = f32(bf16(gm))
        acc_rows[blk, 0] += fold(gm)
        gwindow[pl.ds(MARGIN + c * STRIP, STRIP), middle, :] = gm.reshape(STRIP, COLS, C)

    def tap_sums(window, gwindow, blk, begin, end):
        def three(g, carry):
            base = g * 3
            grads = [gwindow[base + MARGIN + o, middle, :] for o in range(3)]
            for b in range(KSIZE):
                parts = [None] * KSIZE
                for i in range(KSIZE + 2):
                    piece = window[base + i, b : b + COLS, :]
                    for o in range(3):
                        a = i - o
                        if 0 <= a < KSIZE:
                            term = piece * grads[o]
                            parts[a] = term if parts[a] is None else parts[a] + term
                for a in range(KSIZE):
                    acc_taps[blk, a * KSIZE + b] += fold(parts[a])
            return carry

        lax.fori_loop(begin, end, three, 0)

    def adjoint(gwindow, blk, put, begin, end):
        rows = convolve(
            gwindow,
            lambda a, b: taps[a, b, blk : blk + 1, :],
            lambda base: [upstream[base + o] for o in range(3)],
            True,
        )

        def three(g, carry):
            sums = rows(g * 3)
            for o in range(3):
                put(g * 3 + o, sums[o])
            return carry

        lax.fori_loop(begin, end, three, 0)

    def core_sum(blk):
        for q in range(4):
            block = slice(q * 128, q * 128 + 128)
            halves[blk, 0, block, :] = bf16(acc_win[blk, :, block])
            halves[blk, 1, block, :] = bf16(jnp.transpose(acc_wout[blk, :, block]))
        copy = to_sibling(halves.at[blk, 1 - core], from_core.at[blk], sem_core.at[blk])
        copy.start()
        return copy

    def plane_sum(copy, blk):
        copy.wait()
        both = f32(halves[blk, core]) + f32(from_core[blk])
        send_a[blk] = bf16(both).reshape(GROUP, PIECE, C)
        return Exchange("plane", True, send_a.at[blk], recv_a.at[blk], sem_a.at[blk]).start()

    def add_slots(ex, blk):
        ex.wait()
        total[blk] = slot_sum(f32(send_a[blk, plane]), recv_a.at[blk])

    def small_row(blk, r, value):
        i = blk * 4 + r % 4
        small[r // 4, i : i + 1, :] = jnp.sum(value, axis=0, keepdims=True)

    def pack_rows(blk):
        for tap in range(KSIZE * KSIZE):
            small_row(blk, tap, acc_taps[blk, tap])
        for k in range(5):
            small_row(blk, 49 + k, acc_rows[blk, k])
        for q in range(4):
            small_row(blk, 54 + q, acc_bias[blk, :, q * 128 : q * 128 + 128])

    halo.finish()
    mix(win1, 0)

    def forward_one(c, carry):
        result = forward(c, win1, 0, c)
        win2[pl.ds(MARGIN + c * STRIP, STRIP), middle, :] = f32(bf16(result)).reshape(
            STRIP, COLS, C
        )
        return carry

    lax.fori_loop(0, CHUNKS, forward_one, 0)
    halo = Halo(halo_bufs, sem_h, 1, win2)
    halo.start()
    small[...] = jnp.zeros_like(small)

    def seed_two(c, carry):
        seed(c, f32(cotangent[pl.ds(c * STRIP, STRIP)]).reshape(CELLS, C), 1)
        return carry

    lax.fori_loop(0, CHUNKS, seed_two, 0)
    halo.finish()
    mix(win2, 1)

    def both(c, carry):
        result = forward(c, win2, 1, CHUNKS)
        out[pl.ds(c * STRIP, STRIP)] = bf16(result.reshape(STRIP, COLS, C))
        backward(c, gwin2, 1, CHUNKS)
        return carry

    lax.fori_loop(0, CHUNKS, both, 0)
    put_out = pltpu.make_async_copy(out, out_hbm, sem_put.at[0])
    put_out.start()
    halo = Halo(halo_bufs, sem_h, 2, gwin2)
    halo.start()
    second = core_sum(1)
    tap_sums(win2, gwin2, 1, 0, 15)
    second = plane_sum(second, 1)
    halo.finish()

    def put_mixed(row, value):
        mixed[row] = f32(bf16(value))

    adjoint(gwin2, 1, put_mixed, 0, 15)

    def backward_one(c, carry):
        seed(c, mixed[pl.ds(c * STRIP, STRIP)].reshape(CELLS, C), 0)
        backward(c, gwin1, 0, c)
        return carry

    lax.fori_loop(0, CHUNKS, backward_one, 0)
    halo = Halo(halo_bufs, sem_h, 3, gwin1)
    halo.start()
    first = core_sum(0)
    pack_rows(1)
    tap_sums(win1, gwin1, 0, 0, 6)
    first = plane_sum(first, 0)
    tap_sums(win1, gwin1, 0, 6, 15)
    pack_rows(0)
    tiny = Exchange("plane", True, small, tiny_a, sem_tiny).start()
    halo.finish()

    def put_state(row, value):
        grad_state[row] = bf16(value)

    adjoint(gwin1, 0, put_state, 0, 8)
    add_slots(second, 1)
    add_slots(first, 0)
    tiny.wait()
    tiny_total = slot_sum(small[plane], tiny_a)
    for j in range(LINE):
        line_send[j, 0:PART] = total[0, j * PART : j * PART + PART]
        line_send[j, PART : 2 * PART] = total[1, j * PART : j * PART + PART]
        line_send[j, 2 * PART : 2 * PART + 1] = tiny_total[j : j + 1]
    line = Exchange("line", True, line_send, line_recv, sem_line.at[0]).start()
    adjoint(gwin1, 0, put_state, 8, 15)
    put_grad = pltpu.make_async_copy(grad_state, state_hbm, sem_put.at[1])
    put_grad.start()
    line.wait()
    own = slot_sum(line_send[z], line_recv, LINE)
    line_own[...] = own
    line = Exchange("line", False, line_own, line_all, sem_line.at[1]).start()
    line.wait()
    line_all[z] = own
    for j in range(LINE):
        piece[j * PART : j * PART + PART] = line_all[j, 0:PART]
        piece[PIECE + j * PART : PIECE + j * PART + PART] = line_all[j, PART : 2 * PART]
        piece[2 * PIECE + j : 2 * PIECE + j + 1] = line_all[j, 2 * PART : 2 * PART + 1]
    both_halves[core, plane] = bf16(piece[...])
    back = Exchange(
        "plane", False, both_halves.at[core, plane], both_halves.at[core], sem_back
    ).start()
    back.wait()
    swap = to_sibling(both_halves.at[core], both_halves.at[core], sem_core.at[BLOCKS])
    swap.start()
    swap.wait()
    put_sums = pltpu.make_async_copy(both_halves, gathered, sem_put.at[2])
    put_sums.start()
    put_out.wait()
    put_grad.wait()
    put_sums.wait()


def write_kernel(
    grad_norm,
    out_from,
    state_from,
    gathered,
    out,
    grad_state,
    g_kernel,
    g_conv,
    g_gain,
    g_shift,
    g_win,
    g_bias_in,
    g_wout,
    g_bias_out,
    g_scale,
    small,
    held,
    sems,
):
    pairs = ((out_from, out), (state_from, grad_state))
    moves = [
        pltpu.make_async_copy(pair[0], held.at[n], sems.at[n]) for n, pair in enumerate(pairs)
    ]
    for move in moves:
        move.start()
    for n, pair in enumerate(pairs):
        moves[n].wait()
        moves[n] = pltpu.make_async_copy(held.at[n], pair[1], sems.at[2 + n])
        moves[n].start()
    for blk in range(BLOCKS):
        rows = slice(blk * PIECE, blk * PIECE + PIECE)
        for p in range(GROUP):
            g_win[
                blk, (p % 4) * PIECE : (p % 4) * PIECE + PIECE, (p // 4) * 128 : (p // 4) * 128 + 128
            ] = f32(gathered[0, p, rows, :]) * grad_norm
            g_wout[blk, p * PIECE : p * PIECE + PIECE] = f32(gathered[1, p, rows, :]) * grad_norm
    tiny = slice(2 * PIECE, 2 * PIECE + 8)
    for p in range(GROUP):
        small[p] = (f32(gathered[0, p, tiny, :]) + f32(gathered[1, p, tiny, :])) * grad_norm
    for blk in range(BLOCKS):

        def row_of(r):
            return small[r // 4, blk * 4 + r % 4 : blk * 4 + r % 4 + 1, :]

        for a in range(KSIZE):
            for b in range(KSIZE):
                g_kernel[a, b, blk : blk + 1, :] = row_of(a * KSIZE + b)
        for k, ref in enumerate((g_conv, g_gain, g_shift, g_bias_out, g_scale)):
            ref[blk : blk + 1, :] = row_of(49 + k)
        for q in range(4):
            g_bias_in[blk : blk + 1, q * 128 : q * 128 + 128] = row_of(54 + q)
    for move in moves:
        move.wait()


def on_device(
    state,
    land_sea,
    cotangent,
    dw_kernel,
    *rest,
):
    vmem = pl.BlockSpec(memory_space=pltpu.VMEM)
    anywhere = pl.BlockSpec(memory_space=pl.ANY)
    grad_norm = 1.0 / math.sqrt(
        lax.axis_size("lat") * ROWS * lax.axis_size("lon") * COLS
    )
    field = jax.ShapeDtypeStruct((ROWS, COLS, C), jnp.bfloat16)
    row = jax.ShapeDtypeStruct((BLOCKS, C), jnp.float32)

    def vm(*shape, dtype=jnp.float32):
        return pltpu.VMEM(shape, dtype)

    def sems(*shape):
        return pltpu.SemaphoreType.DMA(shape)

    tall, wide = ROWS + 2 * MARGIN, COLS + 8
    half = jnp.bfloat16
    packed = 2 * PIECE + 8
    arguments = (state, land_sea.T, cotangent, jnp.transpose(dw_kernel, (1, 2, 0, 3)), *rest)
    fields = pl.pallas_call(
        step_kernel,
        name="ocean_step",
        out_shape=(
            field,
            field,
            jax.ShapeDtypeStruct((2, GROUP, packed, C), jnp.bfloat16),
        ),
        in_specs=[pl.BlockSpec(memory_space=pltpu.HBM)] * 12,
        out_specs=(anywhere,) * 3,
        scratch_shapes=[
            vm(tall, wide, C),
            vm(tall, wide, C),
            vm(tall, wide, C),
            vm(tall, wide, C),
            vm(KSIZE, KSIZE, BLOCKS, C),
            vm(ROWS, COLS, C),
            vm(ROWS, COLS, C),
            vm(CELLS, F),
            vm(CHUNKS + 1, CELLS, F),
            vm(CHUNKS + 1, CELLS, F),
            vm(CHUNKS + 1, CELLS, C),
            vm(CHUNKS + 1, CELLS, C),
            vm(CHUNKS + 1, CELLS, C),
            vm(ROWS, COLS, C),
            vm(BLOCKS, C, F),
            vm(BLOCKS, C, F),
            vm(BLOCKS, 5, 8, C),
            vm(BLOCKS, 8, F),
            vm(BLOCKS, KSIZE * KSIZE, 8, C),
            vm(4, ROWS, MARGIN, C, dtype=half),
            vm(4, ROWS, MARGIN, C, dtype=half),
            vm(4, MARGIN, COLS, C, dtype=half),
            vm(4, MARGIN, COLS, C, dtype=half),
            vm(4, tall, MARGIN, C, dtype=half),
            vm(4, tall, MARGIN, C, dtype=half),
            vm(4, MARGIN, COLS, C, dtype=half),
            vm(4, MARGIN, COLS, C, dtype=half),
            sems(4, 2, len(AROUND)),
            vm(GROUP, 8, C),
            vm(BLOCKS, 2, F, C, dtype=half),
            vm(BLOCKS, F, C, dtype=half),
            vm(BLOCKS, GROUP, PIECE, C, dtype=half),
            vm(BLOCKS, GROUP, PIECE, C, dtype=half),
            vm(GROUP, 8, C),
            vm(LINE, 2 * PART + 1, C),
            vm(LINE, 2 * PART + 1, C),
            vm(2 * PART + 1, C),
            vm(LINE, 2 * PART + 1, C),
            vm(packed, C),
            vm(BLOCKS, PIECE, C),
            vm(2, GROUP, packed, C, dtype=half),
            vm(CHUNKS, CELLS, C, dtype=half),
            vm(CHUNKS, CELLS, F),
            sems(BLOCKS + 1, 2),
            sems(BLOCKS, 2, GROUP),
            sems(2, GROUP),
            sems(2, 2, LINE),
            sems(2, GROUP),
            sems(len(arguments)),
            vm(ROWS, COLS, C, dtype=half),
            vm(ROWS, COLS, C, dtype=half),
            sems(3),
            *(pltpu.VMEM(array.shape, array.dtype) for array in arguments),
        ],
        compiler_params=pltpu.CompilerParams(
            collective_id=0, has_side_effects=True, vmem_limit_bytes=58 << 20
        ),
    )(*arguments)
    results = pl.pallas_call(
        lambda *refs: write_kernel(grad_norm, *refs),
        name="write_results",
        out_shape=(
            field,
            field,
            jax.ShapeDtypeStruct((KSIZE, KSIZE, BLOCKS, C), jnp.float32),
            row,
            row,
            row,
            jax.ShapeDtypeStruct((BLOCKS, C, F), jnp.float32),
            jax.ShapeDtypeStruct((BLOCKS, F), jnp.float32),
            jax.ShapeDtypeStruct((BLOCKS, F, C), jnp.float32),
            row,
            row,
        ),
        in_specs=[anywhere, anywhere, vmem],
        out_specs=(anywhere, anywhere) + (vmem,) * 9,
        scratch_shapes=[
            vm(GROUP, 8, C),
            vm(2, ROWS, COLS, C, dtype=half),
            sems(4),
        ],
        compiler_params=pltpu.CompilerParams(vmem_limit_bytes=58 << 20),
    )(*fields)
    return results[:2] + (jnp.transpose(results[2], (2, 0, 1, 3)),) + results[3:]


def solution(mesh):
    field = P("lat", "lon", None)
    return jax.shard_map(
        on_device,
        mesh=mesh,
        in_specs=(field, P("lat", "lon"), field) + (P(),) * 9,
        out_specs=(field, field) + (P(),) * 9,
        check_vma=False,
    )
```

```python
import math

import jax
import jax.numpy as jnp
from jax import lax
from jax.experimental import pallas as pl
from jax.experimental.pallas import tpu as pltpu
from jax.sharding import PartitionSpec as P

KSIZE = 7
BLOCKS = 2
C = 128
F = 512
EPS_NORM = 1e-06
INV_ROOT_TWO = 0.7071067811865476
INV_ROOT_TWO_PI = 0.3989422804014327
MESH_ID = pl.DeviceIdType.MESH
GROUP = 16
LINE = 8
PIECE = 32
ROWS = 45
COLS = 24
MARGIN = 3
AROUND = ((1, 0), (-1, 0), (0, 1), (0, -1), (1, 1), (1, -1), (-1, 1), (-1, -1))
STRIP = 9
CHUNKS = ROWS // STRIP
CELLS = STRIP * COLS


def position():
    lon = lax.axis_index("lon")
    plane = lax.rem(lon // 2, 2) * 8 + lax.axis_index("lat")
    return plane, lon // 4, lax.rem(lon, 2)


def device(plane, z, core):
    return {"lon": z * 4 + (plane // 8) * 2 + core, "lat": lax.rem(plane, 8)}


def beside(east, south):
    return {
        "lon": lax.rem(lax.axis_index("lon") + east + 32, 32),
        "lat": lax.rem(lax.axis_index("lat") + south + 8, 8),
    }


def announce(barrier):
    plane, z, core = position()

    def signal(target):
        pl.semaphore_signal(barrier, inc=1, device_id=target, device_id_type=MESH_ID)

    for east, south in AROUND:
        signal(beside(east, south))
    signal(device(plane, z, 1 - core))

    def in_plane(k, carry):
        signal(device(lax.rem(plane + k, GROUP), z, core))
        return carry

    def in_line(k, carry):
        signal(device(plane, lax.rem(z + k, LINE), core))
        return carry

    lax.fori_loop(1, GROUP, in_plane, 0)
    lax.fori_loop(1, LINE, in_line, 0)


class Exchange:
    def __init__(self, kind, scatter, src, dst, sems):
        self.plane, self.z, self.core = position()
        self.kind, self.scatter = kind, scatter
        self.src, self.dst, self.sems = src, dst, sems
        self.me, self.size = (self.plane, GROUP) if kind == "plane" else (self.z, LINE)

    def copy(self, k, arriving):
        other = lax.rem(self.me + k, self.size)
        if self.kind == "plane":
            target = device(other, self.z, self.core)
        else:
            target = device(self.plane, other, self.core)
        if self.scatter:
            src, slot = self.src.at[other], k
        else:
            src = self.src
            slot = lax.rem(self.me - k + self.size, self.size) if arriving else self.me
        return pltpu.make_async_remote_copy(
            src_ref=src,
            dst_ref=self.dst.at[slot],
            send_sem=self.sems.at[0, k],
            recv_sem=self.sems.at[1, k],
            device_id=target,
            device_id_type=MESH_ID,
        )

    def start(self):
        def one(k, carry):
            self.copy(k, False).start()
            return carry

        lax.fori_loop(1, self.size, one, 0)
        return self

    def wait(self):
        def one(k, carry):
            self.copy(k, True).wait()
            return carry

        lax.fori_loop(1, self.size, one, 0)


def to_sibling(src, dst, sems):
    plane, z, core = position()
    return pltpu.make_async_remote_copy(
        src_ref=src,
        dst_ref=dst,
        send_sem=sems.at[0],
        recv_sem=sems.at[1],
        device_id=device(plane, z, 1 - core),
        device_id_type=MESH_ID,
    )


def slot_sum(own, slots, count=GROUP):
    def one(k, total):
        return total + slots[k].astype(jnp.float32)

    return lax.fori_loop(1, count, one, own)


def f32(value):
    return value.astype(jnp.float32)


def bf16(value):
    return value.astype(jnp.bfloat16)


class Halo:
    def __init__(self, bufs, sems, index, window):
        east, west, north, south, from_west, from_east, from_north, from_south = (
            ref.at[index] for ref in bufs
        )
        self.bufs = (east, west, north, south, from_west, from_east, from_north, from_south)
        self.window = window
        last = ROWS - MARGIN
        tall = pl.ds(MARGIN, ROWS)
        above, below = pl.ds(0, MARGIN), pl.ds(MARGIN + ROWS, MARGIN)
        top, bottom = pl.ds(0, MARGIN), pl.ds(last, MARGIN)
        pairs = (
            (east, from_west.at[tall]),
            (west, from_east.at[tall]),
            (south, from_north),
            (north, from_south),
            (east.at[bottom], from_west.at[above]),
            (east.at[top], from_west.at[below]),
            (west.at[bottom], from_east.at[above]),
            (west.at[top], from_east.at[below]),
        )
        self.copies = [
            pltpu.make_async_remote_copy(
                src_ref=pair[0],
                dst_ref=pair[1],
                send_sem=sems.at[index, 0, k],
                recv_sem=sems.at[index, 1, k],
                device_id=beside(*AROUND[k]),
                device_id_type=MESH_ID,
            )
            for k, pair in enumerate(pairs)
        ]

    def start(self):
        self.stage()
        self.launch()

    def stage_from(self, tile):
        east, west, north, south = self.bufs[:4]
        east[...] = tile[:, COLS - MARGIN : COLS, :]
        west[...] = tile[:, 0:MARGIN, :]
        north[...] = tile[0:MARGIN]
        south[...] = tile[ROWS - MARGIN : ROWS]

    def stage(self):
        east, west, north, south = self.bufs[:4]
        window = self.window
        inner = slice(MARGIN, MARGIN + ROWS)
        east[...] = bf16(window[inner, COLS : COLS + MARGIN, :])
        west[...] = bf16(window[inner, MARGIN : 2 * MARGIN, :])
        north[...] = bf16(window[MARGIN : 2 * MARGIN, MARGIN : MARGIN + COLS, :])
        south[...] = bf16(window[ROWS : ROWS + MARGIN, MARGIN : MARGIN + COLS, :])

    def launch(self):
        for copy in self.copies:
            copy.start()

    def finish(self):
        for copy in self.copies:
            copy.wait()
        from_west, from_east, from_north, from_south = self.bufs[4:]
        lat = lax.axis_index("lat")
        has_north = jnp.where(lat > 0, 1.0, 0.0).astype(jnp.float32)
        has_south = jnp.where(lat < 7, 1.0, 0.0).astype(jnp.float32)
        window = self.window
        inner = slice(MARGIN, MARGIN + ROWS)
        above, below = slice(0, MARGIN), slice(MARGIN + ROWS, 2 * MARGIN + ROWS)
        middle = slice(MARGIN, MARGIN + COLS)
        window[above, middle, :] = f32(from_north[...]) * has_north
        window[below, middle, :] = f32(from_south[...]) * has_south
        for ref, side in (
            (from_west, slice(0, MARGIN)),
            (from_east, slice(MARGIN + COLS, 2 * MARGIN + COLS)),
        ):
            window[inner, side, :] = f32(ref[inner])
            window[above, side, :] = f32(ref[above]) * has_north
            window[below, side, :] = f32(ref[below]) * has_south


def convolve(window, weight, first, flip):
    def rows(base):
        sums = first(base)
        for i in range(KSIZE + 2):
            for b in range(KSIZE):
                piece = window[base + i, b : b + COLS, :]
                for o in range(3):
                    a = i - o
                    if 0 <= a < KSIZE:
                        tap = weight(KSIZE - 1 - a, KSIZE - 1 - b) if flip else weight(a, b)
                        sums[o] = sums[o] + piece * tap
        return sums

    return rows


def fold(value):
    return jnp.sum(value.reshape(value.shape[0] // 8, 8, value.shape[1]), axis=0)


def lane_mean(value):
    return jnp.mean(value, axis=-1, keepdims=True)


def step_kernel(
    *refs,
):
    arguments, refs = refs[:12], refs[12:]
    (
    out_hbm,
    state_hbm,
    sums_one,
    sums_two,
    win1,
    win2,
    gwin1,
    gwin2,
    taps,
    mask,
    mixed,
    hidden,
    active,
    slope,
    normed,
    inverse,
    branch,
    upstream,
    acc_win,
    acc_wout,
    acc_rows,
    acc_bias,
    acc_taps,
    h_east,
    h_west,
    h_north,
    h_south,
    h_from_west,
    h_from_east,
    h_from_north,
    h_from_south,
    sem_h,
    small,
    halves,
    from_core,
    send_a,
    recv_a,
    tiny_a,
    line_own,
    line_all,
    gather_one,
    gather_two,
    seeds,
    pulled,
    sem_core,
    sem_a,
    sem_tiny,
    sem_line,
    sem_back,
    sem_load,
    out,
    grad_state,
    sem_put,
    *arrived,
    ) = refs
    loads = [
        pltpu.make_async_copy(source, target, sem_load.at[n])
        for n, (source, target) in enumerate(zip(arguments, arrived))
    ]
    for load in loads:
        load.start()
    (
        state,
        land_sea,
        cotangent,
        dw_kernel,
        conv_bias,
        norm_gain,
        norm_bias,
        weight_in,
        bias_in,
        weight_out,
        bias_out,
        layer_scale,
    ) = arrived
    plane, z, core = position()
    barrier = pltpu.get_barrier_semaphore()
    announce(barrier)
    loads[0].wait()
    halo_bufs = (
        h_east, h_west, h_north, h_south, h_from_west, h_from_east, h_from_north, h_from_south
    )
    middle = slice(MARGIN, MARGIN + COLS)

    halo = Halo(halo_bufs, sem_h, 0, win1)
    halo.stage_from(state)
    pl.semaphore_wait(barrier, GROUP + LINE - 1 + len(AROUND))
    halo.launch()

    def widen(c, carry):
        win1[pl.ds(MARGIN + c * STRIP, STRIP), middle, :] = f32(state[pl.ds(c * STRIP, STRIP)])
        return carry

    lax.fori_loop(0, CHUNKS, widen, 0)
    for load in loads[1:]:
        load.wait()

    taps[...] = f32(dw_kernel[...])
    ocean_t = land_sea[...].astype(jnp.float32)
    for i in range(ROWS):
        mask[i] = jnp.broadcast_to(ocean_t[:, i : i + 1], (COLS, C))
    acc_win[...] = jnp.zeros_like(acc_win)
    acc_wout[...] = jnp.zeros_like(acc_wout)
    acc_rows[...] = jnp.zeros_like(acc_rows)
    acc_bias[...] = jnp.zeros_like(acc_bias)
    acc_taps[...] = jnp.zeros_like(acc_taps)
    small[...] = jnp.zeros_like(small)

    def mix(window, blk):
        start = jnp.broadcast_to(conv_bias[blk : blk + 1, :], (COLS, C))
        rows = convolve(
            window, lambda a, b: taps[a, b, blk : blk + 1, :], lambda base: [start] * 3, False
        )

        def three(g, carry):
            sums = rows(g * 3)
            for o in range(3):
                mixed[g * 3 + o] = sums[o]
            return carry

        lax.fori_loop(0, ROWS // 3, three, 0)

    def forward(c, window, blk, keep):
        x = mixed[pl.ds(c * STRIP, STRIP)].reshape(CELLS, C)
        center = x - lane_mean(x)
        inv = lax.rsqrt(lane_mean(center * center) + EPS_NORM)
        norm = center * inv
        normed[keep] = norm
        inverse[keep] = jnp.broadcast_to(inv, (CELLS, C))
        lifted = bf16(norm * norm_gain[blk : blk + 1, :] + norm_bias[blk : blk + 1, :])
        hidden[...] = jnp.dot(lifted, weight_in[blk], preferred_element_type=jnp.float32)

        def gelu(t, carry):
            rows = pl.ds(pl.multiple_of(t * COLS, 8), COLS)
            h = hidden[rows, :] + bias_in[blk : blk + 1, :]
            cumulative = 0.5 * (1.0 + lax.erf(h * INV_ROOT_TWO))
            density = jnp.exp(-0.5 * h * h) * INV_ROOT_TWO_PI
            active[keep, rows, :] = bf16(h * cumulative)
            slope[keep, rows, :] = cumulative + h * density
            return carry

        lax.fori_loop(0, STRIP, gelu, 0)
        act = active[keep]
        branch_c = (
            jnp.dot(act, weight_out[blk], preferred_element_type=jnp.float32)
            + bias_out[blk : blk + 1, :]
        )
        branch[keep] = branch_c
        inner = window[pl.ds(MARGIN + c * STRIP, STRIP), middle, :].reshape(CELLS, C)
        ocean = mask[pl.ds(c * STRIP, STRIP)].reshape(CELLS, C)
        return (inner + layer_scale[blk : blk + 1, :] * branch_c) * ocean

    def seed(c, incoming, blk):
        ocean = mask[pl.ds(c * STRIP, STRIP)].reshape(CELLS, C)
        masked = incoming * ocean
        upstream[pl.ds(c * STRIP, STRIP)] = masked.reshape(STRIP, COLS, C)
        gb = bf16(masked * layer_scale[blk : blk + 1, :])
        acc_rows[blk, 3] += fold(f32(gb))
        seeds[c] = gb
        pulled[c] = lax.dot_general(
            gb, weight_out[blk], (((1,), (1,)), ((), ())), preferred_element_type=jnp.float32
        )

    def backward(c, gwindow, blk, keep):
        masked = upstream[pl.ds(c * STRIP, STRIP)].reshape(CELLS, C)
        acc_rows[blk, 4] += fold(masked * branch[keep])
        rows_rows = (((0,), (0,)), ((), ()))
        cols_cols = (((1,), (1,)), ((), ()))
        acc_wout[blk] += lax.dot_general(
            seeds[c], active[keep], rows_rows, preferred_element_type=jnp.float32
        )

        gh = bf16(pulled[c] * slope[keep])
        acc_bias[blk] += jnp.dot(
            jnp.ones((8, CELLS), jnp.bfloat16), gh, preferred_element_type=jnp.float32
        )
        norm = normed[keep]
        gain = norm_gain[blk : blk + 1, :]
        lifted = bf16(norm * gain + norm_bias[blk : blk + 1, :])
        acc_win[blk] += lax.dot_general(
            lifted, gh, rows_rows, preferred_element_type=jnp.float32
        )
        gl = lax.dot_general(gh, weight_in[blk], cols_cols, preferred_element_type=jnp.float32)
        acc_rows[blk, 1] += fold(gl * norm)
        acc_rows[blk, 2] += fold(gl)
        s = gl * gain
        gm = inverse[keep] * (s - lane_mean(s) - norm * lane_mean(s * norm))
        gm = f32(bf16(gm))
        acc_rows[blk, 0] += fold(gm)
        gwindow[pl.ds(MARGIN + c * STRIP, STRIP), middle, :] = gm.reshape(STRIP, COLS, C)

    def tap_sums(window, gwindow, blk, begin, end):
        def three(g, carry):
            base = g * 3
            grads = [gwindow[base + MARGIN + o, middle, :] for o in range(3)]
            for b in range(KSIZE):
                parts = [None] * KSIZE
                for i in range(KSIZE + 2):
                    piece = window[base + i, b : b + COLS, :]
                    for o in range(3):
                        a = i - o
                        if 0 <= a < KSIZE:
                            term = piece * grads[o]
                            parts[a] = term if parts[a] is None else parts[a] + term
                for a in range(KSIZE):
                    acc_taps[blk, a * KSIZE + b] += fold(parts[a])
            return carry

        lax.fori_loop(begin, end, three, 0)

    def adjoint(gwindow, blk, put, begin, end):
        rows = convolve(
            gwindow,
            lambda a, b: taps[a, b, blk : blk + 1, :],
            lambda base: [upstream[base + o] for o in range(3)],
            True,
        )

        def three(g, carry):
            sums = rows(g * 3)
            for o in range(3):
                put(g * 3 + o, sums[o])
            return carry

        lax.fori_loop(begin, end, three, 0)

    def core_sum(blk):
        for q in range(4):
            block = slice(q * 128, q * 128 + 128)
            halves[blk, 0, block, :] = bf16(acc_win[blk, :, block])
            halves[blk, 1, block, :] = bf16(jnp.transpose(acc_wout[blk, :, block]))
        copy = to_sibling(halves.at[blk, 1 - core], from_core.at[blk], sem_core.at[blk])
        copy.start()
        return copy

    def plane_sum(copy, blk):
        copy.wait()
        both = f32(halves[blk, core]) + f32(from_core[blk])
        send_a[blk] = bf16(both).reshape(GROUP, PIECE, C)
        return Exchange("plane", True, send_a.at[blk], recv_a.at[blk], sem_a.at[blk]).start()

    def line_sum(ex, blk, tiny):
        ex.wait()
        total = bf16(slot_sum(f32(send_a[blk, plane]), recv_a.at[blk]))
        rows = line_all.at[blk] if tiny is not None else line_all.at[blk, :, 0:PIECE]
        line_all[blk, z, 0:PIECE] = total
        line_own[blk, 0:PIECE] = total
        own = line_own.at[blk, 0:PIECE]
        if tiny is not None:
            tiny.wait()
            tiny_total = bf16(slot_sum(small[plane], tiny_a))
            line_all[blk, z, PIECE : PIECE + 8] = tiny_total
            line_own[blk, PIECE : PIECE + 8] = tiny_total
            own = line_own.at[blk]
        return Exchange("line", False, own, rows, sem_line.at[blk]).start()

    def plane_back(ex, blk, gather):
        ex.wait()
        rows = gather.shape[2]
        own = f32(line_all[blk, 0, 0:rows])
        for j in range(1, LINE):
            own = own + f32(line_all[blk, j, 0:rows])
        gather[core, plane] = bf16(own)
        return Exchange(
            "plane", False, gather.at[core, plane], gather.at[core], sem_back.at[blk]
        ).start()

    def swap_halves(ex, blk, gather):
        ex.wait()
        copy = to_sibling(gather.at[core], gather.at[core], sem_core.at[BLOCKS + blk])
        copy.start()
        return copy

    def small_row(blk, r, value):
        i = blk * 4 + r % 4
        small[r // 4, i : i + 1, :] = jnp.sum(value, axis=0, keepdims=True)

    def pack_rows(blk):
        for tap in range(KSIZE * KSIZE):
            small_row(blk, tap, acc_taps[blk, tap])
        for k in range(5):
            small_row(blk, 49 + k, acc_rows[blk, k])
        for q in range(4):
            small_row(blk, 54 + q, acc_bias[blk, 0:1, q * 128 : q * 128 + 128])

    halo.finish()
    mix(win1, 0)

    def forward_one(c, carry):
        result = forward(c, win1, 0, c)
        win2[pl.ds(MARGIN + c * STRIP, STRIP), middle, :] = f32(bf16(result)).reshape(
            STRIP, COLS, C
        )
        return carry

    lax.fori_loop(0, CHUNKS, forward_one, 0)
    halo = Halo(halo_bufs, sem_h, 1, win2)
    halo.start()

    def seed_two(c, carry):
        seed(c, f32(cotangent[pl.ds(c * STRIP, STRIP)]).reshape(CELLS, C), 1)
        return carry

    lax.fori_loop(0, CHUNKS, seed_two, 0)
    halo.finish()
    mix(win2, 1)

    def both(c, carry):
        result = forward(c, win2, 1, CHUNKS)
        out[pl.ds(c * STRIP, STRIP)] = bf16(result.reshape(STRIP, COLS, C))
        backward(c, gwin2, 1, CHUNKS)
        return carry

    lax.fori_loop(0, CHUNKS, both, 0)
    put_out = pltpu.make_async_copy(out, out_hbm, sem_put.at[0])
    put_out.start()
    halo = Halo(halo_bufs, sem_h, 2, gwin2)
    halo.start()
    second = core_sum(1)
    tap_sums(win2, gwin2, 1, 0, 15)
    second = plane_sum(second, 1)
    pack_rows(1)
    halo.finish()

    def put_mixed(row, value):
        mixed[row] = f32(bf16(value))

    adjoint(gwin2, 1, put_mixed, 0, 15)
    second = line_sum(second, 1, None)

    def backward_one(c, carry):
        seed(c, mixed[pl.ds(c * STRIP, STRIP)].reshape(CELLS, C), 0)
        backward(c, gwin1, 0, c)
        return carry

    lax.fori_loop(0, CHUNKS, backward_one, 0)
    halo = Halo(halo_bufs, sem_h, 3, gwin1)
    halo.start()
    first = core_sum(0)
    second = plane_back(second, 1, gather_two)
    tap_sums(win1, gwin1, 0, 0, 6)
    first = plane_sum(first, 0)
    tap_sums(win1, gwin1, 0, 6, 15)
    pack_rows(0)
    tiny = Exchange("plane", True, small, tiny_a, sem_tiny).start()
    second = swap_halves(second, 1, gather_two)
    halo.finish()

    def put_state(row, value):
        grad_state[row] = bf16(value)

    adjoint(gwin1, 0, put_state, 0, 8)
    first = line_sum(first, 0, tiny)
    adjoint(gwin1, 0, put_state, 8, 15)
    put_grad = pltpu.make_async_copy(grad_state, state_hbm, sem_put.at[1])
    put_grad.start()
    second.wait()
    put_two = pltpu.make_async_copy(gather_two, sums_two, sem_put.at[2])
    put_two.start()
    first = plane_back(first, 0, gather_one)
    first = swap_halves(first, 0, gather_one)
    first.wait()
    put_one = pltpu.make_async_copy(gather_one, sums_one, sem_put.at[3])
    put_one.start()
    for put in (put_out, put_grad, put_two, put_one):
        put.wait()


def write_kernel(
    grad_norm,
    out_from,
    state_from,
    sums_one,
    sums_two,
    out,
    grad_state,
    g_kernel,
    g_conv,
    g_gain,
    g_shift,
    g_win,
    g_bias_in,
    g_wout,
    g_bias_out,
    g_scale,
    small,
    held,
    sems,
):
    pairs = ((out_from, out), (state_from, grad_state))
    moves = [
        pltpu.make_async_copy(pair[0], held.at[n], sems.at[n]) for n, pair in enumerate(pairs)
    ]
    for move in moves:
        move.start()
    for n, pair in enumerate(pairs):
        moves[n].wait()
        moves[n] = pltpu.make_async_copy(held.at[n], pair[1], sems.at[2 + n])
        moves[n].start()
    for blk in range(BLOCKS):
        sums = (sums_one, sums_two)[blk]
        rows = slice(0, PIECE)
        for p in range(GROUP):
            g_win[
                blk, (p % 4) * PIECE : (p % 4) * PIECE + PIECE, (p // 4) * 128 : (p // 4) * 128 + 128
            ] = f32(sums[0, p, rows, :]) * grad_norm
            g_wout[blk, p * PIECE : p * PIECE + PIECE] = f32(sums[1, p, rows, :]) * grad_norm
    tiny = slice(PIECE, PIECE + 8)
    for p in range(GROUP):
        small[p] = (f32(sums_one[0, p, tiny, :]) + f32(sums_one[1, p, tiny, :])) * grad_norm
    for blk in range(BLOCKS):

        def row_of(r):
            return small[r // 4, blk * 4 + r % 4 : blk * 4 + r % 4 + 1, :]

        for a in range(KSIZE):
            for b in range(KSIZE):
                g_kernel[a, b, blk : blk + 1, :] = row_of(a * KSIZE + b)
        for k, ref in enumerate((g_conv, g_gain, g_shift, g_bias_out, g_scale)):
            ref[blk : blk + 1, :] = row_of(49 + k)
        for q in range(4):
            g_bias_in[blk : blk + 1, q * 128 : q * 128 + 128] = row_of(54 + q)
    for move in moves:
        move.wait()


def on_device(
    state,
    land_sea,
    cotangent,
    dw_kernel,
    *rest,
):
    vmem = pl.BlockSpec(memory_space=pltpu.VMEM)
    anywhere = pl.BlockSpec(memory_space=pl.ANY)
    grad_norm = 1.0 / math.sqrt(
        lax.axis_size("lat") * ROWS * lax.axis_size("lon") * COLS
    )
    field = jax.ShapeDtypeStruct((ROWS, COLS, C), jnp.bfloat16)
    row = jax.ShapeDtypeStruct((BLOCKS, C), jnp.float32)

    def vm(*shape, dtype=jnp.float32):
        return pltpu.VMEM(shape, dtype)

    def sems(*shape):
        return pltpu.SemaphoreType.DMA(shape)

    tall, wide = ROWS + 2 * MARGIN, COLS + 8
    half = jnp.bfloat16
    packed = PIECE + 8
    arguments = (state, land_sea.T, cotangent, jnp.transpose(dw_kernel, (1, 2, 0, 3)), *rest)
    fields = pl.pallas_call(
        step_kernel,
        name="ocean_step",
        out_shape=(
            field,
            field,
            jax.ShapeDtypeStruct((2, GROUP, packed, C), jnp.bfloat16),
            jax.ShapeDtypeStruct((2, GROUP, PIECE, C), jnp.bfloat16),
        ),
        in_specs=[pl.BlockSpec(memory_space=pltpu.HBM)] * 12,
        out_specs=(anywhere,) * 4,
        scratch_shapes=[
            vm(tall, wide, C),
            vm(tall, wide, C),
            vm(tall, wide, C),
            vm(tall, wide, C),
            vm(KSIZE, KSIZE, BLOCKS, C),
            vm(ROWS, COLS, C),
            vm(ROWS, COLS, C),
            vm(CELLS, F),
            vm(CHUNKS + 1, CELLS, F, dtype=half),
            vm(CHUNKS + 1, CELLS, F),
            vm(CHUNKS + 1, CELLS, C),
            vm(CHUNKS + 1, CELLS, C),
            vm(CHUNKS + 1, CELLS, C),
            vm(ROWS, COLS, C),
            vm(BLOCKS, C, F),
            vm(BLOCKS, C, F),
            vm(BLOCKS, 5, 8, C),
            vm(BLOCKS, 8, F),
            vm(BLOCKS, KSIZE * KSIZE, 8, C),
            vm(4, ROWS, MARGIN, C, dtype=half),
            vm(4, ROWS, MARGIN, C, dtype=half),
            vm(4, MARGIN, COLS, C, dtype=half),
            vm(4, MARGIN, COLS, C, dtype=half),
            vm(4, tall, MARGIN, C, dtype=half),
            vm(4, tall, MARGIN, C, dtype=half),
            vm(4, MARGIN, COLS, C, dtype=half),
            vm(4, MARGIN, COLS, C, dtype=half),
            sems(4, 2, len(AROUND)),
            vm(GROUP, 8, C),
            vm(BLOCKS, 2, F, C, dtype=half),
            vm(BLOCKS, F, C, dtype=half),
            vm(BLOCKS, GROUP, PIECE, C, dtype=half),
            vm(BLOCKS, GROUP, PIECE, C, dtype=half),
            vm(GROUP, 8, C),
            vm(BLOCKS, packed, C, dtype=half),
            vm(BLOCKS, LINE, packed, C, dtype=half),
            vm(2, GROUP, packed, C, dtype=half),
            vm(2, GROUP, PIECE, C, dtype=half),
            vm(CHUNKS, CELLS, C, dtype=half),
            vm(CHUNKS, CELLS, F),
            sems(2 * BLOCKS, 2),
            sems(BLOCKS, 2, GROUP),
            sems(2, GROUP),
            sems(BLOCKS, 2, LINE),
            sems(BLOCKS, 2, GROUP),
            sems(len(arguments)),
            vm(ROWS, COLS, C, dtype=half),
            vm(ROWS, COLS, C, dtype=half),
            sems(4),
            *(pltpu.VMEM(array.shape, array.dtype) for array in arguments),
        ],
        compiler_params=pltpu.CompilerParams(
            collective_id=0, has_side_effects=True, vmem_limit_bytes=58 << 20
        ),
    )(*arguments)
    results = pl.pallas_call(
        lambda *refs: write_kernel(grad_norm, *refs),
        name="write_results",
        out_shape=(
            field,
            field,
            jax.ShapeDtypeStruct((KSIZE, KSIZE, BLOCKS, C), jnp.float32),
            row,
            row,
            row,
            jax.ShapeDtypeStruct((BLOCKS, C, F), jnp.float32),
            jax.ShapeDtypeStruct((BLOCKS, F), jnp.float32),
            jax.ShapeDtypeStruct((BLOCKS, F, C), jnp.float32),
            row,
            row,
        ),
        in_specs=[anywhere, anywhere, vmem, vmem],
        out_specs=(anywhere, anywhere) + (vmem,) * 9,
        scratch_shapes=[
            vm(GROUP, 8, C),
            vm(2, ROWS, COLS, C, dtype=half),
            sems(4),
        ],
        compiler_params=pltpu.CompilerParams(vmem_limit_bytes=58 << 20),
    )(*fields)
    return results[:2] + (jnp.transpose(results[2], (2, 0, 1, 3)),) + results[3:]


def solution(mesh):
    field = P("lat", "lon", None)
    return jax.shard_map(
        on_device,
        mesh=mesh,
        in_specs=(field, P("lat", "lon"), field) + (P(),) * 9,
        out_specs=(field, field) + (P(),) * 9,
        check_vma=False,
    )
```

```python
import math

import jax
import jax.numpy as jnp
from jax import lax
from jax.experimental import pallas as pl
from jax.experimental.pallas import tpu as pltpu
from jax.sharding import PartitionSpec as P

KSIZE = 7
BLOCKS = 2
C = 128
F = 512
EPS_NORM = 1e-06
INV_ROOT_TWO = 0.7071067811865476
INV_ROOT_TWO_PI = 0.3989422804014327
MESH_ID = pl.DeviceIdType.MESH
GROUP = 16
LINE = 8
PIECE = 32
ROWS = 45
COLS = 24
MARGIN = 3
AROUND = ((1, 0), (-1, 0), (0, 1), (0, -1), (1, 1), (1, -1), (-1, 1), (-1, -1))
STRIP = 9
CHUNKS = ROWS // STRIP
CELLS = STRIP * COLS


def position():
    lon = lax.axis_index("lon")
    plane = lax.rem(lon // 2, 2) * 8 + lax.axis_index("lat")
    return plane, lon // 4, lax.rem(lon, 2)


def device(plane, z, core):
    return {"lon": z * 4 + (plane // 8) * 2 + core, "lat": lax.rem(plane, 8)}


def beside(east, south):
    return {
        "lon": lax.rem(lax.axis_index("lon") + east + 32, 32),
        "lat": lax.rem(lax.axis_index("lat") + south + 8, 8),
    }


def announce(barrier):
    plane, z, core = position()

    def signal(target):
        pl.semaphore_signal(barrier, inc=1, device_id=target, device_id_type=MESH_ID)

    for east, south in AROUND:
        signal(beside(east, south))
    signal(device(plane, z, 1 - core))

    def in_plane(k, carry):
        signal(device(lax.rem(plane + k, GROUP), z, core))
        return carry

    def in_line(k, carry):
        signal(device(plane, lax.rem(z + k, LINE), core))
        return carry

    lax.fori_loop(1, GROUP, in_plane, 0)
    lax.fori_loop(1, LINE, in_line, 0)


class Exchange:
    def __init__(self, kind, scatter, src, dst, sems):
        self.plane, self.z, self.core = position()
        self.kind, self.scatter = kind, scatter
        self.src, self.dst, self.sems = src, dst, sems
        self.me, self.size = (self.plane, GROUP) if kind == "plane" else (self.z, LINE)

    def start(self):
        for k in range(1, self.size):
            other = lax.rem(self.me + k, self.size)
            if self.kind == "plane":
                target = device(other, self.z, self.core)
            else:
                target = device(self.plane, other, self.core)
            pltpu.make_async_remote_copy(
                src_ref=self.src.at[other] if self.scatter else self.src,
                dst_ref=self.dst.at[k if self.scatter else self.me],
                send_sem=self.sems.at[0],
                recv_sem=self.sems.at[1],
                device_id=target,
                device_id_type=MESH_ID,
            ).start()
        return self

    def wait(self):
        others = pl.ds(1, self.size - 1)
        for side in range(2):
            pltpu.make_async_copy(
                self.dst.at[others], self.dst.at[others], self.sems.at[side]
            ).wait()


def to_sibling(src, dst, sems):
    plane, z, core = position()
    return pltpu.make_async_remote_copy(
        src_ref=src,
        dst_ref=dst,
        send_sem=sems.at[0],
        recv_sem=sems.at[1],
        device_id=device(plane, z, 1 - core),
        device_id_type=MESH_ID,
    )


def slot_sum(own, slots, count=GROUP):
    def one(k, total):
        return total + slots[k].astype(jnp.float32)

    return lax.fori_loop(1, count, one, own)


def f32(value):
    return value.astype(jnp.float32)


def bf16(value):
    return value.astype(jnp.bfloat16)


class Halo:
    def __init__(self, bufs, sems, index, window):
        east, west, north, south, from_west, from_east, from_north, from_south = (
            ref.at[index] for ref in bufs
        )
        self.bufs = (east, west, north, south, from_west, from_east, from_north, from_south)
        self.window = window
        last = ROWS - MARGIN
        tall = pl.ds(MARGIN, ROWS)
        above, below = pl.ds(0, MARGIN), pl.ds(MARGIN + ROWS, MARGIN)
        top, bottom = pl.ds(0, MARGIN), pl.ds(last, MARGIN)
        pairs = (
            (east, from_west.at[tall]),
            (west, from_east.at[tall]),
            (south, from_north),
            (north, from_south),
            (east.at[bottom], from_west.at[above]),
            (east.at[top], from_west.at[below]),
            (west.at[bottom], from_east.at[above]),
            (west.at[top], from_east.at[below]),
        )
        self.copies = [
            pltpu.make_async_remote_copy(
                src_ref=pair[0],
                dst_ref=pair[1],
                send_sem=sems.at[index, 0, k],
                recv_sem=sems.at[index, 1, k],
                device_id=beside(*AROUND[k]),
                device_id_type=MESH_ID,
            )
            for k, pair in enumerate(pairs)
        ]

    def start(self):
        self.stage()
        self.launch()

    def stage_from(self, tile):
        east, west, north, south = self.bufs[:4]
        east[...] = tile[:, COLS - MARGIN : COLS, :]
        west[...] = tile[:, 0:MARGIN, :]
        north[...] = tile[0:MARGIN]
        south[...] = tile[ROWS - MARGIN : ROWS]

    def stage(self):
        east, west, north, south = self.bufs[:4]
        window = self.window
        inner = slice(MARGIN, MARGIN + ROWS)
        east[...] = bf16(window[inner, COLS : COLS + MARGIN, :])
        west[...] = bf16(window[inner, MARGIN : 2 * MARGIN, :])
        north[...] = bf16(window[MARGIN : 2 * MARGIN, MARGIN : MARGIN + COLS, :])
        south[...] = bf16(window[ROWS : ROWS + MARGIN, MARGIN : MARGIN + COLS, :])

    def launch(self):
        for copy in self.copies:
            copy.start()

    def finish(self):
        for copy in self.copies:
            copy.wait()
        from_west, from_east, from_north, from_south = self.bufs[4:]
        lat = lax.axis_index("lat")
        has_north = jnp.where(lat > 0, 1.0, 0.0).astype(jnp.float32)
        has_south = jnp.where(lat < 7, 1.0, 0.0).astype(jnp.float32)
        window = self.window
        inner = slice(MARGIN, MARGIN + ROWS)
        above, below = slice(0, MARGIN), slice(MARGIN + ROWS, 2 * MARGIN + ROWS)
        middle = slice(MARGIN, MARGIN + COLS)
        window[above, middle, :] = f32(from_north[...]) * has_north
        window[below, middle, :] = f32(from_south[...]) * has_south
        for ref, side in (
            (from_west, slice(0, MARGIN)),
            (from_east, slice(MARGIN + COLS, 2 * MARGIN + COLS)),
        ):
            window[inner, side, :] = f32(ref[inner])
            window[above, side, :] = f32(ref[above]) * has_north
            window[below, side, :] = f32(ref[below]) * has_south


def convolve(window, weight, first, flip):
    def rows(base):
        sums = first(base)
        for i in range(KSIZE + 2):
            for b in range(KSIZE):
                piece = window[base + i, b : b + COLS, :]
                for o in range(3):
                    a = i - o
                    if 0 <= a < KSIZE:
                        tap = weight(KSIZE - 1 - a, KSIZE - 1 - b) if flip else weight(a, b)
                        sums[o] = sums[o] + piece * tap
        return sums

    return rows


def fold(value):
    return jnp.sum(value.reshape(value.shape[0] // 8, 8, value.shape[1]), axis=0)


def lane_mean(value):
    return jnp.mean(value, axis=-1, keepdims=True)


def step_kernel(
    *refs,
):
    arguments, refs = refs[:12], refs[12:]
    (
    out_hbm,
    state_hbm,
    sums_one,
    sums_two,
    win1,
    win2,
    gwin1,
    gwin2,
    taps,
    mask,
    mixed,
    hidden,
    active,
    slope,
    normed,
    inverse,
    branch,
    upstream,
    acc_win,
    acc_wout,
    acc_rows,
    acc_bias,
    acc_taps,
    h_east,
    h_west,
    h_north,
    h_south,
    h_from_west,
    h_from_east,
    h_from_north,
    h_from_south,
    sem_h,
    small,
    halves,
    from_core,
    send_a,
    recv_a,
    tiny_a,
    line_own,
    line_all,
    gather_one,
    gather_two,
    seeds,
    pulled,
    sem_core,
    sem_a,
    sem_tiny,
    sem_line,
    sem_back,
    sem_load,
    out,
    grad_state,
    sem_put,
    *arrived,
    ) = refs
    loads = [
        pltpu.make_async_copy(source, target, sem_load.at[n])
        for n, (source, target) in enumerate(zip(arguments, arrived))
    ]
    for load in loads:
        load.start()
    (
        state,
        land_sea,
        cotangent,
        dw_kernel,
        conv_bias,
        norm_gain,
        norm_bias,
        weight_in,
        bias_in,
        weight_out,
        bias_out,
        layer_scale,
    ) = arrived
    plane, z, core = position()
    barrier = pltpu.get_barrier_semaphore()
    announce(barrier)
    loads[0].wait()
    halo_bufs = (
        h_east, h_west, h_north, h_south, h_from_west, h_from_east, h_from_north, h_from_south
    )
    middle = slice(MARGIN, MARGIN + COLS)

    halo = Halo(halo_bufs, sem_h, 0, win1)
    halo.stage_from(state)
    pl.semaphore_wait(barrier, GROUP + LINE - 1 + len(AROUND))
    halo.launch()

    def widen(c, carry):
        win1[pl.ds(MARGIN + c * STRIP, STRIP), middle, :] = f32(state[pl.ds(c * STRIP, STRIP)])
        return carry

    lax.fori_loop(0, CHUNKS, widen, 0)
    for load in loads[1:]:
        load.wait()

    taps[...] = f32(dw_kernel[...])
    ocean_t = land_sea[...].astype(jnp.float32)
    for i in range(ROWS):
        mask[i] = jnp.broadcast_to(ocean_t[:, i : i + 1], (COLS, C))
    acc_win[...] = jnp.zeros_like(acc_win)
    acc_wout[...] = jnp.zeros_like(acc_wout)
    acc_rows[...] = jnp.zeros_like(acc_rows)
    acc_bias[...] = jnp.zeros_like(acc_bias)
    acc_taps[...] = jnp.zeros_like(acc_taps)
    small[...] = jnp.zeros_like(small)

    def mix(window, blk):
        start = jnp.broadcast_to(conv_bias[blk : blk + 1, :], (COLS, C))
        rows = convolve(
            window, lambda a, b: taps[a, b, blk : blk + 1, :], lambda base: [start] * 3, False
        )

        def three(g, carry):
            sums = rows(g * 3)
            for o in range(3):
                mixed[g * 3 + o] = sums[o]
            return carry

        lax.fori_loop(0, ROWS // 3, three, 0)

    def forward(c, window, blk, keep):
        x = mixed[pl.ds(c * STRIP, STRIP)].reshape(CELLS, C)
        center = x - lane_mean(x)
        inv = lax.rsqrt(lane_mean(center * center) + EPS_NORM)
        norm = center * inv
        normed[keep] = norm
        inverse[keep] = jnp.broadcast_to(inv, (CELLS, C))
        lifted = bf16(norm * norm_gain[blk : blk + 1, :] + norm_bias[blk : blk + 1, :])
        hidden[...] = jnp.dot(lifted, weight_in[blk], preferred_element_type=jnp.float32)

        def gelu(t, carry):
            rows = pl.ds(pl.multiple_of(t * COLS, 8), COLS)
            h = hidden[rows, :] + bias_in[blk : blk + 1, :]
            cumulative = 0.5 * (1.0 + lax.erf(h * INV_ROOT_TWO))
            density = jnp.exp(-0.5 * h * h) * INV_ROOT_TWO_PI
            active[keep, rows, :] = bf16(h * cumulative)
            slope[keep, rows, :] = cumulative + h * density
            return carry

        lax.fori_loop(0, STRIP, gelu, 0, unroll=3)
        act = active[keep]
        branch_c = (
            jnp.dot(act, weight_out[blk], preferred_element_type=jnp.float32)
            + bias_out[blk : blk + 1, :]
        )
        branch[keep] = branch_c
        inner = window[pl.ds(MARGIN + c * STRIP, STRIP), middle, :].reshape(CELLS, C)
        ocean = mask[pl.ds(c * STRIP, STRIP)].reshape(CELLS, C)
        return (inner + layer_scale[blk : blk + 1, :] * branch_c) * ocean

    def seed(c, incoming, blk):
        ocean = mask[pl.ds(c * STRIP, STRIP)].reshape(CELLS, C)
        masked = incoming * ocean
        upstream[pl.ds(c * STRIP, STRIP)] = masked.reshape(STRIP, COLS, C)
        gb = bf16(masked * layer_scale[blk : blk + 1, :])
        acc_rows[blk, 3] += fold(f32(gb))
        seeds[c] = gb
        pulled[c] = lax.dot_general(
            gb, weight_out[blk], (((1,), (1,)), ((), ())), preferred_element_type=jnp.float32
        )

    def backward(c, gwindow, blk, keep):
        masked = upstream[pl.ds(c * STRIP, STRIP)].reshape(CELLS, C)
        acc_rows[blk, 4] += fold(masked * branch[keep])
        rows_rows = (((0,), (0,)), ((), ()))
        cols_cols = (((1,), (1,)), ((), ()))
        acc_wout[blk] += lax.dot_general(
            seeds[c], active[keep], rows_rows, preferred_element_type=jnp.float32
        )

        gh = bf16(pulled[c] * slope[keep])
        acc_bias[blk] += jnp.dot(
            jnp.ones((8, CELLS), jnp.bfloat16), gh, preferred_element_type=jnp.float32
        )
        norm = normed[keep]
        gain = norm_gain[blk : blk + 1, :]
        lifted = bf16(norm * gain + norm_bias[blk : blk + 1, :])
        acc_win[blk] += lax.dot_general(
            lifted, gh, rows_rows, preferred_element_type=jnp.float32
        )
        gl = lax.dot_general(gh, weight_in[blk], cols_cols, preferred_element_type=jnp.float32)
        acc_rows[blk, 1] += fold(gl * norm)
        acc_rows[blk, 2] += fold(gl)
        s = gl * gain
        gm = inverse[keep] * (s - lane_mean(s) - norm * lane_mean(s * norm))
        gm = f32(bf16(gm))
        acc_rows[blk, 0] += fold(gm)
        gwindow[pl.ds(MARGIN + c * STRIP, STRIP), middle, :] = gm.reshape(STRIP, COLS, C)

    def tap_sums(window, gwindow, blk, begin, end):
        def three(g, carry):
            base = g * 3
            grads = [gwindow[base + MARGIN + o, middle, :] for o in range(3)]
            for b in range(KSIZE):
                parts = [None] * KSIZE
                for i in range(KSIZE + 2):
                    piece = window[base + i, b : b + COLS, :]
                    for o in range(3):
                        a = i - o
                        if 0 <= a < KSIZE:
                            term = piece * grads[o]
                            parts[a] = term if parts[a] is None else parts[a] + term
                for a in range(KSIZE):
                    acc_taps[blk, a * KSIZE + b] += fold(parts[a])
            return carry

        lax.fori_loop(begin, end, three, 0)

    def adjoint(gwindow, blk, put, begin, end):
        rows = convolve(
            gwindow,
            lambda a, b: taps[a, b, blk : blk + 1, :],
            lambda base: [upstream[base + o] for o in range(3)],
            True,
        )

        def three(g, carry):
            sums = rows(g * 3)
            for o in range(3):
                put(g * 3 + o, sums[o])
            return carry

        lax.fori_loop(begin, end, three, 0)

    def core_sum(blk):
        for q in range(4):
            block = slice(q * 128, q * 128 + 128)
            halves[blk, 0, block, :] = bf16(acc_win[blk, :, block])
            halves[blk, 1, block, :] = bf16(jnp.transpose(acc_wout[blk, :, block]))
        copy = to_sibling(halves.at[blk, 1 - core], from_core.at[blk], sem_core.at[blk])
        copy.start()
        return copy

    def plane_sum(copy, blk):
        copy.wait()
        both = f32(halves[blk, core]) + f32(from_core[blk])
        send_a[blk] = bf16(both).reshape(GROUP, PIECE, C)
        return Exchange("plane", True, send_a.at[blk], recv_a.at[blk], sem_a.at[blk]).start()

    def line_sum(ex, blk, tiny):
        ex.wait()
        total = bf16(slot_sum(f32(send_a[blk, plane]), recv_a.at[blk]))
        rows = line_all.at[blk] if tiny is not None else line_all.at[blk, :, 0:PIECE]
        line_all[blk, z, 0:PIECE] = total
        line_own[blk, 0:PIECE] = total
        own = line_own.at[blk, 0:PIECE]
        if tiny is not None:
            tiny.wait()
            tiny_total = bf16(slot_sum(small[plane], tiny_a))
            line_all[blk, z, PIECE : PIECE + 8] = tiny_total
            line_own[blk, PIECE : PIECE + 8] = tiny_total
            own = line_own.at[blk]
        return Exchange("line", False, own, rows, sem_line.at[blk]).start()

    def plane_back(ex, blk, gather):
        ex.wait()
        rows = gather.shape[2]
        own = f32(line_all[blk, 0, 0:rows])
        for j in range(1, LINE):
            own = own + f32(line_all[blk, j, 0:rows])
        gather[core, plane] = bf16(own)
        return Exchange(
            "plane", False, gather.at[core, plane], gather.at[core], sem_back.at[blk]
        ).start()

    def swap_halves(ex, blk, gather):
        ex.wait()
        copy = to_sibling(gather.at[core], gather.at[core], sem_core.at[BLOCKS + blk])
        copy.start()
        return copy

    def small_row(blk, r, value):
        i = blk * 4 + r % 4
        small[r // 4, i : i + 1, :] = jnp.sum(value, axis=0, keepdims=True)

    def pack_rows(blk):
        for tap in range(KSIZE * KSIZE):
            small_row(blk, tap, acc_taps[blk, tap])
        for k in range(5):
            small_row(blk, 49 + k, acc_rows[blk, k])
        for q in range(4):
            small_row(blk, 54 + q, acc_bias[blk, 0:1, q * 128 : q * 128 + 128])

    halo.finish()
    mix(win1, 0)

    def forward_one(c, carry):
        result = forward(c, win1, 0, c)
        win2[pl.ds(MARGIN + c * STRIP, STRIP), middle, :] = f32(bf16(result)).reshape(
            STRIP, COLS, C
        )
        return carry

    lax.fori_loop(0, CHUNKS, forward_one, 0)
    halo = Halo(halo_bufs, sem_h, 1, win2)
    halo.start()

    def seed_two(c, carry):
        seed(c, f32(cotangent[pl.ds(c * STRIP, STRIP)]).reshape(CELLS, C), 1)
        return carry

    lax.fori_loop(0, CHUNKS, seed_two, 0)
    halo.finish()
    mix(win2, 1)

    def both(c, carry):
        result = forward(c, win2, 1, CHUNKS)
        out[pl.ds(c * STRIP, STRIP)] = bf16(result.reshape(STRIP, COLS, C))
        backward(c, gwin2, 1, CHUNKS)
        return carry

    lax.fori_loop(0, CHUNKS, both, 0)
    put_out = pltpu.make_async_copy(out, out_hbm, sem_put.at[0])
    put_out.start()
    halo = Halo(halo_bufs, sem_h, 2, gwin2)
    halo.start()
    second = core_sum(1)
    tap_sums(win2, gwin2, 1, 0, 15)
    second = plane_sum(second, 1)
    pack_rows(1)
    halo.finish()

    def put_mixed(row, value):
        mixed[row] = f32(bf16(value))

    adjoint(gwin2, 1, put_mixed, 0, 15)
    second = line_sum(second, 1, None)

    def backward_one(c, carry):
        seed(c, mixed[pl.ds(c * STRIP, STRIP)].reshape(CELLS, C), 0)
        backward(c, gwin1, 0, c)
        return carry

    lax.fori_loop(0, CHUNKS, backward_one, 0)
    halo = Halo(halo_bufs, sem_h, 3, gwin1)
    halo.start()
    first = core_sum(0)
    second = plane_back(second, 1, gather_two)
    tap_sums(win1, gwin1, 0, 0, 6)
    first = plane_sum(first, 0)
    tap_sums(win1, gwin1, 0, 6, 15)
    pack_rows(0)
    tiny = Exchange("plane", True, small, tiny_a, sem_tiny).start()
    second = swap_halves(second, 1, gather_two)
    halo.finish()

    def put_state(row, value):
        grad_state[row] = bf16(value)

    adjoint(gwin1, 0, put_state, 0, 8)
    first = line_sum(first, 0, tiny)
    adjoint(gwin1, 0, put_state, 8, 15)
    put_grad = pltpu.make_async_copy(grad_state, state_hbm, sem_put.at[1])
    put_grad.start()
    second.wait()
    put_two = pltpu.make_async_copy(gather_two, sums_two, sem_put.at[2])
    put_two.start()
    first = plane_back(first, 0, gather_one)
    first = swap_halves(first, 0, gather_one)
    first.wait()
    put_one = pltpu.make_async_copy(gather_one, sums_one, sem_put.at[3])
    put_one.start()
    for put in (put_out, put_grad, put_two, put_one):
        put.wait()


def write_kernel(
    grad_norm,
    out_from,
    state_from,
    one_from,
    two_from,
    out,
    grad_state,
    g_kernel,
    g_conv,
    g_gain,
    g_shift,
    g_win,
    g_bias_in,
    g_wout,
    g_bias_out,
    g_scale,
    small,
    held,
    sums_one,
    sums_two,
    win,
    wout,
    sems,
):
    def move(source, target, n):
        copy = pltpu.make_async_copy(source, target, sems.at[n])
        copy.start()
        return copy

    two_in = move(two_from, sums_two, 0)
    fields_in = [move(out_from, held.at[0], 1), move(state_from, held.at[1], 2)]
    one_in = move(one_from, sums_one, 3)
    leaving = []

    def widen(blk, sums):
        rows = slice(0, PIECE)
        for p in range(GROUP):
            win[
                blk, (p % 4) * PIECE : (p % 4) * PIECE + PIECE, (p // 4) * 128 : (p // 4) * 128 + 128
            ] = f32(sums[0, p, rows, :]) * grad_norm
            wout[blk, p * PIECE : p * PIECE + PIECE] = f32(sums[1, p, rows, :]) * grad_norm
        leaving.append(move(win.at[blk], g_win.at[blk], 4 + 2 * blk))
        leaving.append(move(wout.at[blk], g_wout.at[blk], 5 + 2 * blk))

    two_in.wait()
    widen(1, sums_two)
    fields_in[0].wait()
    leaving.append(move(held.at[0], out, 8))
    fields_in[1].wait()
    leaving.append(move(held.at[1], grad_state, 9))
    one_in.wait()
    widen(0, sums_one)
    tiny = slice(PIECE, PIECE + 8)
    for p in range(GROUP):
        small[p] = (f32(sums_one[0, p, tiny, :]) + f32(sums_one[1, p, tiny, :])) * grad_norm
    for blk in range(BLOCKS):

        def row_of(r):
            return small[r // 4, blk * 4 + r % 4 : blk * 4 + r % 4 + 1, :]

        for a in range(KSIZE):
            for b in range(KSIZE):
                g_kernel[a, b, blk : blk + 1, :] = row_of(a * KSIZE + b)
        for k, ref in enumerate((g_conv, g_gain, g_shift, g_bias_out, g_scale)):
            ref[blk : blk + 1, :] = row_of(49 + k)
        for q in range(4):
            g_bias_in[blk : blk + 1, q * 128 : q * 128 + 128] = row_of(54 + q)
    for copy in leaving:
        copy.wait()


def on_device(
    state,
    land_sea,
    cotangent,
    dw_kernel,
    *rest,
):
    vmem = pl.BlockSpec(memory_space=pltpu.VMEM)
    anywhere = pl.BlockSpec(memory_space=pl.ANY)
    grad_norm = 1.0 / math.sqrt(
        lax.axis_size("lat") * ROWS * lax.axis_size("lon") * COLS
    )
    field = jax.ShapeDtypeStruct((ROWS, COLS, C), jnp.bfloat16)
    row = jax.ShapeDtypeStruct((BLOCKS, C), jnp.float32)

    def vm(*shape, dtype=jnp.float32):
        return pltpu.VMEM(shape, dtype)

    def sems(*shape):
        return pltpu.SemaphoreType.DMA(shape)

    tall, wide = ROWS + 2 * MARGIN, COLS + 8
    half = jnp.bfloat16
    packed = PIECE + 8
    arguments = (state, land_sea.T, cotangent, jnp.transpose(dw_kernel, (1, 2, 0, 3)), *rest)
    fields = pl.pallas_call(
        step_kernel,
        name="ocean_step",
        out_shape=(
            field,
            field,
            jax.ShapeDtypeStruct((2, GROUP, packed, C), jnp.bfloat16),
            jax.ShapeDtypeStruct((2, GROUP, PIECE, C), jnp.bfloat16),
        ),
        in_specs=[pl.BlockSpec(memory_space=pltpu.HBM)] * 12,
        out_specs=(anywhere,) * 4,
        scratch_shapes=[
            vm(tall, wide, C),
            vm(tall, wide, C),
            vm(tall, wide, C),
            vm(tall, wide, C),
            vm(KSIZE, KSIZE, BLOCKS, C),
            vm(ROWS, COLS, C),
            vm(ROWS, COLS, C),
            vm(CELLS, F),
            vm(CHUNKS + 1, CELLS, F, dtype=half),
            vm(CHUNKS + 1, CELLS, F),
            vm(CHUNKS + 1, CELLS, C),
            vm(CHUNKS + 1, CELLS, C),
            vm(CHUNKS + 1, CELLS, C),
            vm(ROWS, COLS, C),
            vm(BLOCKS, C, F),
            vm(BLOCKS, C, F),
            vm(BLOCKS, 5, 8, C),
            vm(BLOCKS, 8, F),
            vm(BLOCKS, KSIZE * KSIZE, 8, C),
            vm(4, ROWS, MARGIN, C, dtype=half),
            vm(4, ROWS, MARGIN, C, dtype=half),
            vm(4, MARGIN, COLS, C, dtype=half),
            vm(4, MARGIN, COLS, C, dtype=half),
            vm(4, tall, MARGIN, C, dtype=half),
            vm(4, tall, MARGIN, C, dtype=half),
            vm(4, MARGIN, COLS, C, dtype=half),
            vm(4, MARGIN, COLS, C, dtype=half),
            sems(4, 2, len(AROUND)),
            vm(GROUP, 8, C),
            vm(BLOCKS, 2, F, C, dtype=half),
            vm(BLOCKS, F, C, dtype=half),
            vm(BLOCKS, GROUP, PIECE, C, dtype=half),
            vm(BLOCKS, GROUP, PIECE, C, dtype=half),
            vm(GROUP, 8, C),
            vm(BLOCKS, packed, C, dtype=half),
            vm(BLOCKS, LINE, packed, C, dtype=half),
            vm(2, GROUP, packed, C, dtype=half),
            vm(2, GROUP, PIECE, C, dtype=half),
            vm(CHUNKS, CELLS, C, dtype=half),
            vm(CHUNKS, CELLS, F),
            sems(2 * BLOCKS, 2),
            sems(BLOCKS, 2),
            sems(2),
            sems(BLOCKS, 2),
            sems(BLOCKS, 2),
            sems(len(arguments)),
            vm(ROWS, COLS, C, dtype=half),
            vm(ROWS, COLS, C, dtype=half),
            sems(4),
            *(pltpu.VMEM(array.shape, array.dtype) for array in arguments),
        ],
        compiler_params=pltpu.CompilerParams(
            collective_id=0, has_side_effects=True, vmem_limit_bytes=58 << 20
        ),
    )(*arguments)
    results = pl.pallas_call(
        lambda *refs: write_kernel(grad_norm, *refs),
        name="write_results",
        out_shape=(
            field,
            field,
            jax.ShapeDtypeStruct((KSIZE, KSIZE, BLOCKS, C), jnp.float32),
            row,
            row,
            row,
            jax.ShapeDtypeStruct((BLOCKS, C, F), jnp.float32),
            jax.ShapeDtypeStruct((BLOCKS, F), jnp.float32),
            jax.ShapeDtypeStruct((BLOCKS, F, C), jnp.float32),
            row,
            row,
        ),
        in_specs=[anywhere] * 4,
        out_specs=(anywhere, anywhere, vmem, vmem, vmem, vmem, anywhere, vmem, anywhere, vmem, vmem),
        scratch_shapes=[
            vm(GROUP, 8, C),
            vm(2, ROWS, COLS, C, dtype=half),
            vm(2, GROUP, packed, C, dtype=half),
            vm(2, GROUP, PIECE, C, dtype=half),
            vm(BLOCKS, C, F),
            vm(BLOCKS, F, C),
            sems(10),
        ],
        compiler_params=pltpu.CompilerParams(vmem_limit_bytes=58 << 20),
    )(*fields)
    return results[:2] + (jnp.transpose(results[2], (2, 0, 1, 3)),) + results[3:]


def solution(mesh):
    field = P("lat", "lon", None)
    return jax.shard_map(
        on_device,
        mesh=mesh,
        in_specs=(field, P("lat", "lon"), field) + (P(),) * 9,
        out_specs=(field, field) + (P(),) * 9,
        check_vma=False,
    )
```

```python
import math

import jax
import jax.numpy as jnp
from jax import lax
from jax.experimental import pallas as pl
from jax.experimental.pallas import tpu as pltpu
from jax.sharding import PartitionSpec as P

KSIZE = 7
BLOCKS = 2
C = 128
F = 512
EPS_NORM = 1e-06
INV_ROOT_TWO = 0.7071067811865476
INV_ROOT_TWO_PI = 0.3989422804014327
MESH_ID = pl.DeviceIdType.MESH
GROUP = 16
LINE = 8
PIECE = 32
ROWS = 45
COLS = 24
MARGIN = 3
AROUND = ((1, 0), (-1, 0), (0, 1), (0, -1), (1, 1), (1, -1), (-1, 1), (-1, -1))
STRIP = 15
CHUNKS = ROWS // STRIP
CELLS = STRIP * COLS


def position():
    lon = lax.axis_index("lon")
    plane = lax.rem(lon // 2, 2) * 8 + lax.axis_index("lat")
    return plane, lon // 4, lax.rem(lon, 2)


def device(plane, z, core):
    return {"lon": z * 4 + (plane // 8) * 2 + core, "lat": lax.rem(plane, 8)}


def beside(east, south):
    return {
        "lon": lax.rem(lax.axis_index("lon") + east + 32, 32),
        "lat": lax.rem(lax.axis_index("lat") + south + 8, 8),
    }


def announce(barrier):
    plane, z, core = position()

    def signal(target):
        pl.semaphore_signal(barrier, inc=1, device_id=target, device_id_type=MESH_ID)

    for east, south in AROUND:
        signal(beside(east, south))
    signal(device(plane, z, 1 - core))

    def in_plane(k, carry):
        signal(device(lax.rem(plane + k, GROUP), z, core))
        return carry

    def in_line(k, carry):
        signal(device(plane, lax.rem(z + k, LINE), core))
        return carry

    lax.fori_loop(1, GROUP, in_plane, 0)
    lax.fori_loop(1, LINE, in_line, 0)


class Exchange:
    def __init__(self, kind, scatter, src, dst, sems):
        self.plane, self.z, self.core = position()
        self.kind, self.scatter = kind, scatter
        self.src, self.dst, self.sems = src, dst, sems
        self.me, self.size = (self.plane, GROUP) if kind == "plane" else (self.z, LINE)

    def start(self):
        for k in range(1, self.size):
            other = lax.rem(self.me + k, self.size)
            if self.kind == "plane":
                target = device(other, self.z, self.core)
            else:
                target = device(self.plane, other, self.core)
            pltpu.make_async_remote_copy(
                src_ref=self.src.at[other] if self.scatter else self.src,
                dst_ref=self.dst.at[k if self.scatter else self.me],
                send_sem=self.sems.at[0],
                recv_sem=self.sems.at[1],
                device_id=target,
                device_id_type=MESH_ID,
            ).start()
        return self

    def wait(self):
        others = pl.ds(1, self.size - 1)
        for side in range(2):
            pltpu.make_async_copy(
                self.dst.at[others], self.dst.at[others], self.sems.at[side]
            ).wait()


def to_sibling(src, dst, sems):
    plane, z, core = position()
    return pltpu.make_async_remote_copy(
        src_ref=src,
        dst_ref=dst,
        send_sem=sems.at[0],
        recv_sem=sems.at[1],
        device_id=device(plane, z, 1 - core),
        device_id_type=MESH_ID,
    )


def slot_sum(own, slots, count=GROUP):
    def one(k, total):
        return total + slots[k].astype(jnp.float32)

    return lax.fori_loop(1, count, one, own)


def f32(value):
    return value.astype(jnp.float32)


def bf16(value):
    return value.astype(jnp.bfloat16)


class Halo:
    def __init__(self, bufs, sems, index, window):
        east, west, north, south, from_west, from_east, from_north, from_south = (
            ref.at[index] for ref in bufs
        )
        self.bufs = (east, west, north, south, from_west, from_east, from_north, from_south)
        self.window = window
        last = ROWS - MARGIN
        tall = pl.ds(MARGIN, ROWS)
        above, below = pl.ds(0, MARGIN), pl.ds(MARGIN + ROWS, MARGIN)
        top, bottom = pl.ds(0, MARGIN), pl.ds(last, MARGIN)
        pairs = (
            (east, from_west.at[tall]),
            (west, from_east.at[tall]),
            (south, from_north),
            (north, from_south),
            (east.at[bottom], from_west.at[above]),
            (east.at[top], from_west.at[below]),
            (west.at[bottom], from_east.at[above]),
            (west.at[top], from_east.at[below]),
        )
        self.copies = [
            pltpu.make_async_remote_copy(
                src_ref=pair[0],
                dst_ref=pair[1],
                send_sem=sems.at[index, 0, k],
                recv_sem=sems.at[index, 1, k],
                device_id=beside(*AROUND[k]),
                device_id_type=MESH_ID,
            )
            for k, pair in enumerate(pairs)
        ]

    def start(self):
        self.stage()
        self.launch()

    def stage_from(self, tile):
        east, west, north, south = self.bufs[:4]
        east[...] = tile[:, COLS - MARGIN : COLS, :]
        west[...] = tile[:, 0:MARGIN, :]
        north[...] = tile[0:MARGIN]
        south[...] = tile[ROWS - MARGIN : ROWS]

    def stage(self):
        east, west, north, south = self.bufs[:4]
        window = self.window
        inner = slice(MARGIN, MARGIN + ROWS)
        east[...] = bf16(window[inner, COLS : COLS + MARGIN, :])
        west[...] = bf16(window[inner, MARGIN : 2 * MARGIN, :])
        north[...] = bf16(window[MARGIN : 2 * MARGIN, MARGIN : MARGIN + COLS, :])
        south[...] = bf16(window[ROWS : ROWS + MARGIN, MARGIN : MARGIN + COLS, :])

    def launch(self):
        for copy in self.copies:
            copy.start()

    def finish(self):
        for copy in self.copies:
            copy.wait()
        from_west, from_east, from_north, from_south = self.bufs[4:]
        lat = lax.axis_index("lat")
        has_north = jnp.where(lat > 0, 1.0, 0.0).astype(jnp.float32)
        has_south = jnp.where(lat < 7, 1.0, 0.0).astype(jnp.float32)
        window = self.window
        inner = slice(MARGIN, MARGIN + ROWS)
        above, below = slice(0, MARGIN), slice(MARGIN + ROWS, 2 * MARGIN + ROWS)
        middle = slice(MARGIN, MARGIN + COLS)
        window[above, middle, :] = f32(from_north[...]) * has_north
        window[below, middle, :] = f32(from_south[...]) * has_south
        for ref, side in (
            (from_west, slice(0, MARGIN)),
            (from_east, slice(MARGIN + COLS, 2 * MARGIN + COLS)),
        ):
            window[inner, side, :] = f32(ref[inner])
            window[above, side, :] = f32(ref[above]) * has_north
            window[below, side, :] = f32(ref[below]) * has_south


def convolve(window, weight, first, flip):
    def rows(base):
        sums = first(base)
        for i in range(KSIZE + 4):
            for b in range(KSIZE):
                piece = window[base + i, b : b + COLS, :]
                for o in range(5):
                    a = i - o
                    if 0 <= a < KSIZE:
                        tap = weight(KSIZE - 1 - a, KSIZE - 1 - b) if flip else weight(a, b)
                        sums[o] = sums[o] + piece * tap
        return sums

    return rows


def fold(value):
    return jnp.sum(value.reshape(value.shape[0] // 8, 8, value.shape[1]), axis=0)


def lane_mean(value):
    return jnp.mean(value, axis=-1, keepdims=True)


def step_kernel(
    *refs,
):
    arguments, refs = refs[:12], refs[12:]
    (
    out_hbm,
    state_hbm,
    sums_one,
    sums_two,
    win1,
    win2,
    gwin1,
    gwin2,
    taps,
    mask,
    mixed,
    hidden,
    active,
    slope,
    normed,
    inverse,
    branch,
    upstream,
    acc_win,
    acc_wout,
    acc_rows,
    acc_bias,
    acc_taps,
    h_east,
    h_west,
    h_north,
    h_south,
    h_from_west,
    h_from_east,
    h_from_north,
    h_from_south,
    sem_h,
    small,
    halves,
    from_core,
    send_a,
    recv_a,
    tiny_a,
    line_own,
    line_all,
    gather_one,
    gather_two,
    seeds,
    pulled,
    sem_core,
    sem_a,
    sem_tiny,
    sem_line,
    sem_back,
    sem_load,
    out,
    grad_state,
    sem_put,
    *arrived,
    ) = refs
    loads = [
        pltpu.make_async_copy(source, target, sem_load.at[n])
        for n, (source, target) in enumerate(zip(arguments, arrived))
    ]
    for load in loads:
        load.start()
    (
        state,
        land_sea,
        cotangent,
        dw_kernel,
        conv_bias,
        norm_gain,
        norm_bias,
        weight_in,
        bias_in,
        weight_out,
        bias_out,
        layer_scale,
    ) = arrived
    plane, z, core = position()
    barrier = pltpu.get_barrier_semaphore()
    announce(barrier)
    loads[0].wait()
    halo_bufs = (
        h_east, h_west, h_north, h_south, h_from_west, h_from_east, h_from_north, h_from_south
    )
    middle = slice(MARGIN, MARGIN + COLS)

    halo = Halo(halo_bufs, sem_h, 0, win1)
    halo.stage_from(state)
    pl.semaphore_wait(barrier, GROUP + LINE - 1 + len(AROUND))
    halo.launch()

    def widen(c, carry):
        win1[pl.ds(MARGIN + c * STRIP, STRIP), middle, :] = f32(state[pl.ds(c * STRIP, STRIP)])
        return carry

    lax.fori_loop(0, CHUNKS, widen, 0)
    for load in loads[1:]:
        load.wait()

    taps[...] = f32(dw_kernel[...])
    ocean_t = land_sea[...].astype(jnp.float32)
    for i in range(ROWS):
        mask[i] = jnp.broadcast_to(ocean_t[:, i : i + 1], (COLS, C))
    acc_win[...] = jnp.zeros_like(acc_win)
    acc_wout[...] = jnp.zeros_like(acc_wout)
    acc_rows[...] = jnp.zeros_like(acc_rows)
    acc_bias[...] = jnp.zeros_like(acc_bias)
    acc_taps[...] = jnp.zeros_like(acc_taps)
    small[...] = jnp.zeros_like(small)

    def mix(window, blk):
        start = jnp.broadcast_to(conv_bias[blk : blk + 1, :], (COLS, C))
        rows = convolve(
            window, lambda a, b: taps[a, b, blk : blk + 1, :], lambda base: [start] * 5, False
        )

        def five(g, carry):
            sums = rows(g * 5)
            for o in range(5):
                mixed[g * 5 + o] = sums[o]
            return carry

        lax.fori_loop(0, ROWS // 5, five, 0)

    def forward(c, window, blk, keep):
        x = mixed[pl.ds(c * STRIP, STRIP)].reshape(CELLS, C)
        center = x - lane_mean(x)
        inv = lax.rsqrt(lane_mean(center * center) + EPS_NORM)
        norm = center * inv
        normed[keep] = norm
        inverse[keep] = jnp.broadcast_to(inv, (CELLS, C))
        lifted = bf16(norm * norm_gain[blk : blk + 1, :] + norm_bias[blk : blk + 1, :])
        hidden[...] = jnp.dot(lifted, weight_in[blk], preferred_element_type=jnp.float32)

        def gelu(t, carry):
            rows = pl.ds(pl.multiple_of(t * COLS, 8), COLS)
            h = hidden[rows, :] + bias_in[blk : blk + 1, :]
            cumulative = 0.5 * (1.0 + lax.erf(h * INV_ROOT_TWO))
            density = jnp.exp(-0.5 * h * h) * INV_ROOT_TWO_PI
            active[keep, rows, :] = bf16(h * cumulative)
            slope[keep, rows, :] = cumulative + h * density
            return carry

        lax.fori_loop(0, STRIP, gelu, 0, unroll=15)
        act = active[keep]
        branch_c = (
            jnp.dot(act, weight_out[blk], preferred_element_type=jnp.float32)
            + bias_out[blk : blk + 1, :]
        )
        branch[keep] = branch_c
        inner = window[pl.ds(MARGIN + c * STRIP, STRIP), middle, :].reshape(CELLS, C)
        ocean = mask[pl.ds(c * STRIP, STRIP)].reshape(CELLS, C)
        return (inner + layer_scale[blk : blk + 1, :] * branch_c) * ocean

    def seed(c, incoming, blk):
        ocean = mask[pl.ds(c * STRIP, STRIP)].reshape(CELLS, C)
        masked = incoming * ocean
        upstream[pl.ds(c * STRIP, STRIP)] = masked.reshape(STRIP, COLS, C)
        gb = bf16(masked * layer_scale[blk : blk + 1, :])
        acc_rows[blk, 3] += fold(f32(gb))
        seeds[c] = gb
        pulled[c] = lax.dot_general(
            gb, weight_out[blk], (((1,), (1,)), ((), ())), preferred_element_type=jnp.float32
        )

    def backward(c, gwindow, blk, keep):
        masked = upstream[pl.ds(c * STRIP, STRIP)].reshape(CELLS, C)
        acc_rows[blk, 4] += fold(masked * branch[keep])
        rows_rows = (((0,), (0,)), ((), ()))
        cols_cols = (((1,), (1,)), ((), ()))
        acc_wout[blk] += lax.dot_general(
            seeds[c], active[keep], rows_rows, preferred_element_type=jnp.float32
        )

        gh = bf16(pulled[c] * slope[keep])
        acc_bias[blk] += jnp.dot(
            jnp.ones((8, CELLS), jnp.bfloat16), gh, preferred_element_type=jnp.float32
        )
        norm = normed[keep]
        gain = norm_gain[blk : blk + 1, :]
        lifted = bf16(norm * gain + norm_bias[blk : blk + 1, :])
        acc_win[blk] += lax.dot_general(
            lifted, gh, rows_rows, preferred_element_type=jnp.float32
        )
        gl = lax.dot_general(gh, weight_in[blk], cols_cols, preferred_element_type=jnp.float32)
        acc_rows[blk, 1] += fold(gl * norm)
        acc_rows[blk, 2] += fold(gl)
        s = gl * gain
        gm = inverse[keep] * (s - lane_mean(s) - norm * lane_mean(s * norm))
        gm = f32(bf16(gm))
        acc_rows[blk, 0] += fold(gm)
        gwindow[pl.ds(MARGIN + c * STRIP, STRIP), middle, :] = gm.reshape(STRIP, COLS, C)

    def tap_sums(window, gwindow, blk, begin, end):
        def three(g, carry):
            base = g * 3
            grads = [gwindow[base + MARGIN + o, middle, :] for o in range(3)]
            for b in range(KSIZE):
                parts = [None] * KSIZE
                for i in range(KSIZE + 2):
                    piece = window[base + i, b : b + COLS, :]
                    for o in range(3):
                        a = i - o
                        if 0 <= a < KSIZE:
                            term = piece * grads[o]
                            parts[a] = term if parts[a] is None else parts[a] + term
                for a in range(KSIZE):
                    acc_taps[blk, a * KSIZE + b] += fold(parts[a])
            return carry

        lax.fori_loop(begin, end, three, 0)

    def adjoint(gwindow, blk, put, begin, end):
        rows = convolve(
            gwindow,
            lambda a, b: taps[a, b, blk : blk + 1, :],
            lambda base: [upstream[base + o] for o in range(5)],
            True,
        )

        def five(g, carry):
            sums = rows(g * 5)
            for o in range(5):
                put(g * 5 + o, sums[o])
            return carry

        lax.fori_loop(begin, end, five, 0)

    def core_sum(blk):
        for q in range(4):
            block = slice(q * 128, q * 128 + 128)
            halves[blk, 0, block, :] = bf16(acc_win[blk, :, block])
            halves[blk, 1, block, :] = bf16(jnp.transpose(acc_wout[blk, :, block]))
        copy = to_sibling(halves.at[blk, 1 - core], from_core.at[blk], sem_core.at[blk])
        copy.start()
        return copy

    def plane_sum(copy, blk):
        copy.wait()
        both = f32(halves[blk, core]) + f32(from_core[blk])
        send_a[blk] = bf16(both).reshape(GROUP, PIECE, C)
        return Exchange("plane", True, send_a.at[blk], recv_a.at[blk], sem_a.at[blk]).start()

    def line_sum(ex, blk, tiny):
        ex.wait()
        total = bf16(slot_sum(f32(send_a[blk, plane]), recv_a.at[blk]))
        rows = line_all.at[blk] if tiny is not None else line_all.at[blk, :, 0:PIECE]
        line_all[blk, z, 0:PIECE] = total
        line_own[blk, 0:PIECE] = total
        own = line_own.at[blk, 0:PIECE]
        if tiny is not None:
            tiny.wait()
            tiny_total = bf16(slot_sum(small[plane], tiny_a))
            line_all[blk, z, PIECE : PIECE + 8] = tiny_total
            line_own[blk, PIECE : PIECE + 8] = tiny_total
            own = line_own.at[blk]
        return Exchange("line", False, own, rows, sem_line.at[blk]).start()

    def plane_back(ex, blk, gather):
        ex.wait()
        rows = gather.shape[2]
        own = f32(line_all[blk, 0, 0:rows])
        for j in range(1, LINE):
            own = own + f32(line_all[blk, j, 0:rows])
        gather[core, plane] = bf16(own)
        return Exchange(
            "plane", False, gather.at[core, plane], gather.at[core], sem_back.at[blk]
        ).start()

    def swap_halves(ex, blk, gather):
        ex.wait()
        copy = to_sibling(gather.at[core], gather.at[core], sem_core.at[BLOCKS + blk])
        copy.start()
        return copy

    def small_row(blk, r, value):
        i = blk * 4 + r % 4
        small[r // 4, i : i + 1, :] = jnp.sum(value, axis=0, keepdims=True)

    def pack_rows(blk):
        for tap in range(KSIZE * KSIZE):
            small_row(blk, tap, acc_taps[blk, tap])
        for k in range(5):
            small_row(blk, 49 + k, acc_rows[blk, k])
        for q in range(4):
            small_row(blk, 54 + q, acc_bias[blk, 0:1, q * 128 : q * 128 + 128])

    halo.finish()
    mix(win1, 0)

    def forward_one(c, carry):
        result = forward(c, win1, 0, c)
        win2[pl.ds(MARGIN + c * STRIP, STRIP), middle, :] = f32(bf16(result)).reshape(
            STRIP, COLS, C
        )
        return carry

    lax.fori_loop(0, CHUNKS, forward_one, 0)
    halo = Halo(halo_bufs, sem_h, 1, win2)
    halo.start()

    def seed_two(c, carry):
        seed(c, f32(cotangent[pl.ds(c * STRIP, STRIP)]).reshape(CELLS, C), 1)
        return carry

    lax.fori_loop(0, CHUNKS, seed_two, 0)
    halo.finish()
    mix(win2, 1)

    def both(c, carry):
        result = forward(c, win2, 1, CHUNKS)
        out[pl.ds(c * STRIP, STRIP)] = bf16(result.reshape(STRIP, COLS, C))
        backward(c, gwin2, 1, CHUNKS)
        return carry

    lax.fori_loop(0, CHUNKS, both, 0)
    put_out = pltpu.make_async_copy(out, out_hbm, sem_put.at[0])
    put_out.start()
    halo = Halo(halo_bufs, sem_h, 2, gwin2)
    halo.start()
    second = core_sum(1)
    tap_sums(win2, gwin2, 1, 0, 15)
    second = plane_sum(second, 1)
    pack_rows(1)
    halo.finish()

    def put_mixed(row, value):
        mixed[row] = f32(bf16(value))

    adjoint(gwin2, 1, put_mixed, 0, 9)
    second = line_sum(second, 1, None)

    def backward_one(c, carry):
        seed(c, mixed[pl.ds(c * STRIP, STRIP)].reshape(CELLS, C), 0)
        backward(c, gwin1, 0, c)
        return carry

    lax.fori_loop(0, CHUNKS, backward_one, 0)
    halo = Halo(halo_bufs, sem_h, 3, gwin1)
    halo.start()
    first = core_sum(0)
    tap_sums(win1, gwin1, 0, 0, 6)
    first = plane_sum(first, 0)
    tap_sums(win1, gwin1, 0, 6, 15)
    pack_rows(0)
    tiny = Exchange("plane", True, small, tiny_a, sem_tiny).start()
    second = plane_back(second, 1, gather_two)
    halo.finish()

    def put_state(row, value):
        grad_state[row] = bf16(value)

    adjoint(gwin1, 0, put_state, 0, 5)
    first = line_sum(first, 0, tiny)
    second = swap_halves(second, 1, gather_two)
    adjoint(gwin1, 0, put_state, 5, 9)
    put_grad = pltpu.make_async_copy(grad_state, state_hbm, sem_put.at[1])
    put_grad.start()
    second.wait()
    put_two = pltpu.make_async_copy(gather_two, sums_two, sem_put.at[2])
    put_two.start()
    first = plane_back(first, 0, gather_one)
    first = swap_halves(first, 0, gather_one)
    first.wait()
    put_one = pltpu.make_async_copy(gather_one, sums_one, sem_put.at[3])
    put_one.start()
    for put in (put_out, put_grad, put_two, put_one):
        put.wait()


def write_kernel(
    grad_norm,
    out_from,
    state_from,
    one_from,
    two_from,
    out,
    grad_state,
    g_kernel,
    g_conv,
    g_gain,
    g_shift,
    g_win,
    g_bias_in,
    g_wout,
    g_bias_out,
    g_scale,
    small,
    held,
    sums_one,
    sums_two,
    win,
    wout,
    sems,
):
    def move(source, target, n):
        copy = pltpu.make_async_copy(source, target, sems.at[n])
        copy.start()
        return copy

    two_in = move(two_from, sums_two, 0)
    fields_in = [move(out_from, held.at[0], 1), move(state_from, held.at[1], 2)]
    one_in = move(one_from, sums_one, 3)
    leaving = []

    def widen(blk, sums):
        rows = slice(0, PIECE)
        for p in range(GROUP):
            win[
                blk, (p % 4) * PIECE : (p % 4) * PIECE + PIECE, (p // 4) * 128 : (p // 4) * 128 + 128
            ] = f32(sums[0, p, rows, :]) * grad_norm
            wout[blk, p * PIECE : p * PIECE + PIECE] = f32(sums[1, p, rows, :]) * grad_norm
        leaving.append(move(win.at[blk], g_win.at[blk], 4 + 2 * blk))
        leaving.append(move(wout.at[blk], g_wout.at[blk], 5 + 2 * blk))

    two_in.wait()
    widen(1, sums_two)
    fields_in[0].wait()
    leaving.append(move(held.at[0], out, 8))
    fields_in[1].wait()
    leaving.append(move(held.at[1], grad_state, 9))
    one_in.wait()
    widen(0, sums_one)
    tiny = slice(PIECE, PIECE + 8)
    for p in range(GROUP):
        small[p] = (f32(sums_one[0, p, tiny, :]) + f32(sums_one[1, p, tiny, :])) * grad_norm
    for blk in range(BLOCKS):

        def row_of(r):
            return small[r // 4, blk * 4 + r % 4 : blk * 4 + r % 4 + 1, :]

        for a in range(KSIZE):
            for b in range(KSIZE):
                g_kernel[a, b, blk : blk + 1, :] = row_of(a * KSIZE + b)
        for k, ref in enumerate((g_conv, g_gain, g_shift, g_bias_out, g_scale)):
            ref[blk : blk + 1, :] = row_of(49 + k)
        for q in range(4):
            g_bias_in[blk : blk + 1, q * 128 : q * 128 + 128] = row_of(54 + q)
    for copy in leaving:
        copy.wait()


def on_device(
    state,
    land_sea,
    cotangent,
    dw_kernel,
    *rest,
):
    vmem = pl.BlockSpec(memory_space=pltpu.VMEM)
    anywhere = pl.BlockSpec(memory_space=pl.ANY)
    grad_norm = 1.0 / math.sqrt(
        lax.axis_size("lat") * ROWS * lax.axis_size("lon") * COLS
    )
    field = jax.ShapeDtypeStruct((ROWS, COLS, C), jnp.bfloat16)
    row = jax.ShapeDtypeStruct((BLOCKS, C), jnp.float32)

    def vm(*shape, dtype=jnp.float32):
        return pltpu.VMEM(shape, dtype)

    def sems(*shape):
        return pltpu.SemaphoreType.DMA(shape)

    tall, wide = ROWS + 2 * MARGIN, COLS + 8
    half = jnp.bfloat16
    packed = PIECE + 8
    arguments = (state, land_sea.T, cotangent, jnp.transpose(dw_kernel, (1, 2, 0, 3)), *rest)
    fields = pl.pallas_call(
        step_kernel,
        name="ocean_step",
        out_shape=(
            field,
            field,
            jax.ShapeDtypeStruct((2, GROUP, packed, C), jnp.bfloat16),
            jax.ShapeDtypeStruct((2, GROUP, PIECE, C), jnp.bfloat16),
        ),
        in_specs=[pl.BlockSpec(memory_space=pltpu.HBM)] * 12,
        out_specs=(anywhere,) * 4,
        scratch_shapes=[
            vm(tall, wide, C),
            vm(tall, wide, C),
            vm(tall, wide, C),
            vm(tall, wide, C),
            vm(KSIZE, KSIZE, BLOCKS, C),
            vm(ROWS, COLS, C),
            vm(ROWS, COLS, C),
            vm(CELLS, F),
            vm(CHUNKS + 1, CELLS, F, dtype=half),
            vm(CHUNKS + 1, CELLS, F),
            vm(CHUNKS + 1, CELLS, C),
            vm(CHUNKS + 1, CELLS, C),
            vm(CHUNKS + 1, CELLS, C),
            vm(ROWS, COLS, C),
            vm(BLOCKS, C, F),
            vm(BLOCKS, C, F),
            vm(BLOCKS, 5, 8, C),
            vm(BLOCKS, 8, F),
            vm(BLOCKS, KSIZE * KSIZE, 8, C),
            vm(4, ROWS, MARGIN, C, dtype=half),
            vm(4, ROWS, MARGIN, C, dtype=half),
            vm(4, MARGIN, COLS, C, dtype=half),
            vm(4, MARGIN, COLS, C, dtype=half),
            vm(4, tall, MARGIN, C, dtype=half),
            vm(4, tall, MARGIN, C, dtype=half),
            vm(4, MARGIN, COLS, C, dtype=half),
            vm(4, MARGIN, COLS, C, dtype=half),
            sems(4, 2, len(AROUND)),
            vm(GROUP, 8, C),
            vm(BLOCKS, 2, F, C, dtype=half),
            vm(BLOCKS, F, C, dtype=half),
            vm(BLOCKS, GROUP, PIECE, C, dtype=half),
            vm(BLOCKS, GROUP, PIECE, C, dtype=half),
            vm(GROUP, 8, C),
            vm(BLOCKS, packed, C, dtype=half),
            vm(BLOCKS, LINE, packed, C, dtype=half),
            vm(2, GROUP, packed, C, dtype=half),
            vm(2, GROUP, PIECE, C, dtype=half),
            vm(CHUNKS, CELLS, C, dtype=half),
            vm(CHUNKS, CELLS, F),
            sems(2 * BLOCKS, 2),
            sems(BLOCKS, 2),
            sems(2),
            sems(BLOCKS, 2),
            sems(BLOCKS, 2),
            sems(len(arguments)),
            vm(ROWS, COLS, C, dtype=half),
            vm(ROWS, COLS, C, dtype=half),
            sems(4),
            *(pltpu.VMEM(array.shape, array.dtype) for array in arguments),
        ],
        compiler_params=pltpu.CompilerParams(
            collective_id=0, has_side_effects=True, vmem_limit_bytes=58 << 20
        ),
    )(*arguments)
    results = pl.pallas_call(
        lambda *refs: write_kernel(grad_norm, *refs),
        name="write_results",
        out_shape=(
            field,
            field,
            jax.ShapeDtypeStruct((KSIZE, KSIZE, BLOCKS, C), jnp.float32),
            row,
            row,
            row,
            jax.ShapeDtypeStruct((BLOCKS, C, F), jnp.float32),
            jax.ShapeDtypeStruct((BLOCKS, F), jnp.float32),
            jax.ShapeDtypeStruct((BLOCKS, F, C), jnp.float32),
            row,
            row,
        ),
        in_specs=[anywhere] * 4,
        out_specs=(anywhere, anywhere, vmem, vmem, vmem, vmem, anywhere, vmem, anywhere, vmem, vmem),
        scratch_shapes=[
            vm(GROUP, 8, C),
            vm(2, ROWS, COLS, C, dtype=half),
            vm(2, GROUP, packed, C, dtype=half),
            vm(2, GROUP, PIECE, C, dtype=half),
            vm(BLOCKS, C, F),
            vm(BLOCKS, F, C),
            sems(10),
        ],
        compiler_params=pltpu.CompilerParams(vmem_limit_bytes=58 << 20),
    )(*fields)
    return results[:2] + (jnp.transpose(results[2], (2, 0, 1, 3)),) + results[3:]


def solution(mesh):
    field = P("lat", "lon", None)
    return jax.shard_map(
        on_device,
        mesh=mesh,
        in_specs=(field, P("lat", "lon"), field) + (P(),) * 9,
        out_specs=(field, field) + (P(),) * 9,
        check_vma=False,
    )
```

```python
import math

import jax
import jax.numpy as jnp
from jax import lax
from jax.experimental import pallas as pl
from jax.experimental.pallas import tpu as pltpu
from jax.sharding import PartitionSpec as P

KSIZE = 7
BLOCKS = 2
C = 128
F = 512
EPS_NORM = 1e-06
INV_ROOT_TWO = 0.7071067811865476
INV_ROOT_TWO_PI = 0.3989422804014327
MESH_ID = pl.DeviceIdType.MESH
GROUP = 16
LINE = 8
PIECE = 32
ROWS = 45
COLS = 24
MARGIN = 3
AROUND = ((1, 0), (-1, 0), (0, 1), (0, -1), (1, 1), (1, -1), (-1, 1), (-1, -1))
STRIP = 15
CHUNKS = ROWS // STRIP
CELLS = STRIP * COLS


def position():
    lon = lax.axis_index("lon")
    plane = lax.rem(lon // 2, 2) * 8 + lax.axis_index("lat")
    return plane, lon // 4, lax.rem(lon, 2)


def device(plane, z, core):
    return {"lon": z * 4 + (plane // 8) * 2 + core, "lat": lax.rem(plane, 8)}


def beside(east, south):
    return {
        "lon": lax.rem(lax.axis_index("lon") + east + 32, 32),
        "lat": lax.rem(lax.axis_index("lat") + south + 8, 8),
    }


def announce(barrier):
    plane, z, core = position()

    def signal(target):
        pl.semaphore_signal(barrier, inc=1, device_id=target, device_id_type=MESH_ID)

    for east, south in AROUND:
        signal(beside(east, south))
    signal(device(plane, z, 1 - core))

    def in_plane(k, carry):
        signal(device(lax.rem(plane + k, GROUP), z, core))
        return carry

    def in_line(k, carry):
        signal(device(plane, lax.rem(z + k, LINE), core))
        return carry

    lax.fori_loop(1, GROUP, in_plane, 0)
    lax.fori_loop(1, LINE, in_line, 0)


class Exchange:
    def __init__(self, kind, scatter, src, dst, sems):
        self.plane, self.z, self.core = position()
        self.kind, self.scatter = kind, scatter
        self.src, self.dst, self.sems = src, dst, sems
        self.me, self.size = (self.plane, GROUP) if kind == "plane" else (self.z, LINE)

    def start(self):
        for k in range(1, self.size):
            other = lax.rem(self.me + k, self.size)
            if self.kind == "plane":
                target = device(other, self.z, self.core)
            else:
                target = device(self.plane, other, self.core)
            pltpu.make_async_remote_copy(
                src_ref=self.src.at[other] if self.scatter else self.src,
                dst_ref=self.dst.at[k if self.scatter else self.me],
                send_sem=self.sems.at[0],
                recv_sem=self.sems.at[1],
                device_id=target,
                device_id_type=MESH_ID,
            ).start()
        return self

    def wait(self):
        others = pl.ds(1, self.size - 1)
        for side in range(2):
            pltpu.make_async_copy(
                self.dst.at[others], self.dst.at[others], self.sems.at[side]
            ).wait()


def to_sibling(src, dst, sems):
    plane, z, core = position()
    return pltpu.make_async_remote_copy(
        src_ref=src,
        dst_ref=dst,
        send_sem=sems.at[0],
        recv_sem=sems.at[1],
        device_id=device(plane, z, 1 - core),
        device_id_type=MESH_ID,
    )


def slot_sum(own, slots, count=GROUP):
    def one(k, total):
        return total + slots[k].astype(jnp.float32)

    return lax.fori_loop(1, count, one, own)


def f32(value):
    return value.astype(jnp.float32)


def bf16(value):
    return value.astype(jnp.bfloat16)


class Halo:
    def __init__(self, bufs, sems, index, window):
        east, west, north, south, self.sides, self.ends = (ref.at[index] for ref in bufs)
        from_west, from_east = self.sides.at[0], self.sides.at[1]
        from_north, from_south = self.ends.at[0], self.ends.at[1]
        self.sems = sems.at[index]
        self.bufs = (east, west, north, south, from_west, from_east, from_north, from_south)
        self.window = window
        last = ROWS - MARGIN
        tall = pl.ds(MARGIN, ROWS)
        above, below = pl.ds(0, MARGIN), pl.ds(MARGIN + ROWS, MARGIN)
        top, bottom = pl.ds(0, MARGIN), pl.ds(last, MARGIN)
        pairs = (
            (east, from_west.at[tall]),
            (west, from_east.at[tall]),
            (south, from_north),
            (north, from_south),
            (east.at[bottom], from_west.at[above]),
            (east.at[top], from_west.at[below]),
            (west.at[bottom], from_east.at[above]),
            (west.at[top], from_east.at[below]),
        )
        self.copies = [
            pltpu.make_async_remote_copy(
                src_ref=pair[0],
                dst_ref=pair[1],
                send_sem=sems.at[index, 0, int(k in (2, 3))],
                recv_sem=sems.at[index, 1, int(k in (2, 3))],
                device_id=beside(*AROUND[k]),
                device_id_type=MESH_ID,
            )
            for k, pair in enumerate(pairs)
        ]

    def start(self):
        self.stage()
        self.launch()

    def stage_from(self, tile):
        east, west, north, south = self.bufs[:4]
        east[...] = tile[:, COLS - MARGIN : COLS, :]
        west[...] = tile[:, 0:MARGIN, :]
        north[...] = tile[0:MARGIN]
        south[...] = tile[ROWS - MARGIN : ROWS]

    def stage(self):
        east, west, north, south = self.bufs[:4]
        window = self.window
        inner = slice(MARGIN, MARGIN + ROWS)
        east[...] = bf16(window[inner, COLS : COLS + MARGIN, :])
        west[...] = bf16(window[inner, MARGIN : 2 * MARGIN, :])
        north[...] = bf16(window[MARGIN : 2 * MARGIN, MARGIN : MARGIN + COLS, :])
        south[...] = bf16(window[ROWS : ROWS + MARGIN, MARGIN : MARGIN + COLS, :])

    def launch(self):
        for copy in self.copies:
            copy.start()

    def finish(self):
        for kind, ref in enumerate((self.sides, self.ends)):
            for side in range(2):
                pltpu.make_async_copy(ref, ref, self.sems.at[side, kind]).wait()
        from_west, from_east, from_north, from_south = self.bufs[4:]
        lat = lax.axis_index("lat")
        has_north = jnp.where(lat > 0, 1.0, 0.0).astype(jnp.float32)
        has_south = jnp.where(lat < 7, 1.0, 0.0).astype(jnp.float32)
        window = self.window
        inner = slice(MARGIN, MARGIN + ROWS)
        above, below = slice(0, MARGIN), slice(MARGIN + ROWS, 2 * MARGIN + ROWS)
        middle = slice(MARGIN, MARGIN + COLS)
        window[above, middle, :] = f32(from_north[...]) * has_north
        window[below, middle, :] = f32(from_south[...]) * has_south
        for ref, side in (
            (from_west, slice(0, MARGIN)),
            (from_east, slice(MARGIN + COLS, 2 * MARGIN + COLS)),
        ):
            window[inner, side, :] = f32(ref[inner])
            window[above, side, :] = f32(ref[above]) * has_north
            window[below, side, :] = f32(ref[below]) * has_south


def convolve(window, weight, first, flip):
    def rows(base):
        sums = first(base)
        for i in range(KSIZE + 4):
            for b in range(KSIZE):
                piece = window[base + i, b : b + COLS, :]
                for o in range(5):
                    a = i - o
                    if 0 <= a < KSIZE:
                        tap = weight(KSIZE - 1 - a, KSIZE - 1 - b) if flip else weight(a, b)
                        sums[o] = sums[o] + piece * tap
        return sums

    return rows


def fold(value):
    return jnp.sum(value.reshape(value.shape[0] // 8, 8, value.shape[1]), axis=0)


def lane_mean(value):
    return jnp.mean(value, axis=-1, keepdims=True)


def step_kernel(
    *refs,
):
    arguments, refs = refs[:12], refs[12:]
    (
    out_hbm,
    state_hbm,
    sums_one,
    sums_two,
    win1,
    win2,
    gwin1,
    gwin2,
    taps,
    mask,
    mixed,
    hidden,
    active,
    slope,
    normed,
    inverse,
    branch,
    upstream,
    acc_win,
    acc_wout,
    acc_rows,
    acc_bias,
    acc_taps,
    h_east,
    h_west,
    h_north,
    h_south,
    h_sides,
    h_ends,
    sem_h,
    small,
    halves,
    from_core,
    send_a,
    recv_a,
    tiny_a,
    line_own,
    line_all,
    gather_one,
    gather_two,
    seeds,
    pulled,
    sem_core,
    sem_a,
    sem_tiny,
    sem_line,
    sem_back,
    sem_load,
    out,
    grad_state,
    sem_put,
    *arrived,
    ) = refs
    loads = [
        pltpu.make_async_copy(source, target, sem_load.at[n])
        for n, (source, target) in enumerate(zip(arguments, arrived))
    ]
    for load in loads:
        load.start()
    (
        state,
        land_sea,
        cotangent,
        dw_kernel,
        conv_bias,
        norm_gain,
        norm_bias,
        weight_in,
        bias_in,
        weight_out,
        bias_out,
        layer_scale,
    ) = arrived
    plane, z, core = position()
    barrier = pltpu.get_barrier_semaphore()
    announce(barrier)
    loads[0].wait()
    halo_bufs = (
        h_east, h_west, h_north, h_south, h_sides, h_ends
    )
    middle = slice(MARGIN, MARGIN + COLS)

    halo = Halo(halo_bufs, sem_h, 0, win1)
    halo.stage_from(state)
    pl.semaphore_wait(barrier, GROUP + LINE - 1 + len(AROUND))
    halo.launch()

    def widen(c, carry):
        win1[pl.ds(MARGIN + c * STRIP, STRIP), middle, :] = f32(state[pl.ds(c * STRIP, STRIP)])
        return carry

    lax.fori_loop(0, CHUNKS, widen, 0)
    for load in loads[1:]:
        load.wait()

    taps[...] = f32(dw_kernel[...])
    ocean_t = land_sea[...].astype(jnp.float32)
    for i in range(ROWS):
        mask[i] = jnp.broadcast_to(ocean_t[:, i : i + 1], (COLS, C))
    acc_win[...] = jnp.zeros_like(acc_win)
    acc_wout[...] = jnp.zeros_like(acc_wout)
    acc_rows[...] = jnp.zeros_like(acc_rows)
    acc_bias[...] = jnp.zeros_like(acc_bias)
    acc_taps[...] = jnp.zeros_like(acc_taps)
    small[...] = jnp.zeros_like(small)

    def mix(window, blk):
        start = jnp.broadcast_to(conv_bias[blk : blk + 1, :], (COLS, C))
        rows = convolve(
            window, lambda a, b: taps[a, b, blk : blk + 1, :], lambda base: [start] * 5, False
        )

        def five(g, carry):
            sums = rows(g * 5)
            for o in range(5):
                mixed[g * 5 + o] = sums[o]
            return carry

        lax.fori_loop(0, ROWS // 5, five, 0)

    def forward(c, window, blk, keep):
        x = mixed[pl.ds(c * STRIP, STRIP)].reshape(CELLS, C)
        center = x - lane_mean(x)
        inv = lax.rsqrt(lane_mean(center * center) + EPS_NORM)
        norm = center * inv
        normed[keep] = norm
        inverse[keep] = jnp.broadcast_to(inv, (CELLS, C))
        lifted = bf16(norm * norm_gain[blk : blk + 1, :] + norm_bias[blk : blk + 1, :])
        hidden[...] = jnp.dot(lifted, weight_in[blk], preferred_element_type=jnp.float32)

        def gelu(t, carry):
            rows = pl.ds(pl.multiple_of(t * COLS, 8), COLS)
            h = hidden[rows, :] + bias_in[blk : blk + 1, :]
            cumulative = 0.5 * (1.0 + lax.erf(h * INV_ROOT_TWO))
            density = jnp.exp(-0.5 * h * h) * INV_ROOT_TWO_PI
            active[keep, rows, :] = bf16(h * cumulative)
            slope[keep, rows, :] = cumulative + h * density
            return carry

        lax.fori_loop(0, STRIP, gelu, 0, unroll=15)
        act = active[keep]
        branch_c = (
            jnp.dot(act, weight_out[blk], preferred_element_type=jnp.float32)
            + bias_out[blk : blk + 1, :]
        )
        branch[keep] = branch_c
        inner = window[pl.ds(MARGIN + c * STRIP, STRIP), middle, :].reshape(CELLS, C)
        ocean = mask[pl.ds(c * STRIP, STRIP)].reshape(CELLS, C)
        return (inner + layer_scale[blk : blk + 1, :] * branch_c) * ocean

    def seed(c, incoming, blk):
        ocean = mask[pl.ds(c * STRIP, STRIP)].reshape(CELLS, C)
        masked = incoming * ocean
        upstream[pl.ds(c * STRIP, STRIP)] = masked.reshape(STRIP, COLS, C)
        gb = bf16(masked * layer_scale[blk : blk + 1, :])
        acc_rows[blk, 3] += fold(f32(gb))
        seeds[c] = gb
        pulled[c] = lax.dot_general(
            gb, weight_out[blk], (((1,), (1,)), ((), ())), preferred_element_type=jnp.float32
        )

    def backward(c, gwindow, blk, keep):
        masked = upstream[pl.ds(c * STRIP, STRIP)].reshape(CELLS, C)
        acc_rows[blk, 4] += fold(masked * branch[keep])
        rows_rows = (((0,), (0,)), ((), ()))
        cols_cols = (((1,), (1,)), ((), ()))
        acc_wout[blk] += lax.dot_general(
            seeds[c], active[keep], rows_rows, preferred_element_type=jnp.float32
        )

        gh = bf16(pulled[c] * slope[keep])
        acc_bias[blk] += jnp.dot(
            jnp.ones((8, CELLS), jnp.bfloat16), gh, preferred_element_type=jnp.float32
        )
        norm = normed[keep]
        gain = norm_gain[blk : blk + 1, :]
        lifted = bf16(norm * gain + norm_bias[blk : blk + 1, :])
        acc_win[blk] += lax.dot_general(
            lifted, gh, rows_rows, preferred_element_type=jnp.float32
        )
        gl = lax.dot_general(gh, weight_in[blk], cols_cols, preferred_element_type=jnp.float32)
        acc_rows[blk, 1] += fold(gl * norm)
        acc_rows[blk, 2] += fold(gl)
        s = gl * gain
        gm = inverse[keep] * (s - lane_mean(s) - norm * lane_mean(s * norm))
        gm = f32(bf16(gm))
        acc_rows[blk, 0] += fold(gm)
        gwindow[pl.ds(MARGIN + c * STRIP, STRIP), middle, :] = gm.reshape(STRIP, COLS, C)

    def tap_sums(window, gwindow, blk, begin, end):
        def five(g, carry):
            base = g * 5
            grads = [gwindow[base + MARGIN + o, middle, :] for o in range(5)]
            for b in range(KSIZE):
                parts = [None] * KSIZE
                for i in range(KSIZE + 4):
                    piece = window[base + i, b : b + COLS, :]
                    for o in range(5):
                        a = i - o
                        if 0 <= a < KSIZE:
                            term = piece * grads[o]
                            parts[a] = term if parts[a] is None else parts[a] + term
                for a in range(KSIZE):
                    acc_taps[blk, a * KSIZE + b] += fold(parts[a])
            return carry

        lax.fori_loop(begin, end, five, 0)

    def adjoint(gwindow, blk, put, begin, end):
        rows = convolve(
            gwindow,
            lambda a, b: taps[a, b, blk : blk + 1, :],
            lambda base: [upstream[base + o] for o in range(5)],
            True,
        )

        def five(g, carry):
            sums = rows(g * 5)
            for o in range(5):
                put(g * 5 + o, sums[o])
            return carry

        lax.fori_loop(begin, end, five, 0)

    def core_sum(blk):
        for q in range(4):
            block = slice(q * 128, q * 128 + 128)
            halves[blk, 0, block, :] = bf16(acc_win[blk, :, block])
            halves[blk, 1, block, :] = bf16(jnp.transpose(acc_wout[blk, :, block]))
        copy = to_sibling(halves.at[blk, 1 - core], from_core.at[blk], sem_core.at[blk])
        copy.start()
        return copy

    def plane_sum(copy, blk):
        copy.wait()
        both = f32(halves[blk, core]) + f32(from_core[blk])
        send_a[blk] = bf16(both).reshape(GROUP, PIECE, C)
        return Exchange("plane", True, send_a.at[blk], recv_a.at[blk], sem_a.at[blk]).start()

    def line_sum(ex, blk, tiny):
        ex.wait()
        total = bf16(slot_sum(f32(send_a[blk, plane]), recv_a.at[blk]))
        rows = line_all.at[blk] if tiny is not None else line_all.at[blk, :, 0:PIECE]
        line_all[blk, z, 0:PIECE] = total
        line_own[blk, 0:PIECE] = total
        own = line_own.at[blk, 0:PIECE]
        if tiny is not None:
            tiny.wait()
            tiny_total = bf16(slot_sum(small[plane], tiny_a))
            line_all[blk, z, PIECE : PIECE + 8] = tiny_total
            line_own[blk, PIECE : PIECE + 8] = tiny_total
            own = line_own.at[blk]
        return Exchange("line", False, own, rows, sem_line.at[blk]).start()

    def plane_back(ex, blk, gather):
        ex.wait()
        rows = gather.shape[2]
        own = f32(line_all[blk, 0, 0:rows])
        for j in range(1, LINE):
            own = own + f32(line_all[blk, j, 0:rows])
        gather[core, plane] = bf16(own)
        return Exchange(
            "plane", False, gather.at[core, plane], gather.at[core], sem_back.at[blk]
        ).start()

    def swap_halves(ex, blk, gather):
        ex.wait()
        copy = to_sibling(gather.at[core], gather.at[core], sem_core.at[BLOCKS + blk])
        copy.start()
        return copy

    def small_row(blk, r, value):
        i = blk * 4 + r % 4
        small[r // 4, i : i + 1, :] = jnp.sum(value, axis=0, keepdims=True)

    def pack_rows(blk):
        for tap in range(KSIZE * KSIZE):
            small_row(blk, tap, acc_taps[blk, tap])
        for k in range(5):
            small_row(blk, 49 + k, acc_rows[blk, k])
        for q in range(4):
            small_row(blk, 54 + q, acc_bias[blk, 0:1, q * 128 : q * 128 + 128])

    halo.finish()
    mix(win1, 0)

    def forward_one(c, carry):
        result = forward(c, win1, 0, c)
        win2[pl.ds(MARGIN + c * STRIP, STRIP), middle, :] = f32(bf16(result)).reshape(
            STRIP, COLS, C
        )
        return carry

    lax.fori_loop(0, CHUNKS, forward_one, 0, unroll=True)
    halo = Halo(halo_bufs, sem_h, 1, win2)
    halo.start()

    def seed_two(c, carry):
        seed(c, f32(cotangent[pl.ds(c * STRIP, STRIP)]).reshape(CELLS, C), 1)
        return carry

    lax.fori_loop(0, CHUNKS, seed_two, 0, unroll=True)
    halo.finish()
    mix(win2, 1)

    def both(c, carry):
        result = forward(c, win2, 1, CHUNKS)
        out[pl.ds(c * STRIP, STRIP)] = bf16(result.reshape(STRIP, COLS, C))
        backward(c, gwin2, 1, CHUNKS)
        return carry

    lax.fori_loop(0, CHUNKS, both, 0, unroll=True)
    put_out = pltpu.make_async_copy(out, out_hbm, sem_put.at[0])
    put_out.start()
    halo = Halo(halo_bufs, sem_h, 2, gwin2)
    halo.start()
    second = core_sum(1)
    tap_sums(win2, gwin2, 1, 0, 9)
    second = plane_sum(second, 1)
    pack_rows(1)
    halo.finish()

    def put_mixed(row, value):
        mixed[row] = f32(bf16(value))

    adjoint(gwin2, 1, put_mixed, 0, 9)
    second = line_sum(second, 1, None)

    def backward_one(c, carry):
        seed(c, mixed[pl.ds(c * STRIP, STRIP)].reshape(CELLS, C), 0)
        backward(c, gwin1, 0, c)
        return carry

    lax.fori_loop(0, CHUNKS, backward_one, 0, unroll=True)
    halo = Halo(halo_bufs, sem_h, 3, gwin1)
    halo.start()
    first = core_sum(0)
    tap_sums(win1, gwin1, 0, 0, 4)
    first = plane_sum(first, 0)
    tap_sums(win1, gwin1, 0, 4, 9)
    pack_rows(0)
    tiny = Exchange("plane", True, small, tiny_a, sem_tiny).start()
    second = plane_back(second, 1, gather_two)
    halo.finish()

    def put_state(row, value):
        grad_state[row] = bf16(value)

    adjoint(gwin1, 0, put_state, 0, 5)
    first = line_sum(first, 0, tiny)
    second = swap_halves(second, 1, gather_two)
    adjoint(gwin1, 0, put_state, 5, 9)
    put_grad = pltpu.make_async_copy(grad_state, state_hbm, sem_put.at[1])
    put_grad.start()
    second.wait()
    put_two = pltpu.make_async_copy(gather_two, sums_two, sem_put.at[2])
    put_two.start()
    first = plane_back(first, 0, gather_one)
    first = swap_halves(first, 0, gather_one)
    first.wait()
    put_one = pltpu.make_async_copy(gather_one, sums_one, sem_put.at[3])
    put_one.start()
    for put in (put_out, put_grad, put_two, put_one):
        put.wait()


def write_kernel(
    grad_norm,
    out_from,
    state_from,
    one_from,
    two_from,
    out,
    grad_state,
    g_kernel,
    g_conv,
    g_gain,
    g_shift,
    g_win,
    g_bias_in,
    g_wout,
    g_bias_out,
    g_scale,
    small,
    held,
    sums_one,
    sums_two,
    win,
    wout,
    sems,
):
    def move(source, target, n):
        copy = pltpu.make_async_copy(source, target, sems.at[n])
        copy.start()
        return copy

    two_in = move(two_from, sums_two, 0)
    fields_in = [move(out_from, held.at[0], 1), move(state_from, held.at[1], 2)]
    one_in = move(one_from, sums_one, 3)
    leaving = []

    def widen(blk, sums):
        rows = slice(0, PIECE)
        for p in range(GROUP):
            win[
                blk, (p % 4) * PIECE : (p % 4) * PIECE + PIECE, (p // 4) * 128 : (p // 4) * 128 + 128
            ] = f32(sums[0, p, rows, :]) * grad_norm
            wout[blk, p * PIECE : p * PIECE + PIECE] = f32(sums[1, p, rows, :]) * grad_norm
        leaving.append(move(win.at[blk], g_win.at[blk], 4 + 2 * blk))
        leaving.append(move(wout.at[blk], g_wout.at[blk], 5 + 2 * blk))

    two_in.wait()
    widen(1, sums_two)
    fields_in[0].wait()
    leaving.append(move(held.at[0], out, 8))
    fields_in[1].wait()
    leaving.append(move(held.at[1], grad_state, 9))
    one_in.wait()
    widen(0, sums_one)
    tiny = slice(PIECE, PIECE + 8)
    for p in range(GROUP):
        small[p] = (f32(sums_one[0, p, tiny, :]) + f32(sums_one[1, p, tiny, :])) * grad_norm
    for blk in range(BLOCKS):

        def row_of(r):
            return small[r // 4, blk * 4 + r % 4 : blk * 4 + r % 4 + 1, :]

        for a in range(KSIZE):
            for b in range(KSIZE):
                g_kernel[a, b, blk : blk + 1, :] = row_of(a * KSIZE + b)
        for k, ref in enumerate((g_conv, g_gain, g_shift, g_bias_out, g_scale)):
            ref[blk : blk + 1, :] = row_of(49 + k)
        for q in range(4):
            g_bias_in[blk : blk + 1, q * 128 : q * 128 + 128] = row_of(54 + q)
    for copy in leaving:
        copy.wait()


def on_device(
    state,
    land_sea,
    cotangent,
    dw_kernel,
    *rest,
):
    vmem = pl.BlockSpec(memory_space=pltpu.VMEM)
    anywhere = pl.BlockSpec(memory_space=pl.ANY)
    grad_norm = 1.0 / math.sqrt(
        lax.axis_size("lat") * ROWS * lax.axis_size("lon") * COLS
    )
    field = jax.ShapeDtypeStruct((ROWS, COLS, C), jnp.bfloat16)
    row = jax.ShapeDtypeStruct((BLOCKS, C), jnp.float32)

    def vm(*shape, dtype=jnp.float32):
        return pltpu.VMEM(shape, dtype)

    def sems(*shape):
        return pltpu.SemaphoreType.DMA(shape)

    tall, wide = ROWS + 2 * MARGIN, COLS + 8
    half = jnp.bfloat16
    packed = PIECE + 8
    arguments = (state, land_sea.T, cotangent, jnp.transpose(dw_kernel, (1, 2, 0, 3)), *rest)
    fields = pl.pallas_call(
        step_kernel,
        name="ocean_step",
        out_shape=(
            field,
            field,
            jax.ShapeDtypeStruct((2, GROUP, packed, C), jnp.bfloat16),
            jax.ShapeDtypeStruct((2, GROUP, PIECE, C), jnp.bfloat16),
        ),
        in_specs=[pl.BlockSpec(memory_space=pltpu.HBM)] * 12,
        out_specs=(anywhere,) * 4,
        scratch_shapes=[
            vm(tall, wide, C),
            vm(tall, wide, C),
            vm(tall, wide, C),
            vm(tall, wide, C),
            vm(KSIZE, KSIZE, BLOCKS, C),
            vm(ROWS, COLS, C),
            vm(ROWS, COLS, C),
            vm(CELLS, F),
            vm(CHUNKS + 1, CELLS, F, dtype=half),
            vm(CHUNKS + 1, CELLS, F),
            vm(CHUNKS + 1, CELLS, C),
            vm(CHUNKS + 1, CELLS, C),
            vm(CHUNKS + 1, CELLS, C),
            vm(ROWS, COLS, C),
            vm(BLOCKS, C, F),
            vm(BLOCKS, C, F),
            vm(BLOCKS, 5, 8, C),
            vm(BLOCKS, 8, F),
            vm(BLOCKS, KSIZE * KSIZE, 8, C),
            vm(4, ROWS, MARGIN, C, dtype=half),
            vm(4, ROWS, MARGIN, C, dtype=half),
            vm(4, MARGIN, COLS, C, dtype=half),
            vm(4, MARGIN, COLS, C, dtype=half),
            vm(4, 2, tall, MARGIN, C, dtype=half),
            vm(4, 2, MARGIN, COLS, C, dtype=half),
            sems(4, 2, 2),
            vm(GROUP, 8, C),
            vm(BLOCKS, 2, F, C, dtype=half),
            vm(BLOCKS, F, C, dtype=half),
            vm(BLOCKS, GROUP, PIECE, C, dtype=half),
            vm(BLOCKS, GROUP, PIECE, C, dtype=half),
            vm(GROUP, 8, C),
            vm(BLOCKS, packed, C, dtype=half),
            vm(BLOCKS, LINE, packed, C, dtype=half),
            vm(2, GROUP, packed, C, dtype=half),
            vm(2, GROUP, PIECE, C, dtype=half),
            vm(CHUNKS, CELLS, C, dtype=half),
            vm(CHUNKS, CELLS, F),
            sems(2 * BLOCKS, 2),
            sems(BLOCKS, 2),
            sems(2),
            sems(BLOCKS, 2),
            sems(BLOCKS, 2),
            sems(len(arguments)),
            vm(ROWS, COLS, C, dtype=half),
            vm(ROWS, COLS, C, dtype=half),
            sems(4),
            *(pltpu.VMEM(array.shape, array.dtype) for array in arguments),
        ],
        compiler_params=pltpu.CompilerParams(
            collective_id=0, has_side_effects=True, vmem_limit_bytes=58 << 20
        ),
    )(*arguments)
    results = pl.pallas_call(
        lambda *refs: write_kernel(grad_norm, *refs),
        name="write_results",
        out_shape=(
            field,
            field,
            jax.ShapeDtypeStruct((KSIZE, KSIZE, BLOCKS, C), jnp.float32),
            row,
            row,
            row,
            jax.ShapeDtypeStruct((BLOCKS, C, F), jnp.float32),
            jax.ShapeDtypeStruct((BLOCKS, F), jnp.float32),
            jax.ShapeDtypeStruct((BLOCKS, F, C), jnp.float32),
            row,
            row,
        ),
        in_specs=[anywhere] * 4,
        out_specs=(anywhere, anywhere, vmem, vmem, vmem, vmem, anywhere, vmem, anywhere, vmem, vmem),
        scratch_shapes=[
            vm(GROUP, 8, C),
            vm(2, ROWS, COLS, C, dtype=half),
            vm(2, GROUP, packed, C, dtype=half),
            vm(2, GROUP, PIECE, C, dtype=half),
            vm(BLOCKS, C, F),
            vm(BLOCKS, F, C),
            sems(10),
        ],
        compiler_params=pltpu.CompilerParams(vmem_limit_bytes=58 << 20),
    )(*fields)
    return results[:2] + (jnp.transpose(results[2], (2, 0, 1, 3)),) + results[3:]


def solution(mesh):
    field = P("lat", "lon", None)
    return jax.shard_map(
        on_device,
        mesh=mesh,
        in_specs=(field, P("lat", "lon"), field) + (P(),) * 9,
        out_specs=(field, field) + (P(),) * 9,
        check_vma=False,
    )
```

```python
import math

import jax
import jax.numpy as jnp
from jax import lax
from jax.experimental import pallas as pl
from jax.experimental.pallas import tpu as pltpu
from jax.sharding import PartitionSpec as P

KSIZE = 7
BLOCKS = 2
C = 128
F = 512
EPS_NORM = 1e-06
INV_ROOT_TWO = 0.7071067811865476
INV_ROOT_TWO_PI = 0.3989422804014327
MESH_ID = pl.DeviceIdType.MESH
GROUP = 16
LINE = 8
PIECE = 32
ROWS = 45
COLS = 24
MARGIN = 3
AROUND = ((1, 0), (-1, 0), (0, 1), (0, -1), (1, 1), (1, -1), (-1, 1), (-1, -1))
STRIP = 15
CHUNKS = ROWS // STRIP
CELLS = STRIP * COLS


def position():
    lon = lax.axis_index("lon")
    plane = lax.rem(lon // 2, 2) * 8 + lax.axis_index("lat")
    return plane, lon // 4, lax.rem(lon, 2)


def device(plane, z, core):
    return {"lon": z * 4 + (plane // 8) * 2 + core, "lat": lax.rem(plane, 8)}


def beside(east, south):
    return {
        "lon": lax.rem(lax.axis_index("lon") + east + 32, 32),
        "lat": lax.rem(lax.axis_index("lat") + south + 8, 8),
    }


def announce(barrier):
    plane, z, core = position()

    def signal(target):
        pl.semaphore_signal(barrier, inc=1, device_id=target, device_id_type=MESH_ID)

    for east, south in AROUND:
        signal(beside(east, south))
    signal(device(plane, z, 1 - core))

    def in_plane(k, carry):
        signal(device(lax.rem(plane + k, GROUP), z, core))
        return carry

    def in_line(k, carry):
        signal(device(plane, lax.rem(z + k, LINE), core))
        return carry

    for k in range(1, GROUP):
        in_plane(k, 0)
    for k in range(1, LINE):
        in_line(k, 0)


class Exchange:
    def __init__(self, kind, scatter, src, dst, sems):
        self.plane, self.z, self.core = position()
        self.kind, self.scatter = kind, scatter
        self.src, self.dst, self.sems = src, dst, sems
        self.me, self.size = (self.plane, GROUP) if kind == "plane" else (self.z, LINE)

    def start(self):
        for k in range(1, self.size):
            other = lax.rem(self.me + k, self.size)
            if self.kind == "plane":
                target = device(other, self.z, self.core)
            else:
                target = device(self.plane, other, self.core)
            pltpu.make_async_remote_copy(
                src_ref=self.src.at[other] if self.scatter else self.src,
                dst_ref=self.dst.at[k if self.scatter else self.me],
                send_sem=self.sems.at[0],
                recv_sem=self.sems.at[1],
                device_id=target,
                device_id_type=MESH_ID,
            ).start()
        return self

    def wait(self):
        others = pl.ds(1, self.size - 1)
        for side in range(2):
            pltpu.make_async_copy(
                self.dst.at[others], self.dst.at[others], self.sems.at[side]
            ).wait()


def to_sibling(src, dst, sems):
    plane, z, core = position()
    return pltpu.make_async_remote_copy(
        src_ref=src,
        dst_ref=dst,
        send_sem=sems.at[0],
        recv_sem=sems.at[1],
        device_id=device(plane, z, 1 - core),
        device_id_type=MESH_ID,
    )


def slot_sum(own, slots, count=GROUP):
    def one(k, total):
        return total + slots[k].astype(jnp.float32)

    return lax.fori_loop(1, count, one, own)


def f32(value):
    return value.astype(jnp.float32)


def bf16(value):
    return value.astype(jnp.bfloat16)


class Halo:
    def __init__(self, bufs, sems, index, window):
        east, west, north, south, self.sides, self.ends = (ref.at[index] for ref in bufs)
        from_west, from_east = self.sides.at[0], self.sides.at[1]
        from_north, from_south = self.ends.at[0], self.ends.at[1]
        self.sems = sems.at[index]
        self.bufs = (east, west, north, south, from_west, from_east, from_north, from_south)
        self.window = window
        last = ROWS - MARGIN
        tall = pl.ds(MARGIN, ROWS)
        above, below = pl.ds(0, MARGIN), pl.ds(MARGIN + ROWS, MARGIN)
        top, bottom = pl.ds(0, MARGIN), pl.ds(last, MARGIN)
        pairs = (
            (east, from_west.at[tall]),
            (west, from_east.at[tall]),
            (south, from_north),
            (north, from_south),
            (east.at[bottom], from_west.at[above]),
            (east.at[top], from_west.at[below]),
            (west.at[bottom], from_east.at[above]),
            (west.at[top], from_east.at[below]),
        )
        self.copies = [
            pltpu.make_async_remote_copy(
                src_ref=pair[0],
                dst_ref=pair[1],
                send_sem=sems.at[index, 0, int(k in (2, 3))],
                recv_sem=sems.at[index, 1, int(k in (2, 3))],
                device_id=beside(*AROUND[k]),
                device_id_type=MESH_ID,
            )
            for k, pair in enumerate(pairs)
        ]

    def start(self):
        self.stage()
        self.launch()

    def stage_from(self, tile):
        east, west, north, south = self.bufs[:4]
        east[...] = tile[:, COLS - MARGIN : COLS, :]
        west[...] = tile[:, 0:MARGIN, :]
        north[...] = tile[0:MARGIN]
        south[...] = tile[ROWS - MARGIN : ROWS]

    def stage(self):
        east, west, north, south = self.bufs[:4]
        window = self.window
        inner = slice(MARGIN, MARGIN + ROWS)
        east[...] = bf16(window[inner, COLS : COLS + MARGIN, :])
        west[...] = bf16(window[inner, MARGIN : 2 * MARGIN, :])
        north[...] = bf16(window[MARGIN : 2 * MARGIN, MARGIN : MARGIN + COLS, :])
        south[...] = bf16(window[ROWS : ROWS + MARGIN, MARGIN : MARGIN + COLS, :])

    def launch(self):
        for copy in self.copies:
            copy.start()

    def finish(self):
        for kind, ref in enumerate((self.sides, self.ends)):
            for side in range(2):
                pltpu.make_async_copy(ref, ref, self.sems.at[side, kind]).wait()
        from_west, from_east, from_north, from_south = self.bufs[4:]
        lat = lax.axis_index("lat")
        has_north = jnp.where(lat > 0, 1.0, 0.0).astype(jnp.float32)
        has_south = jnp.where(lat < 7, 1.0, 0.0).astype(jnp.float32)
        window = self.window
        inner = slice(MARGIN, MARGIN + ROWS)
        above, below = slice(0, MARGIN), slice(MARGIN + ROWS, 2 * MARGIN + ROWS)
        middle = slice(MARGIN, MARGIN + COLS)
        window[above, middle, :] = f32(from_north[...]) * has_north
        window[below, middle, :] = f32(from_south[...]) * has_south
        for ref, side in (
            (from_west, slice(0, MARGIN)),
            (from_east, slice(MARGIN + COLS, 2 * MARGIN + COLS)),
        ):
            window[inner, side, :] = f32(ref[inner])
            window[above, side, :] = f32(ref[above]) * has_north
            window[below, side, :] = f32(ref[below]) * has_south


def convolve(window, weight, first, flip):
    def rows(base):
        sums = first(base)
        for i in range(KSIZE + 4):
            for b in range(KSIZE):
                piece = window[base + i, b : b + COLS, :]
                for o in range(5):
                    a = i - o
                    if 0 <= a < KSIZE:
                        tap = weight(KSIZE - 1 - a, KSIZE - 1 - b) if flip else weight(a, b)
                        sums[o] = sums[o] + piece * tap
        return sums

    return rows


def fold(value):
    return jnp.sum(value.reshape(value.shape[0] // 8, 8, value.shape[1]), axis=0)


def lane_mean(value):
    return jnp.mean(value, axis=-1, keepdims=True)


def step_kernel(
    *refs,
):
    arguments, refs = refs[:12], refs[12:]
    (
    out_hbm,
    state_hbm,
    sums_one,
    sums_two,
    win1,
    win2,
    gwin1,
    gwin2,
    taps,
    mask,
    mixed,
    hidden,
    active,
    slope,
    normed,
    inverse,
    branch,
    upstream,
    acc_win,
    acc_wout,
    acc_rows,
    acc_bias,
    acc_taps,
    h_east,
    h_west,
    h_north,
    h_south,
    h_sides,
    h_ends,
    sem_h,
    small,
    halves,
    from_core,
    send_a,
    recv_a,
    tiny_a,
    line_own,
    line_all,
    gather_one,
    gather_two,
    seeds,
    pulled,
    sem_core,
    sem_a,
    sem_tiny,
    sem_line,
    sem_back,
    sem_load,
    out,
    grad_state,
    sem_put,
    *arrived,
    ) = refs
    loads = [
        pltpu.make_async_copy(source, target, sem_load.at[n])
        for n, (source, target) in enumerate(zip(arguments, arrived))
    ]
    for load in loads:
        load.start()
    (
        state,
        land_sea,
        cotangent,
        dw_kernel,
        conv_bias,
        norm_gain,
        norm_bias,
        weight_in,
        bias_in,
        weight_out,
        bias_out,
        layer_scale,
    ) = arrived
    plane, z, core = position()
    barrier = pltpu.get_barrier_semaphore()
    announce(barrier)
    loads[0].wait()
    halo_bufs = (
        h_east, h_west, h_north, h_south, h_sides, h_ends
    )
    middle = slice(MARGIN, MARGIN + COLS)

    halo = Halo(halo_bufs, sem_h, 0, win1)
    halo.stage_from(state)
    pl.semaphore_wait(barrier, GROUP + LINE - 1 + len(AROUND))
    halo.launch()

    def widen(c, carry):
        win1[pl.ds(MARGIN + c * STRIP, STRIP), middle, :] = f32(state[pl.ds(c * STRIP, STRIP)])
        return carry

    lax.fori_loop(0, CHUNKS, widen, 0)
    for load in loads[1:]:
        load.wait()

    taps[...] = f32(dw_kernel[...])
    ocean_t = land_sea[...].astype(jnp.float32)
    for i in range(ROWS):
        mask[i] = jnp.broadcast_to(ocean_t[:, i : i + 1], (COLS, C))
    acc_win[...] = jnp.zeros_like(acc_win)
    acc_wout[...] = jnp.zeros_like(acc_wout)
    acc_rows[...] = jnp.zeros_like(acc_rows)
    acc_bias[...] = jnp.zeros_like(acc_bias)
    acc_taps[...] = jnp.zeros_like(acc_taps)
    small[...] = jnp.zeros_like(small)

    def mix(window, blk):
        start = jnp.broadcast_to(conv_bias[blk : blk + 1, :], (COLS, C))
        rows = convolve(
            window, lambda a, b: taps[a, b, blk : blk + 1, :], lambda base: [start] * 5, False
        )

        def five(g, carry):
            sums = rows(g * 5)
            for o in range(5):
                mixed[g * 5 + o] = sums[o]
            return carry

        lax.fori_loop(0, ROWS // 5, five, 0, unroll=3)

    def forward(c, window, blk, keep):
        x = mixed[pl.ds(c * STRIP, STRIP)].reshape(CELLS, C)
        center = x - lane_mean(x)
        inv = lax.rsqrt(lane_mean(center * center) + EPS_NORM)
        norm = center * inv
        normed[keep] = norm
        inverse[keep] = jnp.broadcast_to(inv, (CELLS, C))
        lifted = bf16(norm * norm_gain[blk : blk + 1, :] + norm_bias[blk : blk + 1, :])
        hidden[...] = jnp.dot(lifted, weight_in[blk], preferred_element_type=jnp.float32)

        def gelu(t, carry):
            rows = pl.ds(pl.multiple_of(t * COLS, 8), COLS)
            h = hidden[rows, :] + bias_in[blk : blk + 1, :]
            cumulative = 0.5 * (1.0 + lax.erf(h * INV_ROOT_TWO))
            density = jnp.exp(-0.5 * h * h) * INV_ROOT_TWO_PI
            active[keep, rows, :] = bf16(h * cumulative)
            slope[keep, rows, :] = cumulative + h * density
            return carry

        lax.fori_loop(0, STRIP, gelu, 0, unroll=15)
        act = active[keep]
        branch_c = (
            jnp.dot(act, weight_out[blk], preferred_element_type=jnp.float32)
            + bias_out[blk : blk + 1, :]
        )
        branch[keep] = branch_c
        inner = window[pl.ds(MARGIN + c * STRIP, STRIP), middle, :].reshape(CELLS, C)
        ocean = mask[pl.ds(c * STRIP, STRIP)].reshape(CELLS, C)
        return (inner + layer_scale[blk : blk + 1, :] * branch_c) * ocean

    def seed(c, incoming, blk):
        ocean = mask[pl.ds(c * STRIP, STRIP)].reshape(CELLS, C)
        masked = incoming * ocean
        upstream[pl.ds(c * STRIP, STRIP)] = masked.reshape(STRIP, COLS, C)
        gb = bf16(masked * layer_scale[blk : blk + 1, :])
        acc_rows[blk, 3] += fold(f32(gb))
        seeds[c] = gb
        pulled[c] = lax.dot_general(
            gb, weight_out[blk], (((1,), (1,)), ((), ())), preferred_element_type=jnp.float32
        )

    def backward(c, gwindow, blk, keep):
        masked = upstream[pl.ds(c * STRIP, STRIP)].reshape(CELLS, C)
        acc_rows[blk, 4] += fold(masked * branch[keep])
        rows_rows = (((0,), (0,)), ((), ()))
        cols_cols = (((1,), (1,)), ((), ()))
        acc_wout[blk] += lax.dot_general(
            seeds[c], active[keep], rows_rows, preferred_element_type=jnp.float32
        )

        gh = bf16(pulled[c] * slope[keep])
        acc_bias[blk] += jnp.dot(
            jnp.ones((8, CELLS), jnp.bfloat16), gh, preferred_element_type=jnp.float32
        )
        norm = normed[keep]
        gain = norm_gain[blk : blk + 1, :]
        lifted = bf16(norm * gain + norm_bias[blk : blk + 1, :])
        acc_win[blk] += lax.dot_general(
            lifted, gh, rows_rows, preferred_element_type=jnp.float32
        )
        gl = lax.dot_general(gh, weight_in[blk], cols_cols, preferred_element_type=jnp.float32)
        acc_rows[blk, 1] += fold(gl * norm)
        acc_rows[blk, 2] += fold(gl)
        s = gl * gain
        gm = inverse[keep] * (s - lane_mean(s) - norm * lane_mean(s * norm))
        gm = f32(bf16(gm))
        acc_rows[blk, 0] += fold(gm)
        gwindow[pl.ds(MARGIN + c * STRIP, STRIP), middle, :] = gm.reshape(STRIP, COLS, C)

    def tap_sums(window, gwindow, blk, begin, end):
        def five(g, carry):
            base = g * 5
            grads = [gwindow[base + MARGIN + o, middle, :] for o in range(5)]
            for b in range(KSIZE):
                parts = [None] * KSIZE
                for i in range(KSIZE + 4):
                    piece = window[base + i, b : b + COLS, :]
                    for o in range(5):
                        a = i - o
                        if 0 <= a < KSIZE:
                            term = piece * grads[o]
                            parts[a] = term if parts[a] is None else parts[a] + term
                for a in range(KSIZE):
                    acc_taps[blk, a * KSIZE + b] += fold(parts[a])
            return carry

        lax.fori_loop(begin, end, five, 0)

    def adjoint(gwindow, blk, put, begin, end):
        rows = convolve(
            gwindow,
            lambda a, b: taps[a, b, blk : blk + 1, :],
            lambda base: [upstream[base + o] for o in range(5)],
            True,
        )

        def five(g, carry):
            sums = rows(g * 5)
            for o in range(5):
                put(g * 5 + o, sums[o])
            return carry

        lax.fori_loop(begin, end, five, 0)

    def core_sum(blk):
        for q in range(4):
            block = slice(q * 128, q * 128 + 128)
            halves[blk, 0, block, :] = bf16(acc_win[blk, :, block])
            halves[blk, 1, block, :] = bf16(jnp.transpose(acc_wout[blk, :, block]))
        copy = to_sibling(halves.at[blk, 1 - core], from_core.at[blk], sem_core.at[blk])
        copy.start()
        return copy

    def plane_sum(copy, blk):
        copy.wait()
        both = f32(halves[blk, core]) + f32(from_core[blk])
        send_a[blk] = bf16(both).reshape(GROUP, PIECE, C)
        return Exchange("plane", True, send_a.at[blk], recv_a.at[blk], sem_a.at[blk]).start()

    def line_sum(ex, blk, tiny):
        ex.wait()
        total = bf16(slot_sum(f32(send_a[blk, plane]), recv_a.at[blk]))
        rows = line_all.at[blk] if tiny is not None else line_all.at[blk, :, 0:PIECE]
        line_all[blk, z, 0:PIECE] = total
        line_own[blk, 0:PIECE] = total
        own = line_own.at[blk, 0:PIECE]
        if tiny is not None:
            tiny.wait()
            tiny_total = bf16(slot_sum(small[plane], tiny_a))
            line_all[blk, z, PIECE : PIECE + 8] = tiny_total
            line_own[blk, PIECE : PIECE + 8] = tiny_total
            own = line_own.at[blk]
        return Exchange("line", False, own, rows, sem_line.at[blk]).start()

    def plane_back(ex, blk, gather):
        ex.wait()
        rows = gather.shape[2]
        own = f32(line_all[blk, 0, 0:rows])
        for j in range(1, LINE):
            own = own + f32(line_all[blk, j, 0:rows])
        gather[core, plane] = bf16(own)
        return Exchange(
            "plane", False, gather.at[core, plane], gather.at[core], sem_back.at[blk]
        ).start()

    def swap_halves(ex, blk, gather):
        ex.wait()
        copy = to_sibling(gather.at[core], gather.at[core], sem_core.at[BLOCKS + blk])
        copy.start()
        return copy

    def small_row(blk, r, value):
        i = blk * 4 + r % 4
        small[r // 4, i : i + 1, :] = jnp.sum(value, axis=0, keepdims=True)

    def pack_rows(blk):
        for tap in range(KSIZE * KSIZE):
            small_row(blk, tap, acc_taps[blk, tap])
        for k in range(5):
            small_row(blk, 49 + k, acc_rows[blk, k])
        for q in range(4):
            small_row(blk, 54 + q, acc_bias[blk, 0:1, q * 128 : q * 128 + 128])

    halo.finish()
    mix(win1, 0)

    def forward_one(c, carry):
        result = forward(c, win1, 0, c)
        win2[pl.ds(MARGIN + c * STRIP, STRIP), middle, :] = f32(bf16(result)).reshape(
            STRIP, COLS, C
        )
        return carry

    lax.fori_loop(0, CHUNKS, forward_one, 0, unroll=True)
    halo = Halo(halo_bufs, sem_h, 1, win2)
    halo.start()

    def seed_two(c, carry):
        seed(c, f32(cotangent[pl.ds(c * STRIP, STRIP)]).reshape(CELLS, C), 1)
        return carry

    lax.fori_loop(0, CHUNKS, seed_two, 0, unroll=True)
    halo.finish()
    mix(win2, 1)

    def both(c, carry):
        result = forward(c, win2, 1, CHUNKS)
        out[pl.ds(c * STRIP, STRIP)] = bf16(result.reshape(STRIP, COLS, C))
        backward(c, gwin2, 1, CHUNKS)
        return carry

    lax.fori_loop(0, CHUNKS, both, 0, unroll=True)
    put_out = pltpu.make_async_copy(out, out_hbm, sem_put.at[0])
    put_out.start()
    halo = Halo(halo_bufs, sem_h, 2, gwin2)
    halo.start()
    second = core_sum(1)
    tap_sums(win2, gwin2, 1, 0, 9)
    second = plane_sum(second, 1)
    pack_rows(1)
    halo.finish()

    def put_mixed(row, value):
        mixed[row] = f32(bf16(value))

    adjoint(gwin2, 1, put_mixed, 0, 9)
    second = line_sum(second, 1, None)

    def backward_one(c, carry):
        seed(c, mixed[pl.ds(c * STRIP, STRIP)].reshape(CELLS, C), 0)
        backward(c, gwin1, 0, c)
        return carry

    lax.fori_loop(0, CHUNKS, backward_one, 0, unroll=True)
    halo = Halo(halo_bufs, sem_h, 3, gwin1)
    halo.start()
    first = core_sum(0)
    tap_sums(win1, gwin1, 0, 0, 4)
    first = plane_sum(first, 0)
    tap_sums(win1, gwin1, 0, 4, 9)
    pack_rows(0)
    tiny = Exchange("plane", True, small, tiny_a, sem_tiny).start()
    second = plane_back(second, 1, gather_two)
    halo.finish()

    def put_state(row, value):
        grad_state[row] = bf16(value)

    adjoint(gwin1, 0, put_state, 0, 5)
    first = line_sum(first, 0, tiny)
    second = swap_halves(second, 1, gather_two)
    adjoint(gwin1, 0, put_state, 5, 9)
    put_grad = pltpu.make_async_copy(grad_state, state_hbm, sem_put.at[1])
    put_grad.start()
    second.wait()
    put_two = pltpu.make_async_copy(gather_two, sums_two, sem_put.at[2])
    put_two.start()
    first = plane_back(first, 0, gather_one)
    first = swap_halves(first, 0, gather_one)
    first.wait()
    put_one = pltpu.make_async_copy(gather_one, sums_one, sem_put.at[3])
    put_one.start()
    for put in (put_out, put_grad, put_two, put_one):
        put.wait()


def write_kernel(
    grad_norm,
    out_from,
    state_from,
    one_from,
    two_from,
    out,
    grad_state,
    g_kernel,
    g_conv,
    g_gain,
    g_shift,
    g_win,
    g_bias_in,
    g_wout,
    g_bias_out,
    g_scale,
    small,
    held,
    sums_one,
    sums_two,
    win,
    wout,
    sems,
):
    def move(source, target, n):
        copy = pltpu.make_async_copy(source, target, sems.at[n])
        copy.start()
        return copy

    two_in = move(two_from, sums_two, 0)
    fields_in = [move(out_from, held.at[0], 1), move(state_from, held.at[1], 2)]
    one_in = move(one_from, sums_one, 3)
    leaving = []

    def widen(blk, sums):
        rows = slice(0, PIECE)
        for p in range(GROUP):
            win[
                blk, (p % 4) * PIECE : (p % 4) * PIECE + PIECE, (p // 4) * 128 : (p // 4) * 128 + 128
            ] = f32(sums[0, p, rows, :]) * grad_norm
            wout[blk, p * PIECE : p * PIECE + PIECE] = f32(sums[1, p, rows, :]) * grad_norm
        leaving.append(move(win.at[blk], g_win.at[blk], 4 + 2 * blk))
        leaving.append(move(wout.at[blk], g_wout.at[blk], 5 + 2 * blk))

    two_in.wait()
    widen(1, sums_two)
    fields_in[0].wait()
    leaving.append(move(held.at[0], out, 8))
    fields_in[1].wait()
    leaving.append(move(held.at[1], grad_state, 9))
    one_in.wait()
    widen(0, sums_one)
    tiny = slice(PIECE, PIECE + 8)
    for p in range(GROUP):
        small[p] = (f32(sums_one[0, p, tiny, :]) + f32(sums_one[1, p, tiny, :])) * grad_norm
    for blk in range(BLOCKS):

        def row_of(r):
            return small[r // 4, blk * 4 + r % 4 : blk * 4 + r % 4 + 1, :]

        for a in range(KSIZE):
            for b in range(KSIZE):
                g_kernel[a, b, blk : blk + 1, :] = row_of(a * KSIZE + b)
        for k, ref in enumerate((g_conv, g_gain, g_shift, g_bias_out, g_scale)):
            ref[blk : blk + 1, :] = row_of(49 + k)
        for q in range(4):
            g_bias_in[blk : blk + 1, q * 128 : q * 128 + 128] = row_of(54 + q)
    for copy in leaving:
        copy.wait()


def on_device(
    state,
    land_sea,
    cotangent,
    dw_kernel,
    *rest,
):
    vmem = pl.BlockSpec(memory_space=pltpu.VMEM)
    anywhere = pl.BlockSpec(memory_space=pl.ANY)
    grad_norm = 1.0 / math.sqrt(
        lax.axis_size("lat") * ROWS * lax.axis_size("lon") * COLS
    )
    field = jax.ShapeDtypeStruct((ROWS, COLS, C), jnp.bfloat16)
    row = jax.ShapeDtypeStruct((BLOCKS, C), jnp.float32)

    def vm(*shape, dtype=jnp.float32):
        return pltpu.VMEM(shape, dtype)

    def sems(*shape):
        return pltpu.SemaphoreType.DMA(shape)

    tall, wide = ROWS + 2 * MARGIN, COLS + 8
    half = jnp.bfloat16
    packed = PIECE + 8
    arguments = (state, land_sea.T, cotangent, jnp.transpose(dw_kernel, (1, 2, 0, 3)), *rest)
    fields = pl.pallas_call(
        step_kernel,
        name="ocean_step",
        out_shape=(
            field,
            field,
            jax.ShapeDtypeStruct((2, GROUP, packed, C), jnp.bfloat16),
            jax.ShapeDtypeStruct((2, GROUP, PIECE, C), jnp.bfloat16),
        ),
        in_specs=[pl.BlockSpec(memory_space=pltpu.HBM)] * 12,
        out_specs=(anywhere,) * 4,
        scratch_shapes=[
            vm(tall, wide, C),
            vm(tall, wide, C),
            vm(tall, wide, C),
            vm(tall, wide, C),
            vm(KSIZE, KSIZE, BLOCKS, C),
            vm(ROWS, COLS, C),
            vm(ROWS, COLS, C),
            vm(CELLS, F),
            vm(CHUNKS + 1, CELLS, F, dtype=half),
            vm(CHUNKS + 1, CELLS, F),
            vm(CHUNKS + 1, CELLS, C),
            vm(CHUNKS + 1, CELLS, C),
            vm(CHUNKS + 1, CELLS, C),
            vm(ROWS, COLS, C),
            vm(BLOCKS, C, F),
            vm(BLOCKS, C, F),
            vm(BLOCKS, 5, 8, C),
            vm(BLOCKS, 8, F),
            vm(BLOCKS, KSIZE * KSIZE, 8, C),
            vm(4, ROWS, MARGIN, C, dtype=half),
            vm(4, ROWS, MARGIN, C, dtype=half),
            vm(4, MARGIN, COLS, C, dtype=half),
            vm(4, MARGIN, COLS, C, dtype=half),
            vm(4, 2, tall, MARGIN, C, dtype=half),
            vm(4, 2, MARGIN, COLS, C, dtype=half),
            sems(4, 2, 2),
            vm(GROUP, 8, C),
            vm(BLOCKS, 2, F, C, dtype=half),
            vm(BLOCKS, F, C, dtype=half),
            vm(BLOCKS, GROUP, PIECE, C, dtype=half),
            vm(BLOCKS, GROUP, PIECE, C, dtype=half),
            vm(GROUP, 8, C),
            vm(BLOCKS, packed, C, dtype=half),
            vm(BLOCKS, LINE, packed, C, dtype=half),
            vm(2, GROUP, packed, C, dtype=half),
            vm(2, GROUP, PIECE, C, dtype=half),
            vm(CHUNKS, CELLS, C, dtype=half),
            vm(CHUNKS, CELLS, F),
            sems(2 * BLOCKS, 2),
            sems(BLOCKS, 2),
            sems(2),
            sems(BLOCKS, 2),
            sems(BLOCKS, 2),
            sems(len(arguments)),
            vm(ROWS, COLS, C, dtype=half),
            vm(ROWS, COLS, C, dtype=half),
            sems(4),
            *(pltpu.VMEM(array.shape, array.dtype) for array in arguments),
        ],
        compiler_params=pltpu.CompilerParams(
            collective_id=0, has_side_effects=True, vmem_limit_bytes=58 << 20
        ),
    )(*arguments)
    results = pl.pallas_call(
        lambda *refs: write_kernel(grad_norm, *refs),
        name="write_results",
        out_shape=(
            field,
            field,
            jax.ShapeDtypeStruct((KSIZE, KSIZE, BLOCKS, C), jnp.float32),
            row,
            row,
            row,
            jax.ShapeDtypeStruct((BLOCKS, C, F), jnp.float32),
            jax.ShapeDtypeStruct((BLOCKS, F), jnp.float32),
            jax.ShapeDtypeStruct((BLOCKS, F, C), jnp.float32),
            row,
            row,
        ),
        in_specs=[anywhere] * 4,
        out_specs=(anywhere, anywhere, vmem, vmem, vmem, vmem, anywhere, vmem, anywhere, vmem, vmem),
        scratch_shapes=[
            vm(GROUP, 8, C),
            vm(2, ROWS, COLS, C, dtype=half),
            vm(2, GROUP, packed, C, dtype=half),
            vm(2, GROUP, PIECE, C, dtype=half),
            vm(BLOCKS, C, F),
            vm(BLOCKS, F, C),
            sems(10),
        ],
        compiler_params=pltpu.CompilerParams(vmem_limit_bytes=58 << 20),
    )(*fields)
    return results[:2] + (jnp.transpose(results[2], (2, 0, 1, 3)),) + results[3:]


def solution(mesh):
    field = P("lat", "lon", None)
    return jax.shard_map(
        on_device,
        mesh=mesh,
        in_specs=(field, P("lat", "lon"), field) + (P(),) * 9,
        out_specs=(field, field) + (P(),) * 9,
        check_vma=False,
    )
```

```python
import math

import jax
import jax.numpy as jnp
from jax import lax
from jax.experimental import pallas as pl
from jax.experimental.pallas import tpu as pltpu
from jax.sharding import PartitionSpec as P

KSIZE = 7
BLOCKS = 2
C = 128
F = 512
EPS_NORM = 1e-06
INV_ROOT_TWO = 0.7071067811865476
INV_ROOT_TWO_PI = 0.3989422804014327
MESH_ID = pl.DeviceIdType.MESH
GROUP = 16
LINE = 8
PIECE = 32
ROWS = 45
COLS = 24
MARGIN = 3
AROUND = ((1, 0), (-1, 0), (0, 1), (0, -1), (1, 1), (1, -1), (-1, 1), (-1, -1))
STRIP = 15
CHUNKS = ROWS // STRIP
CELLS = STRIP * COLS


def position():
    lon = lax.axis_index("lon")
    plane = lax.rem(lon // 2, 2) * 8 + lax.axis_index("lat")
    return plane, lon // 4, lax.rem(lon, 2)


def device(plane, z, core):
    return {"lon": z * 4 + (plane // 8) * 2 + core, "lat": lax.rem(plane, 8)}


def beside(east, south):
    return {
        "lon": lax.rem(lax.axis_index("lon") + east + 32, 32),
        "lat": lax.rem(lax.axis_index("lat") + south + 8, 8),
    }


def announce(barrier):
    plane, z, core = position()

    def signal(target):
        pl.semaphore_signal(barrier, inc=1, device_id=target, device_id_type=MESH_ID)

    for east, south in AROUND:
        signal(beside(east, south))
    signal(device(plane, z, 1 - core))

    def in_plane(k, carry):
        signal(device(lax.rem(plane + k, GROUP), z, core))
        return carry

    def in_line(k, carry):
        signal(device(plane, lax.rem(z + k, LINE), core))
        return carry

    for k in range(1, GROUP):
        in_plane(k, 0)
    for k in range(1, LINE):
        in_line(k, 0)


class Exchange:
    def __init__(self, kind, scatter, src, dst, sems):
        self.plane, self.z, self.core = position()
        self.kind, self.scatter = kind, scatter
        self.src, self.dst, self.sems = src, dst, sems
        self.me, self.size = (self.plane, GROUP) if kind == "plane" else (self.z, LINE)

    def start(self):
        for k in range(1, self.size):
            other = lax.rem(self.me + k, self.size)
            if self.kind == "plane":
                target = device(other, self.z, self.core)
            else:
                target = device(self.plane, other, self.core)
            pltpu.make_async_remote_copy(
                src_ref=self.src.at[other] if self.scatter else self.src,
                dst_ref=self.dst.at[k if self.scatter else self.me],
                send_sem=self.sems.at[0],
                recv_sem=self.sems.at[1],
                device_id=target,
                device_id_type=MESH_ID,
            ).start()
        return self

    def wait(self):
        others = pl.ds(1, self.size - 1)
        for side in range(2):
            pltpu.make_async_copy(
                self.dst.at[others], self.dst.at[others], self.sems.at[side]
            ).wait()


def to_sibling(src, dst, sems):
    plane, z, core = position()
    return pltpu.make_async_remote_copy(
        src_ref=src,
        dst_ref=dst,
        send_sem=sems.at[0],
        recv_sem=sems.at[1],
        device_id=device(plane, z, 1 - core),
        device_id_type=MESH_ID,
    )


def slot_sum(own, slots, count=GROUP):
    def one(k, total):
        return total + slots[k].astype(jnp.float32)

    return lax.fori_loop(1, count, one, own)


def f32(value):
    return value.astype(jnp.float32)


def bf16(value):
    return value.astype(jnp.bfloat16)


class Halo:
    def __init__(self, bufs, sems, index, window):
        east, west, north, south, self.sides, self.ends = (ref.at[index] for ref in bufs)
        from_west, from_east = self.sides.at[0], self.sides.at[1]
        from_north, from_south = self.ends.at[0], self.ends.at[1]
        self.sems = sems.at[index]
        self.bufs = (east, west, north, south, from_west, from_east, from_north, from_south)
        self.window = window
        last = ROWS - MARGIN
        tall = pl.ds(MARGIN, ROWS)
        above, below = pl.ds(0, MARGIN), pl.ds(MARGIN + ROWS, MARGIN)
        top, bottom = pl.ds(0, MARGIN), pl.ds(last, MARGIN)
        pairs = (
            (east, from_west.at[tall]),
            (west, from_east.at[tall]),
            (south, from_north),
            (north, from_south),
            (east.at[bottom], from_west.at[above]),
            (east.at[top], from_west.at[below]),
            (west.at[bottom], from_east.at[above]),
            (west.at[top], from_east.at[below]),
        )
        self.copies = [
            pltpu.make_async_remote_copy(
                src_ref=pair[0],
                dst_ref=pair[1],
                send_sem=sems.at[index, 0, int(k in (2, 3))],
                recv_sem=sems.at[index, 1, int(k in (2, 3))],
                device_id=beside(*AROUND[k]),
                device_id_type=MESH_ID,
            )
            for k, pair in enumerate(pairs)
        ]

    def start(self):
        self.stage()
        self.launch()

    def stage_from(self, tile):
        east, west, north, south = self.bufs[:4]
        east[...] = tile[:, COLS - MARGIN : COLS, :]
        west[...] = tile[:, 0:MARGIN, :]
        north[...] = tile[0:MARGIN]
        south[...] = tile[ROWS - MARGIN : ROWS]

    def stage(self):
        east, west, north, south = self.bufs[:4]
        window = self.window
        inner = slice(MARGIN, MARGIN + ROWS)
        east[...] = bf16(window[inner, COLS : COLS + MARGIN, :])
        west[...] = bf16(window[inner, MARGIN : 2 * MARGIN, :])
        north[...] = bf16(window[MARGIN : 2 * MARGIN, MARGIN : MARGIN + COLS, :])
        south[...] = bf16(window[ROWS : ROWS + MARGIN, MARGIN : MARGIN + COLS, :])

    def launch(self):
        for copy in self.copies:
            copy.start()

    def finish(self):
        for kind, ref in enumerate((self.sides, self.ends)):
            for side in range(2):
                pltpu.make_async_copy(ref, ref, self.sems.at[side, kind]).wait()
        from_west, from_east, from_north, from_south = self.bufs[4:]
        lat = lax.axis_index("lat")
        has_north = jnp.where(lat > 0, 1.0, 0.0).astype(jnp.float32)
        has_south = jnp.where(lat < 7, 1.0, 0.0).astype(jnp.float32)
        window = self.window
        inner = slice(MARGIN, MARGIN + ROWS)
        above, below = slice(0, MARGIN), slice(MARGIN + ROWS, 2 * MARGIN + ROWS)
        middle = slice(MARGIN, MARGIN + COLS)
        window[above, middle, :] = f32(from_north[...]) * has_north
        window[below, middle, :] = f32(from_south[...]) * has_south
        for ref, side in (
            (from_west, slice(0, MARGIN)),
            (from_east, slice(MARGIN + COLS, 2 * MARGIN + COLS)),
        ):
            window[inner, side, :] = f32(ref[inner])
            window[above, side, :] = f32(ref[above]) * has_north
            window[below, side, :] = f32(ref[below]) * has_south


def convolve(window, weight, first, flip):
    def rows(base):
        sums = first(base)
        for i in range(KSIZE + 4):
            for b in range(KSIZE):
                piece = window[base + i, b : b + COLS, :]
                for o in range(5):
                    a = i - o
                    if 0 <= a < KSIZE:
                        tap = weight(KSIZE - 1 - a, KSIZE - 1 - b) if flip else weight(a, b)
                        sums[o] = sums[o] + piece * tap
        return sums

    return rows


def fold(value):
    return jnp.sum(value.reshape(value.shape[0] // 8, 8, value.shape[1]), axis=0)


def lane_mean(value):
    return jnp.mean(value, axis=-1, keepdims=True)


def step_kernel(
    *refs,
):
    arguments, refs = refs[:12], refs[12:]
    (
    out_hbm,
    state_hbm,
    sums_one,
    sums_two,
    win1,
    win2,
    gwin1,
    gwin2,
    taps,
    mask,
    mixed,
    hidden,
    active,
    slope,
    normed,
    inverse,
    branch,
    upstream,
    acc_win,
    acc_wout,
    acc_rows,
    acc_bias,
    acc_taps,
    h_east,
    h_west,
    h_north,
    h_south,
    h_sides,
    h_ends,
    sem_h,
    small,
    halves,
    from_core,
    send_a,
    recv_a,
    tiny_a,
    line_own,
    line_all,
    gather_one,
    gather_two,
    seeds,
    pulled,
    sem_core,
    sem_a,
    sem_tiny,
    sem_line,
    sem_back,
    sem_load,
    out,
    grad_state,
    sem_put,
    *arrived,
    ) = refs
    loads = [
        pltpu.make_async_copy(source, target, sem_load.at[n])
        for n, (source, target) in enumerate(zip(arguments, arrived))
    ]
    for load in loads:
        load.start()
    (
        state,
        land_sea,
        cotangent,
        dw_kernel,
        conv_bias,
        norm_gain,
        norm_bias,
        weight_in,
        bias_in,
        weight_out,
        bias_out,
        layer_scale,
    ) = arrived
    plane, z, core = position()
    barrier = pltpu.get_barrier_semaphore()
    announce(barrier)
    loads[0].wait()
    halo_bufs = (
        h_east, h_west, h_north, h_south, h_sides, h_ends
    )
    middle = slice(MARGIN, MARGIN + COLS)

    halo = Halo(halo_bufs, sem_h, 0, win1)
    halo.stage_from(state)
    pl.semaphore_wait(barrier, GROUP + LINE - 1 + len(AROUND))
    halo.launch()

    def widen(c, carry):
        win1[pl.ds(MARGIN + c * STRIP, STRIP), middle, :] = f32(state[pl.ds(c * STRIP, STRIP)])
        return carry

    lax.fori_loop(0, CHUNKS, widen, 0)
    for load in loads[1:]:
        load.wait()

    taps[...] = f32(dw_kernel[...])
    ocean_t = land_sea[...].astype(jnp.float32)
    for i in range(ROWS):
        mask[i] = jnp.broadcast_to(ocean_t[:, i : i + 1], (COLS, C))
    acc_win[...] = jnp.zeros_like(acc_win)
    acc_wout[...] = jnp.zeros_like(acc_wout)
    acc_rows[...] = jnp.zeros_like(acc_rows)
    acc_bias[...] = jnp.zeros_like(acc_bias)
    acc_taps[...] = jnp.zeros_like(acc_taps)
    small[...] = jnp.zeros_like(small)

    def mix(window, blk):
        start = jnp.broadcast_to(conv_bias[blk : blk + 1, :], (COLS, C))
        rows = convolve(
            window, lambda a, b: taps[a, b, blk : blk + 1, :], lambda base: [start] * 5, False
        )

        def five(g, carry):
            sums = rows(g * 5)
            for o in range(5):
                mixed[g * 5 + o] = sums[o]
            return carry

        lax.fori_loop(0, ROWS // 5, five, 0, unroll=3)

    def forward(c, window, blk, keep):
        x = mixed[pl.ds(c * STRIP, STRIP)].reshape(CELLS, C)
        center = x - lane_mean(x)
        inv = lax.rsqrt(lane_mean(center * center) + EPS_NORM)
        norm = center * inv
        normed[keep] = norm
        inverse[keep] = jnp.broadcast_to(inv, (CELLS, C))
        lifted = bf16(norm * norm_gain[blk : blk + 1, :] + norm_bias[blk : blk + 1, :])
        hidden[keep] = jnp.dot(lifted, weight_in[blk], preferred_element_type=jnp.float32)

        def gelu(t, carry):
            rows = pl.ds(pl.multiple_of(t * COLS, 8), COLS)
            h = hidden[keep, rows, :] + bias_in[blk : blk + 1, :]
            cumulative = 0.5 * (1.0 + lax.erf(h * INV_ROOT_TWO))
            density = jnp.exp(-0.5 * h * h) * INV_ROOT_TWO_PI
            active[keep, rows, :] = bf16(h * cumulative)
            slope[keep, rows, :] = cumulative + h * density
            return carry

        lax.fori_loop(0, STRIP, gelu, 0, unroll=15)
        act = active[keep]
        branch_c = (
            jnp.dot(act, weight_out[blk], preferred_element_type=jnp.float32)
            + bias_out[blk : blk + 1, :]
        )
        branch[keep] = branch_c
        inner = window[pl.ds(MARGIN + c * STRIP, STRIP), middle, :].reshape(CELLS, C)
        ocean = mask[pl.ds(c * STRIP, STRIP)].reshape(CELLS, C)
        return (inner + layer_scale[blk : blk + 1, :] * branch_c) * ocean

    def seed(c, incoming, blk):
        ocean = mask[pl.ds(c * STRIP, STRIP)].reshape(CELLS, C)
        masked = incoming * ocean
        upstream[pl.ds(c * STRIP, STRIP)] = masked.reshape(STRIP, COLS, C)
        gb = bf16(masked * layer_scale[blk : blk + 1, :])
        acc_rows[blk, 3] += fold(f32(gb))
        seeds[c] = gb
        pulled[c] = lax.dot_general(
            gb, weight_out[blk], (((1,), (1,)), ((), ())), preferred_element_type=jnp.float32
        )

    def backward(c, gwindow, blk, keep):
        masked = upstream[pl.ds(c * STRIP, STRIP)].reshape(CELLS, C)
        acc_rows[blk, 4] += fold(masked * branch[keep])
        rows_rows = (((0,), (0,)), ((), ()))
        cols_cols = (((1,), (1,)), ((), ()))
        acc_wout[blk] += lax.dot_general(
            seeds[c], active[keep], rows_rows, preferred_element_type=jnp.float32
        )

        gh = bf16(pulled[c] * slope[keep])
        acc_bias[blk] += jnp.dot(
            jnp.ones((8, CELLS), jnp.bfloat16), gh, preferred_element_type=jnp.float32
        )
        norm = normed[keep]
        gain = norm_gain[blk : blk + 1, :]
        lifted = bf16(norm * gain + norm_bias[blk : blk + 1, :])
        acc_win[blk] += lax.dot_general(
            lifted, gh, rows_rows, preferred_element_type=jnp.float32
        )
        gl = lax.dot_general(gh, weight_in[blk], cols_cols, preferred_element_type=jnp.float32)
        acc_rows[blk, 1] += fold(gl * norm)
        acc_rows[blk, 2] += fold(gl)
        s = gl * gain
        gm = inverse[keep] * (s - lane_mean(s) - norm * lane_mean(s * norm))
        gm = f32(bf16(gm))
        acc_rows[blk, 0] += fold(gm)
        gwindow[pl.ds(MARGIN + c * STRIP, STRIP), middle, :] = gm.reshape(STRIP, COLS, C)

    def tap_sums(window, gwindow, blk, begin, end):
        def five(g, carry):
            base = g * 5
            grads = [gwindow[base + MARGIN + o, middle, :] for o in range(5)]
            for b in range(KSIZE):
                parts = [None] * KSIZE
                for i in range(KSIZE + 4):
                    piece = window[base + i, b : b + COLS, :]
                    for o in range(5):
                        a = i - o
                        if 0 <= a < KSIZE:
                            term = piece * grads[o]
                            parts[a] = term if parts[a] is None else parts[a] + term
                for a in range(KSIZE):
                    acc_taps[blk, a * KSIZE + b] += fold(parts[a])
            return carry

        lax.fori_loop(begin, end, five, 0)

    def adjoint(gwindow, blk, put, begin, end):
        rows = convolve(
            gwindow,
            lambda a, b: taps[a, b, blk : blk + 1, :],
            lambda base: [upstream[base + o] for o in range(5)],
            True,
        )

        def five(g, carry):
            sums = rows(g * 5)
            for o in range(5):
                put(g * 5 + o, sums[o])
            return carry

        lax.fori_loop(begin, end, five, 0)

    def core_sum(blk):
        for q in range(4):
            block = slice(q * 128, q * 128 + 128)
            halves[blk, 0, block, :] = bf16(acc_win[blk, :, block])
            halves[blk, 1, block, :] = bf16(jnp.transpose(acc_wout[blk, :, block]))
        copy = to_sibling(halves.at[blk, 1 - core], from_core.at[blk], sem_core.at[blk])
        copy.start()
        return copy

    def plane_sum(copy, blk):
        copy.wait()
        both = f32(halves[blk, core]) + f32(from_core[blk])
        send_a[blk] = bf16(both).reshape(GROUP, PIECE, C)
        return Exchange("plane", True, send_a.at[blk], recv_a.at[blk], sem_a.at[blk]).start()

    def line_sum(ex, blk, tiny):
        ex.wait()
        total = bf16(slot_sum(f32(send_a[blk, plane]), recv_a.at[blk]))
        rows = line_all.at[blk] if tiny is not None else line_all.at[blk, :, 0:PIECE]
        line_all[blk, z, 0:PIECE] = total
        line_own[blk, 0:PIECE] = total
        own = line_own.at[blk, 0:PIECE]
        if tiny is not None:
            tiny.wait()
            tiny_total = bf16(slot_sum(small[plane], tiny_a))
            line_all[blk, z, PIECE : PIECE + 8] = tiny_total
            line_own[blk, PIECE : PIECE + 8] = tiny_total
            own = line_own.at[blk]
        return Exchange("line", False, own, rows, sem_line.at[blk]).start()

    def plane_back(ex, blk, gather):
        ex.wait()
        rows = gather.shape[2]
        own = f32(line_all[blk, 0, 0:rows])
        for j in range(1, LINE):
            own = own + f32(line_all[blk, j, 0:rows])
        gather[core, plane] = bf16(own)
        return Exchange(
            "plane", False, gather.at[core, plane], gather.at[core], sem_back.at[blk]
        ).start()

    def swap_halves(ex, blk, gather):
        ex.wait()
        copy = to_sibling(gather.at[core], gather.at[core], sem_core.at[BLOCKS + blk])
        copy.start()
        return copy

    def small_row(blk, r, value):
        i = blk * 4 + r % 4
        small[r // 4, i : i + 1, :] = jnp.sum(value, axis=0, keepdims=True)

    def pack_rows(blk):
        for tap in range(KSIZE * KSIZE):
            small_row(blk, tap, acc_taps[blk, tap])
        for k in range(5):
            small_row(blk, 49 + k, acc_rows[blk, k])
        for q in range(4):
            small_row(blk, 54 + q, acc_bias[blk, 0:1, q * 128 : q * 128 + 128])

    halo.finish()
    mix(win1, 0)

    def forward_one(c, carry):
        result = forward(c, win1, 0, c)
        win2[pl.ds(MARGIN + c * STRIP, STRIP), middle, :] = f32(bf16(result)).reshape(
            STRIP, COLS, C
        )
        return carry

    lax.fori_loop(0, CHUNKS, forward_one, 0, unroll=True)
    halo = Halo(halo_bufs, sem_h, 1, win2)
    halo.start()

    def seed_two(c, carry):
        seed(c, f32(cotangent[pl.ds(c * STRIP, STRIP)]).reshape(CELLS, C), 1)
        return carry

    lax.fori_loop(0, CHUNKS, seed_two, 0, unroll=True)
    halo.finish()
    mix(win2, 1)

    def both(c, carry):
        result = forward(c, win2, 1, CHUNKS + c)
        out[pl.ds(c * STRIP, STRIP)] = bf16(result.reshape(STRIP, COLS, C))
        backward(c, gwin2, 1, CHUNKS + c)
        return carry

    lax.fori_loop(0, CHUNKS, both, 0, unroll=True)
    put_out = pltpu.make_async_copy(out, out_hbm, sem_put.at[0])
    put_out.start()
    halo = Halo(halo_bufs, sem_h, 2, gwin2)
    halo.start()
    second = core_sum(1)
    tap_sums(win2, gwin2, 1, 0, 9)
    second = plane_sum(second, 1)
    pack_rows(1)
    halo.finish()

    def put_mixed(row, value):
        mixed[row] = f32(bf16(value))

    adjoint(gwin2, 1, put_mixed, 0, 9)
    second = line_sum(second, 1, None)

    def backward_one(c, carry):
        seed(c, mixed[pl.ds(c * STRIP, STRIP)].reshape(CELLS, C), 0)
        backward(c, gwin1, 0, c)
        return carry

    lax.fori_loop(0, CHUNKS, backward_one, 0, unroll=True)
    halo = Halo(halo_bufs, sem_h, 3, gwin1)
    halo.start()
    first = core_sum(0)
    tap_sums(win1, gwin1, 0, 0, 4)
    first = plane_sum(first, 0)
    tap_sums(win1, gwin1, 0, 4, 9)
    pack_rows(0)
    tiny = Exchange("plane", True, small, tiny_a, sem_tiny).start()
    second = plane_back(second, 1, gather_two)
    halo.finish()

    def put_state(row, value):
        grad_state[row] = bf16(value)

    adjoint(gwin1, 0, put_state, 0, 5)
    first = line_sum(first, 0, tiny)
    second = swap_halves(second, 1, gather_two)
    adjoint(gwin1, 0, put_state, 5, 9)
    put_grad = pltpu.make_async_copy(grad_state, state_hbm, sem_put.at[1])
    put_grad.start()
    second.wait()
    put_two = pltpu.make_async_copy(gather_two, sums_two, sem_put.at[2])
    put_two.start()
    first = plane_back(first, 0, gather_one)
    first = swap_halves(first, 0, gather_one)
    first.wait()
    put_one = pltpu.make_async_copy(gather_one, sums_one, sem_put.at[3])
    put_one.start()
    for put in (put_out, put_grad, put_two, put_one):
        put.wait()


def write_kernel(
    grad_norm,
    out_from,
    state_from,
    one_from,
    two_from,
    out,
    grad_state,
    g_kernel,
    g_conv,
    g_gain,
    g_shift,
    g_win,
    g_bias_in,
    g_wout,
    g_bias_out,
    g_scale,
    small,
    held,
    sums_one,
    sums_two,
    win,
    wout,
    sems,
):
    def move(source, target, n):
        copy = pltpu.make_async_copy(source, target, sems.at[n])
        copy.start()
        return copy

    two_in = move(two_from, sums_two, 0)
    fields_in = [move(out_from, held.at[0], 1), move(state_from, held.at[1], 2)]
    one_in = move(one_from, sums_one, 3)
    leaving = []

    def widen(blk, sums):
        rows = slice(0, PIECE)
        for p in range(GROUP):
            win[
                blk, (p % 4) * PIECE : (p % 4) * PIECE + PIECE, (p // 4) * 128 : (p // 4) * 128 + 128
            ] = f32(sums[0, p, rows, :]) * grad_norm
            wout[blk, p * PIECE : p * PIECE + PIECE] = f32(sums[1, p, rows, :]) * grad_norm
        leaving.append(move(win.at[blk], g_win.at[blk], 4 + 2 * blk))
        leaving.append(move(wout.at[blk], g_wout.at[blk], 5 + 2 * blk))

    two_in.wait()
    widen(1, sums_two)
    fields_in[0].wait()
    leaving.append(move(held.at[0], out, 8))
    fields_in[1].wait()
    leaving.append(move(held.at[1], grad_state, 9))
    one_in.wait()
    widen(0, sums_one)
    tiny = slice(PIECE, PIECE + 8)
    for p in range(GROUP):
        small[p] = (f32(sums_one[0, p, tiny, :]) + f32(sums_one[1, p, tiny, :])) * grad_norm
    for blk in range(BLOCKS):

        def row_of(r):
            return small[r // 4, blk * 4 + r % 4 : blk * 4 + r % 4 + 1, :]

        for a in range(KSIZE):
            for b in range(KSIZE):
                g_kernel[a, b, blk : blk + 1, :] = row_of(a * KSIZE + b)
        for k, ref in enumerate((g_conv, g_gain, g_shift, g_bias_out, g_scale)):
            ref[blk : blk + 1, :] = row_of(49 + k)
        for q in range(4):
            g_bias_in[blk : blk + 1, q * 128 : q * 128 + 128] = row_of(54 + q)
    for copy in leaving:
        copy.wait()


def on_device(
    state,
    land_sea,
    cotangent,
    dw_kernel,
    *rest,
):
    vmem = pl.BlockSpec(memory_space=pltpu.VMEM)
    anywhere = pl.BlockSpec(memory_space=pl.ANY)
    grad_norm = 1.0 / math.sqrt(
        lax.axis_size("lat") * ROWS * lax.axis_size("lon") * COLS
    )
    field = jax.ShapeDtypeStruct((ROWS, COLS, C), jnp.bfloat16)
    row = jax.ShapeDtypeStruct((BLOCKS, C), jnp.float32)

    def vm(*shape, dtype=jnp.float32):
        return pltpu.VMEM(shape, dtype)

    def sems(*shape):
        return pltpu.SemaphoreType.DMA(shape)

    tall, wide = ROWS + 2 * MARGIN, COLS + 8
    half = jnp.bfloat16
    packed = PIECE + 8
    arguments = (state, land_sea.T, cotangent, jnp.transpose(dw_kernel, (1, 2, 0, 3)), *rest)
    fields = pl.pallas_call(
        step_kernel,
        name="ocean_step",
        out_shape=(
            field,
            field,
            jax.ShapeDtypeStruct((2, GROUP, packed, C), jnp.bfloat16),
            jax.ShapeDtypeStruct((2, GROUP, PIECE, C), jnp.bfloat16),
        ),
        in_specs=[pl.BlockSpec(memory_space=pltpu.HBM)] * 12,
        out_specs=(anywhere,) * 4,
        scratch_shapes=[
            vm(tall, wide, C),
            vm(tall, wide, C),
            vm(tall, wide, C),
            vm(tall, wide, C),
            vm(KSIZE, KSIZE, BLOCKS, C),
            vm(ROWS, COLS, C),
            vm(ROWS, COLS, C),
            vm(2 * CHUNKS, CELLS, F),
            vm(2 * CHUNKS, CELLS, F, dtype=half),
            vm(2 * CHUNKS, CELLS, F),
            vm(2 * CHUNKS, CELLS, C),
            vm(2 * CHUNKS, CELLS, C),
            vm(2 * CHUNKS, CELLS, C),
            vm(ROWS, COLS, C),
            vm(BLOCKS, C, F),
            vm(BLOCKS, C, F),
            vm(BLOCKS, 5, 8, C),
            vm(BLOCKS, 8, F),
            vm(BLOCKS, KSIZE * KSIZE, 8, C),
            vm(4, ROWS, MARGIN, C, dtype=half),
            vm(4, ROWS, MARGIN, C, dtype=half),
            vm(4, MARGIN, COLS, C, dtype=half),
            vm(4, MARGIN, COLS, C, dtype=half),
            vm(4, 2, tall, MARGIN, C, dtype=half),
            vm(4, 2, MARGIN, COLS, C, dtype=half),
            sems(4, 2, 2),
            vm(GROUP, 8, C),
            vm(BLOCKS, 2, F, C, dtype=half),
            vm(BLOCKS, F, C, dtype=half),
            vm(BLOCKS, GROUP, PIECE, C, dtype=half),
            vm(BLOCKS, GROUP, PIECE, C, dtype=half),
            vm(GROUP, 8, C),
            vm(BLOCKS, packed, C, dtype=half),
            vm(BLOCKS, LINE, packed, C, dtype=half),
            vm(2, GROUP, packed, C, dtype=half),
            vm(2, GROUP, PIECE, C, dtype=half),
            vm(CHUNKS, CELLS, C, dtype=half),
            vm(CHUNKS, CELLS, F),
            sems(2 * BLOCKS, 2),
            sems(BLOCKS, 2),
            sems(2),
            sems(BLOCKS, 2),
            sems(BLOCKS, 2),
            sems(len(arguments)),
            vm(ROWS, COLS, C, dtype=half),
            vm(ROWS, COLS, C, dtype=half),
            sems(4),
            *(pltpu.VMEM(array.shape, array.dtype) for array in arguments),
        ],
        compiler_params=pltpu.CompilerParams(
            collective_id=0, has_side_effects=True, vmem_limit_bytes=58 << 20
        ),
    )(*arguments)
    results = pl.pallas_call(
        lambda *refs: write_kernel(grad_norm, *refs),
        name="write_results",
        out_shape=(
            field,
            field,
            jax.ShapeDtypeStruct((KSIZE, KSIZE, BLOCKS, C), jnp.float32),
            row,
            row,
            row,
            jax.ShapeDtypeStruct((BLOCKS, C, F), jnp.float32),
            jax.ShapeDtypeStruct((BLOCKS, F), jnp.float32),
            jax.ShapeDtypeStruct((BLOCKS, F, C), jnp.float32),
            row,
            row,
        ),
        in_specs=[anywhere] * 4,
        out_specs=(anywhere, anywhere, vmem, vmem, vmem, vmem, anywhere, vmem, anywhere, vmem, vmem),
        scratch_shapes=[
            vm(GROUP, 8, C),
            vm(2, ROWS, COLS, C, dtype=half),
            vm(2, GROUP, packed, C, dtype=half),
            vm(2, GROUP, PIECE, C, dtype=half),
            vm(BLOCKS, C, F),
            vm(BLOCKS, F, C),
            sems(10),
        ],
        compiler_params=pltpu.CompilerParams(vmem_limit_bytes=58 << 20),
    )(*fields)
    return results[:2] + (jnp.transpose(results[2], (2, 0, 1, 3)),) + results[3:]


def solution(mesh):
    field = P("lat", "lon", None)
    return jax.shard_map(
        on_device,
        mesh=mesh,
        in_specs=(field, P("lat", "lon"), field) + (P(),) * 9,
        out_specs=(field, field) + (P(),) * 9,
        check_vma=False,
    )
```
